256 devices in a mesh: gx: 4 (over z_lo), gy: 8 (over z_hi, y), gz: 8 (over x, core).
Axes of the slice: x: 4, y: 4, z: 8 (z_hi: 2, z_lo: 4; z = z_hi * 4 + z_lo), core: 2. Of those that a mesh axis runs over, the one named last changes fastest.
Arguments:
- positions: float32 [4, 8, 8, 3, 128], P('gx', 'gy', 'gz'), may hold values from 0 to 5
- species: int32 [4, 8, 8, 128], P('gx', 'gy', 'gz'), may hold values from 0 to 5
- atom_count: int32 [4, 8, 8], P('gx', 'gy', 'gz'), may hold values from 16 to 128, as said below
- export_union: int32 [4, 8, 8, 64], P('gx', 'gy', 'gz'), may hold values from 0 to 127, as said below
- ghost_map: int32 [4, 8, 8, 27, 16], P('gx', 'gy', 'gz'), may hold values from 0 to 63, as said below
- edge_receiver: int32 [4, 8, 8, 1024], P('gx', 'gy', 'gz'), may hold values from 0 to 127, as said below
- edge_sender: int32 [4, 8, 8, 1024], P('gx', 'gy', 'gz'), may hold values from 0 to 559, as said below
- embed: float32 [6, 128], replicated, may hold values from -6 to 6
- species_energy: float32 [6], replicated, may hold values from -6 to 6
- radial_in: float32 [2, 8, 64], replicated, may hold values from -2 to 2
- radial_out: float32 [2, 64, 384], replicated, may hold values from -0.75 to 0.75
- mixing: float32 [2, 3, 128, 128], replicated, may hold values from -0.5 to 0.5
- product: float32 [2, 384, 128], replicated, may hold values from -0.3125 to 0.3125
- residual: float32 [2, 128, 128], replicated, may hold values from -0.5 to 0.5
- read_one: float32 [128], replicated, may hold values from -0.5 to 0.5
- read_hidden: float32 [128, 16], replicated, may hold values from -0.5 to 0.5
- read_two: float32 [16], replicated, may hold values from -1.5 to 1.5
Outputs:
- forces: float32 [4, 8, 8, 3, 128], P('gx', 'gy', 'gz')
- atom_energy: float32 [4, 8, 8, 128], P('gx', 'gy', 'gz')
- virial: float32 [3, 3], replicated
The draws below stay inside these ranges and needn't reach their ends.
Inputs may be any that keep to these rules, and one draw needn't show every extreme that they name: `atom_count`: the two middle layers of domains along gz are denser than the others, and one domain of them is full in every draw. `export_union`: every entry is a live atom of its own domain (below its count); entries may repeat. `ghost_map`: entry [k, s] is a position in the export_union of the neighbour at offset (k // 9 - 1, k // 3 % 3 - 1, k % 3 - 1) along (gx, gy, gz), all axes periodic. `edge_receiver`: edge slots below 8 times the domain's count are live and their receivers are live atoms; the other slots hold 0. `edge_sender`: A live sender below 128 is a live local atom; otherwise it is 128 + k * 16 + s, slot s of ghost block k, never k = 13. Padding slots hold 0.
All inputs are finite; a program needn't handle non-finite values.
Results may differ from the reference program's by a relative error of at most 0.0003.
Values sent between devices are 32-bit elements; how exact they have to be, the bound alone decides.
A program may use at most 64 MiB of HBM per device.

```python
import jax
import jax.numpy as jnp
import numpy as np
from jax import lax

C = 128
NB = 8
RH = 64
RHID = 16
NSPEC = 6
DEG = 8
ATOMS_DEV = 128
EDGES = 1024
UNION = 64
GHOSTS = 16
DOMX = 4
DOMY = 8
DOMZ = 8


def domain_counts(key):
    base_key = jax.random.fold_in(key, 101)
    key_light, key_dense, key_full = jax.random.split(base_key, 3)
    light_counts = jax.random.randint(key_light, (DOMX, DOMY, DOMZ), ATOMS_DEV // 8, ATOMS_DEV // 3 + 1)
    dense_counts = jax.random.randint(key_dense, (DOMX, DOMY, DOMZ), ATOMS_DEV // 2, ATOMS_DEV + 1)
    layer_index = jnp.arange(DOMZ, dtype=jnp.int32)
    middle = (layer_index == DOMZ // 2 - 1) | (layer_index == DOMZ // 2)
    counts = jnp.where(middle[None, None, :], dense_counts, light_counts)
    chosen = jax.random.randint(key_full, (), 0, DOMX * DOMY)
    flat_spot = chosen * DOMZ + DOMZ // 2
    return counts.reshape(-1).at[flat_spot].set(ATOMS_DEV).reshape(DOMX, DOMY, DOMZ).astype(jnp.int32)


def draw_atom_count(key, part):
    return domain_counts(key)


def draw_export_union(key, part):
    counts = domain_counts(key)
    raw_bits = jax.random.randint(jax.random.fold_in(key, 102), (DOMX, DOMY, DOMZ, UNION), 0, 1 << 20)
    return (raw_bits % counts[..., None]).astype(jnp.int32)


def direction_lists(key):
    return jax.random.randint(jax.random.fold_in(key, 103), (DOMX, DOMY, DOMZ, 27, GHOSTS), 0, UNION).astype(jnp.int32)


def draw_ghost_map(key, part):
    direction_table = direction_lists(key)
    columns = []
    for direction in range(27):
        roll_shift = (1 - direction // 9, 1 - direction // 3 % 3, 1 - direction % 3)
        columns.append(jnp.roll(direction_table[:, :, :, 26 - direction, :], roll_shift, axis=(0, 1, 2)))
    return jnp.stack(columns, axis=3)


def edge_lists(key):
    counts = domain_counts(key)
    random_keys = jax.random.split(jax.random.fold_in(key, 104), 5)
    edge_shape = (DOMX, DOMY, DOMZ, EDGES)
    count_limit = counts[..., None]
    receiver = jax.random.randint(random_keys[0], edge_shape, 0, 1 << 20) % count_limit
    local_sender = jax.random.randint(random_keys[1], edge_shape, 0, 1 << 20) % count_limit
    ghost_block = jax.random.randint(random_keys[2], edge_shape, 0, 26)
    ghost_block = ghost_block + (ghost_block >= 13).astype(jnp.int32)
    ghost_slot = jax.random.randint(random_keys[3], edge_shape, 0, GHOSTS)
    remote = jax.random.randint(random_keys[4], edge_shape, 0, 2)
    sender = jnp.where(remote == 1, ATOMS_DEV + ghost_block * GHOSTS + ghost_slot, local_sender)
    edge_alive = jnp.arange(EDGES, dtype=jnp.int32)[None, None, None, :] < DEG * count_limit
    return (jnp.where(edge_alive, receiver, 0).astype(jnp.int32), jnp.where(edge_alive, sender, 0).astype(jnp.int32))


def draw_edge_receiver(key, part):
    return edge_lists(key)[0]


def draw_edge_sender(key, part):
    return edge_lists(key)[1]


def with_ends(entries, stream_key, low, high):
    longest = entries.shape.index(max(entries.shape))
    spots = []
    for shift in (0, 1):
        where = [jax.random.randint(jax.random.fold_in(stream_key, axis), (), 0, length) for axis, length in enumerate(entries.shape)]
        where[longest] = (where[longest] + shift) % entries.shape[longest]
        spots.append(tuple(where))
    return entries.at[spots[0]].set(low).at[spots[1]].set(high)


def block_levels(rng, extent, cuts, least, top_value):
    def one(position, shards_of):
        draws = jax.random.uniform(jax.random.fold_in(jax.random.fold_in(rng, 6), position), (shards_of,), jnp.float32, least / len(cuts), top_value / len(cuts))
        return jnp.repeat(jnp.exp(draws), extent[position] // shards_of).reshape((-1,) + (1,) * (len(extent) - position - 1))

    factor_of = one(*cuts[0])
    for cut in cuts[1:]:
        factor_of = factor_of * one(*cut)
    return factor_of


def bell_draw(own_key, dims, spread, bound, kind=jnp.bfloat16):
    values = spread * jax.random.normal(own_key, dims, jnp.float32)
    return jnp.clip(values, min=-bound, max=bound).astype(kind)


def setup_inputs(seed: int = 0) -> dict:
    arg_keys = jax.random.split(jax.random.key(seed), 18)
    positions = jnp.clip(5.0 * jax.random.uniform(arg_keys[0], (DOMX, DOMY, DOMZ, 3, ATOMS_DEV), jnp.float32) ** block_levels(arg_keys[0], (DOMX, DOMY, DOMZ, 3, ATOMS_DEV), ((0, 4), (1, 8), (2, 8)), -0.2, 0.2), 0.0, 5.0)
    species = with_ends(jax.random.randint(arg_keys[1], (DOMX, DOMY, DOMZ, ATOMS_DEV), 0, NSPEC), jax.random.fold_in(arg_keys[1], 1), 0, NSPEC - 1).astype(jnp.int32)
    atom_count = draw_atom_count(jax.random.fold_in(arg_keys[17], 71), 0)
    export_union = draw_export_union(jax.random.fold_in(arg_keys[17], 71), 0)
    ghost_map = draw_ghost_map(jax.random.fold_in(arg_keys[17], 71), 0)
    edge_receiver = draw_edge_receiver(jax.random.fold_in(arg_keys[17], 71), 0)
    edge_sender = draw_edge_sender(jax.random.fold_in(arg_keys[17], 71), 0)
    embed = bell_draw(arg_keys[7], (NSPEC, C), 1.0, 6.0, jnp.float32)
    species_energy = bell_draw(arg_keys[8], (NSPEC,), 1.0, 6.0, jnp.float32)
    radial_in = bell_draw(arg_keys[9], (2, NB, RH), NB ** -0.5, 2.0, jnp.float32)
    radial_out = bell_draw(arg_keys[10], (2, RH, 3 * C), RH ** -0.5, 0.75, jnp.float32)
    mixing = bell_draw(arg_keys[11], (2, 3, C, C), C ** -0.5, 0.5, jnp.float32)
    product = bell_draw(arg_keys[12], (2, 3 * C, C), (3 * C) ** -0.5, 0.3125, jnp.float32)
    residual = bell_draw(arg_keys[13], (2, C, C), C ** -0.5, 0.5, jnp.float32)
    read_one = bell_draw(arg_keys[14], (C,), C ** -0.5, 0.5, jnp.float32)
    read_hidden = bell_draw(arg_keys[15], (C, RHID), C ** -0.5, 0.5, jnp.float32)
    read_two = bell_draw(arg_keys[16], (RHID,), RHID ** -0.5, 1.5, jnp.float32)
    return {"positions": positions, "species": species, "atom_count": atom_count, "export_union": export_union, "ghost_map": ghost_map, "edge_receiver": edge_receiver, "edge_sender": edge_sender, "embed": embed, "species_energy": species_energy, "radial_in": radial_in, "radial_out": radial_out, "mixing": mixing, "product": product, "residual": residual, "read_one": read_one, "read_hidden": read_hidden, "read_two": read_two}


DOMAIN_SIDE = 5.0
SOFTENING = 0.25
RADIAL_RANGE = 18.0
ROOT_THREE = 3.0 ** 0.5
ROOT_FIVE = 5.0 ** 0.5
ROOT_FIFTEEN = 15.0 ** 0.5
COMPONENT_DEGREE = np.array([0, 1, 1, 1, 2, 2, 2, 2, 2], dtype=np.int32)
FULL_PRECISION = lax.Precision.HIGHEST

def harmonics(unit):
    along_x, along_y, along_z = (unit[0], unit[1], unit[2])
    return jnp.stack([jnp.ones_like(along_x), ROOT_THREE * along_x, ROOT_THREE * along_y, ROOT_THREE * along_z, ROOT_FIFTEEN * along_x * along_y, ROOT_FIFTEEN * along_y * along_z, 0.5 * ROOT_FIVE * (3.0 * along_z * along_z - 1.0), ROOT_FIFTEEN * along_x * along_z, 0.5 * ROOT_FIFTEEN * (along_x * along_x - along_y * along_y)])

def offset_table(ghost_count):
    direction = np.arange(27)
    offsets = np.stack([direction // 9 - 1, direction // 3 % 3 - 1, direction % 3 - 1]).astype(np.float32) * DOMAIN_SIDE
    return jnp.asarray(np.repeat(offsets, ghost_count, axis=1))

def neighbour_table():
    domain = np.arange(DOMX * DOMY * DOMZ)
    along_x = domain // (DOMY * DOMZ)
    along_y = domain // DOMZ % DOMY
    along_z = domain % DOMZ
    columns = []
    for direction in range(27):
        step_x = direction // 9 - 1
        step_y = direction // 3 % 3 - 1
        step_z = direction % 3 - 1
        columns.append(((along_x + step_x) % DOMX * DOMY + (along_y + step_y) % DOMY) * DOMZ + (along_z + step_z) % DOMZ)
    return np.stack(columns, axis=1).astype(np.int32)

def edge_terms(h_table, coord_table, strain, receiver, sender, edge_live, radial_in, radial_out, atom_slots):
    separation = coord_table[:, sender] - coord_table[:, receiver]
    separation = separation + jnp.dot(strain, separation, precision=FULL_PRECISION)
    length = jnp.sqrt(lax.optimization_barrier(jnp.sum(separation * separation, axis=0)) + SOFTENING)
    unit = separation / length[None, :]
    angular = harmonics(unit)
    orders = jnp.arange(1, radial_in.shape[0] + 1, dtype=jnp.int32).astype(jnp.float32)[:, None]
    radial_basis = (2.0 / RADIAL_RANGE) ** 0.5 * jnp.sin(orders * (jnp.pi / RADIAL_RANGE) * length[None, :]) / length[None, :]
    hidden = jax.nn.silu(jnp.dot(radial_in.T, radial_basis, precision=FULL_PRECISION))
    channels = h_table.shape[0]
    radial = jnp.dot(radial_out.T, hidden, precision=FULL_PRECISION).reshape(3, channels, -1)
    per_component = radial[COMPONENT_DEGREE]
    message = per_component * angular[:, None, :] * (h_table[:, sender] * edge_live[None, :])[None]
    return jnp.zeros((9, channels, atom_slots), jnp.float32).at[:, :, receiver].add(message)

def interact(h_table, coord_table, strain, receiver, sender, edge_live, radial_in, radial_out, mixing, product, residual, atom_slots):
    edge_count = receiver.shape[0]
    block_size = min(1024, edge_count)
    block_count = edge_count // block_size
    channels = h_table.shape[0]

    def block_sum(receiver_part, sender_part, live_part):
        return edge_terms(h_table, coord_table, strain, receiver_part, sender_part, live_part, radial_in, radial_out, atom_slots)
    checked = jax.checkpoint(block_sum)

    def advance(summed, inputs):
        return (summed + checked(inputs[0], inputs[1], inputs[2]), None)
    start = jnp.zeros((9, channels, atom_slots), jnp.float32)
    summed, unused = lax.scan(advance, start, (receiver.reshape(block_count, block_size), sender.reshape(block_count, block_size), edge_live.reshape(block_count, block_size)))
    summed = summed * float(DEG) ** (-0.5)
    scalar_part = jnp.dot(mixing[0].T, summed[0], precision=FULL_PRECISION)
    vector_mix = jnp.einsum('dc,mda->mca', mixing[1], summed[1:4], precision=FULL_PRECISION)
    tensor_mix = jnp.einsum('dc,mda->mca', mixing[2], summed[4:9], precision=FULL_PRECISION)
    invariants = jnp.concatenate([scalar_part, lax.optimization_barrier(jnp.sum(vector_mix * vector_mix, axis=0)), lax.optimization_barrier(jnp.sum(tensor_mix * tensor_mix, axis=0))], axis=0)
    return jnp.dot(product.T, invariants, precision=FULL_PRECISION) + jnp.dot(residual.T, h_table[:, :atom_slots], precision=FULL_PRECISION)

def reference(positions, species, atom_count, export_union, ghost_map, edge_receiver, edge_sender, embed, species_energy, radial_in, radial_out, mixing, product, residual, read_one, read_hidden, read_two):
    domains = DOMX * DOMY * DOMZ
    coords = positions.reshape(domains, 3, ATOMS_DEV)
    species_flat = species.reshape(domains, ATOMS_DEV)
    counts = atom_count.reshape(domains)
    union_rows = export_union.reshape(domains, UNION)
    ghost_rows = ghost_map.reshape(domains, 27, GHOSTS)
    receivers = edge_receiver.reshape(domains, EDGES)
    senders = edge_sender.reshape(domains, EDGES)
    neighbour_of = jnp.asarray(neighbour_table()).astype(jnp.int32)
    ghost_domain = jnp.broadcast_to(neighbour_of[:, :, None], (domains, 27, GHOSTS)).reshape(domains, 27 * GHOSTS)
    ghost_atom = union_rows[neighbour_of[:, :, None], ghost_rows].reshape(domains, 27 * GHOSTS)
    onehot = (species_flat[:, None, :] == jnp.arange(NSPEC, dtype=jnp.int32)[None, :, None]).astype(jnp.float32)
    atom_live = (jnp.arange(ATOMS_DEV, dtype=jnp.int32)[None, :] < counts[:, None]).astype(jnp.float32)
    edge_live = (jnp.arange(EDGES, dtype=jnp.int32)[None, :] < DEG * counts[:, None]).astype(jnp.float32)
    onehot_table = jnp.concatenate([onehot, jnp.swapaxes(onehot[ghost_domain, :, ghost_atom], 1, 2)], axis=2)
    h0_tables = jnp.einsum('sc,dsa->dca', embed, onehot_table, precision=FULL_PRECISION)
    shifts = offset_table(GHOSTS)

    def apply_layer(h_tables, coord_tables, strain, layer_index):

        def one_domain(inputs):
            return interact(inputs[0], inputs[1], strain, inputs[2], inputs[3], inputs[4], radial_in[layer_index], radial_out[layer_index], mixing[layer_index], product[layer_index], residual[layer_index], ATOMS_DEV)
        return lax.map(jax.checkpoint(one_domain), (h_tables, coord_tables, receivers, senders, edge_live))

    def energy(coords, strain):
        ghost_coords = jnp.swapaxes(coords[ghost_domain, :, ghost_atom], 1, 2) + shifts[None]
        coord_tables = jnp.concatenate([coords, ghost_coords], axis=2)
        first = apply_layer(h0_tables, coord_tables, strain, 0)
        ghost_first = jnp.swapaxes(first[ghost_domain, :, ghost_atom], 1, 2)
        second = apply_layer(jnp.concatenate([first, ghost_first], axis=2), coord_tables, strain, 1)
        energy_one = jnp.einsum('c,dca->da', read_one, first, precision=FULL_PRECISION)
        hidden_read = jax.nn.silu(jnp.einsum('ck,dca->dka', read_hidden, second, precision=FULL_PRECISION))
        energy_two = jnp.einsum('k,dka->da', read_two, hidden_read, precision=FULL_PRECISION)
        base_energy = jnp.einsum('s,dsa->da', species_energy, onehot, precision=FULL_PRECISION)
        per_atom = (base_energy + energy_one + energy_two) * atom_live
        return (jnp.sum(per_atom), per_atom)
    (total, per_atom), (coord_grad, strain_grad) = jax.value_and_grad(energy, argnums=(0, 1), has_aux=True)(coords, jnp.zeros((3, 3), jnp.float32))
    forces = -coord_grad.reshape(positions.shape)
    virial = -strain_grad / jnp.sum(counts).astype(jnp.float32)
    return (forces, per_atom.reshape(species.shape), virial)
```

```python
import functools

import jax
import jax.numpy as jnp
import numpy as np
from jax import lax
from jax.experimental import pallas as pl
from jax.experimental.pallas import tpu as pltpu
from jax.sharding import PartitionSpec as P

F32 = jnp.float32
BF16 = jnp.bfloat16
MESH = pl.DeviceIdType.MESH
HIGHEST = lax.Precision.HIGHEST

C = 128
ATOMS = 128
EDGES = 1024
CHUNK = 256
CHUNKS = EDGES // CHUNK
GHOST = 16
BLOCKS = 27
SELF = 13
TABLE = ATOMS + BLOCKS * GHOST
UNION = 64
RH = 64
DEG = 8
DOMAIN_SIDE = 5.0
SOFTENING = 0.25
STEP = float(np.pi / 18.0)
BASIS_SCALE = float((2.0 / 18.0) ** 0.5)
R3 = 3.0**0.5
R5 = 5.0**0.5
R15 = 15.0**0.5
DEGREE = (0, 1, 1, 1, 2, 2, 2, 2, 2)
SPREAD = float(DEG) ** (-0.5)
GROUPS = ((0, 8), (8, 8), (16, 8), (24, 3))


def place(j):
    return (2 - j) % 8


def row_block(k):
    return 8 * (k // 8) + place(k % 8)


def mm(a, b):
    return lax.dot_general(a, b, (((1,), (0,)), ((), ())), preferred_element_type=F32)


def mm_nt(a, b):
    return lax.dot_general(a, b, (((1,), (1,)), ((), ())), preferred_element_type=F32)


def exact(a, b, dims=((1,), (0,))):
    return lax.dot_general(a, b, (dims, ((), ())), precision=HIGHEST, preferred_element_type=F32)


def split(x):
    hi = x.astype(BF16)
    return hi, (x - hi.astype(F32)).astype(BF16)


def stack2(x):
    return jnp.concatenate(split(x), axis=0)


def mm3(w2, x):
    half = w2.shape[0] // 2
    hi, lo = split(x)
    first = mm(w2, hi)
    return first[:half] + first[half:] + mm(w2[:half], lo)


def pieces(x):
    hi = x.astype(BF16).astype(F32)
    rest = x - hi
    mid = rest.astype(BF16).astype(F32)
    low = rest - mid
    return jnp.concatenate([hi, mid, low, jnp.zeros_like(x)], axis=0).astype(BF16)


def three(y):
    return y[0:8] + y[8:16] + y[16:24]


def onehot(cond):
    return jnp.where(cond, 1.0, 0.0).astype(BF16)


def iota(shape, dim):
    return lax.broadcasted_iota(jnp.int32, shape, dim)


def sin_cos(x):
    turns = jnp.floor(x * float(1.0 / np.pi) + 0.5)
    r = x - turns * 3.140625
    r = r - turns * 9.67502593994140625e-4
    r = r - turns * 1.509957990978376432e-7
    odd = turns - 2.0 * jnp.floor(turns * 0.5)
    sign = 1.0 - 2.0 * odd
    q = r * r
    s = 1.0 / 6227020800.0
    for c in (-1.0 / 39916800.0, 1.0 / 362880.0, -1.0 / 5040.0, 1.0 / 120.0, -1.0 / 6.0, 1.0):
        s = s * q + c
    c0 = -1.0 / 87178291200.0
    for c in (
        1.0 / 479001600.0,
        -1.0 / 3628800.0,
        1.0 / 40320.0,
        -1.0 / 720.0,
        1.0 / 24.0,
        -0.5,
        1.0,
    ):
        c0 = c0 * q + c
    return sign * (r * s), sign * c0


def neighbour(k, at, sizes):
    offsets = (k // 9 - 1, k // 3 % 3 - 1, k % 3 - 1)
    return tuple(lax.rem(a + (o + n), n) for a, o, n in zip(at, offsets, sizes))


def ring_partner(s, at):
    x, y, z = at
    dx, dh, dc = s % 4, s // 4 % 2, s // 8
    high = lax.rem(y // 4 + dh, 2)
    core = lax.rem(lax.rem(z, 2) + dc, 2)
    return (lax.rem(x + dx, 4), high * 4 + lax.rem(y, 4), z // 2 * 2 + core)


def plane_partner(s, at):
    x, y, z = at
    dy, dz = s % 4, s // 4
    return (x, y // 4 * 4 + lax.rem(lax.rem(y, 4) + dy, 4), lax.rem(z // 2 + dz, 4) * 2 + lax.rem(z, 2))


def body(
    sizes,
    cnt_ref,
    pos_ref,
    spec_ref,
    uni_ref,
    gmap_ref,
    recv_ref,
    send_ref,
    emb_ref,
    sen_ref,
    rin_ref,
    rout_ref,
    mix_ref,
    prod_ref,
    res_ref,
    ro_ref,
    rh_ref,
    rt_ref,
    forces_ref,
    energy_ref,
    virial_ref,
    msg0,
    u_buf,
    snd1,
    rcv1,
    snd2,
    rcv2,
    snd3,
    rcv3,
    red_a,
    red_b,
    part_a,
    part_b,
    pst,
    prt,
    bsel,
    selt,
    sel,
    tile_i,
    tile_f,
    woT,
    wo2,
    mixT,
    mix2,
    prT,
    prod2,
    res2,
    ybuf,
    xyz,
    sbuf,
    hid,
    dsil,
    rbuf,
    hsbuf,
    dhs,
    drb,
    dyb,
    acc,
    mixed,
    table2,
    hloc,
    dbas,
    dvb,
    send_sem,
    recv_sem,
):
    at = (lax.axis_index("gx"), lax.axis_index("gy"), lax.axis_index("gz"))
    near = [k for k in range(BLOCKS) if k != SELF]
    others = list(range(1, 16))
    ids = {k: neighbour(k, at, sizes) for k in near}
    ring = {s: ring_partner(s, at) for s in others}
    plane = {s: plane_partner(s, at) for s in others}

    barrier = pltpu.get_barrier_semaphore()
    for target in list(ids.values()) + list(ring.values()) + list(plane.values()):
        pl.semaphore_signal(barrier, inc=1, device_id=target, device_id_type=MESH)

    def ship(src, dst, phase, target):
        pltpu.make_async_remote_copy(
            src_ref=src,
            dst_ref=dst,
            send_sem=send_sem.at[phase],
            recv_sem=recv_sem.at[phase],
            device_id=target,
            device_id_type=MESH,
        ).start()

    def await_bytes(ref, sem, count):
        view = ref.at[pl.ds(0, count)]
        pltpu.make_async_copy(view, view, sem).wait()

    lane = iota((1, 128), 1)
    lane_group = lane >> 4
    row8 = iota((8, 128), 0)

    u_buf[SELF] = jnp.zeros((8, 128), F32)
    rcv3[SELF] = jnp.zeros((8, 128), F32)
    rcv1[SELF] = jnp.zeros((GHOST, C), F32)
    for b in (13, 27, 28, 29, 30, 31):
        rcv2[b] = jnp.zeros((GHOST, C), F32)

    count = cnt_ref[0]
    tile_i[...] = jnp.full((8, 128), -1, jnp.int32)
    tile_i[0:1, 0:UNION] = uni_ref[...]
    union_row = tile_i[0:1, :]
    union_t = onehot(iota((ATOMS, 128), 0) == union_row)
    species = spec_ref[...]
    geometry = jnp.concatenate(
        [pos_ref[...], species.astype(F32), jnp.zeros((4, ATOMS), F32)], axis=0
    )
    offered = three(mm(pieces(geometry), union_t))
    tile_f[...] = jnp.zeros((128, 128), F32)
    tile_f[0:BLOCKS, 0:GHOST] = gmap_ref[...].astype(F32)
    tiling = onehot(iota((128, 128), 0) == (iota((128, 128), 1) & 15))
    tiled = mm(tile_f[0:32, :].astype(BF16), tiling)
    tiled = jnp.where((iota((32, 128), 1) >> 4) == (iota((32, 128), 0) & 7), tiled, 0.0)
    own_lists = [jnp.sum(tiled[8 * g : 8 * g + 8], axis=0, keepdims=True) for g in range(4)]
    for g in range(4):
        msg0[g] = jnp.where(row8 == 4, own_lists[g], offered)

    pl.semaphore_wait(barrier, len(near) + 2 * len(others))
    for k in near:
        ship(msg0.at[k // 8], u_buf.at[26 - k], 0, ids[k])

    def edge_tables(k, carry):
        at_k = pl.ds(pl.multiple_of(k * CHUNK, CHUNK), CHUNK)
        pst[k] = onehot(iota((TABLE, CHUNK), 0) == send_ref[:, at_k])
        alive = iota((1, CHUNK), 1) + k * CHUNK < DEG * count
        prt[k] = onehot((iota((ATOMS, CHUNK), 0) == recv_ref[:, at_k]) & alive)
        return carry

    lax.fori_loop(0, CHUNKS, edge_tables, 0)
    for g, (first, size) in enumerate(GROUPS):
        target = jnp.where(
            lane_group < size, lane_group * 128 + own_lists[g].astype(jnp.int32), -1
        )
        bsel[128 * first : 128 * (first + size), :] = onehot(
            iota((size * 128, 128), 0) == target
        )

    def flipped(x):
        return jnp.transpose(x, (1, 0))

    tile_f[...] = jnp.zeros((128, 128), F32)
    for t in range(2):
        tile_f[0:8, RH * t : RH * (t + 1)] = rin_ref[t]
    rin_both = tile_f[0:8, :]
    rin_hi = rin_both.astype(BF16).astype(F32)
    rin_lo = (rin_both - rin_hi).astype(BF16).astype(F32)
    rin_rows = jnp.concatenate(
        [rin_hi, rin_lo, rin_hi, rin_lo, jnp.zeros((96, 128), F32)], axis=0
    )
    winT = flipped(rin_rows).astype(BF16)[:, 0:32]
    rin_pair = jnp.concatenate([rin_hi, rin_lo], axis=0).astype(BF16)
    tile_f[...] = jnp.zeros((128, 128), F32)
    tile_f[0:6, :] = emb_ref[...]
    embT = stack2(flipped(tile_f[...]))[:, 0:16]
    for t in range(2):
        w = rout_ref[t]
        w_hi = w.astype(BF16).astype(F32)
        w_lo = (w - w_hi).astype(BF16).astype(F32)
        woT[t] = flipped(jnp.concatenate([w_hi, w_lo, w_hi, w_lo], axis=0)).astype(BF16)
        wo2[t] = jnp.concatenate([w_hi, w_lo], axis=0).astype(BF16)
        for l in range(3):
            mix2[t, l] = stack2(mix_ref[t, l])
            mixT[t, l] = stack2(flipped(mix_ref[t, l]))
        prod2[t] = stack2(prod_ref[t])
        res2[t] = stack2(res_ref[t])
        rows = [flipped(prod_ref[t, 128 * l : 128 * (l + 1), :]) for l in range(3)]
        prT[t] = stack2(jnp.concatenate(rows + [flipped(res_ref[t])], axis=1))
    tile_f[...] = jnp.zeros((128, 128), F32)
    tile_f[:, 0:16] = rh_ref[...]
    rhT = flipped(tile_f[...])[0:16]
    rh = tile_f[:, 0:16]
    tile_f[0:16, :] = jnp.zeros((16, 128), F32)
    tile_f[0:1, 0:16] = rt_ref[...]
    tile_f[1:2, 0:6] = sen_ref[...]
    scalars = flipped(tile_f[...])
    rt_col = scalars[0:16, 0:1]
    sen_col = scalars[0:16, 1:2]

    hot = jnp.where(iota((16, ATOMS), 0) == species, 1.0, 0.0)
    base_energy = jnp.sum(hot * sen_col, axis=0, keepdims=True)
    h0 = mm(embT, hot.astype(BF16))
    hloc[...] = h0[0:128] + h0[128:256]
    live = jnp.where(lane < count, 1.0, 0.0)

    await_bytes(u_buf, recv_sem.at[0], len(near))
    tables = [geometry]
    for g, (first, size) in enumerate(GROUPS):
        u_cat = jnp.concatenate([u_buf[first + j] for j in range(size)], axis=1)
        ghost = three(mm(pieces(u_cat), bsel[128 * first : 128 * (first + size), :]))
        block = first + lane_group
        ninth = jnp.where(block >= 9, 1, 0) + jnp.where(block >= 18, 1, 0)
        third = sum(jnp.where(block >= 3 * n, 1, 0) for n in range(1, 9))
        steps = (ninth, third - 3 * ninth, block - 3 * third)
        shift = jnp.zeros((8, 128), F32)
        for axis, step in enumerate(steps):
            shift = jnp.where(row8 == axis, (step - 1).astype(F32) * DOMAIN_SIDE, shift)
        ghost = ghost + shift
        tables.append(ghost[:, 0 : size * GHOST])
    coord24 = pieces(jnp.concatenate(tables, axis=1))
    local24 = coord24[:, 0:ATOMS]
    for k in range(CHUNKS):
        lanes = slice(k * CHUNK, (k + 1) * CHUNK)
        from_sender = three(mm(coord24, pst[k]))
        at_receiver = three(mm(local24, prt[k]))
        apart = from_sender - at_receiver
        xyz[:, lanes] = apart
        kind = from_sender[3:4, :].astype(jnp.int32)
        sbuf[k] = onehot(iota((16, CHUNK), 0) == kind)
    for g, (first, size) in enumerate(GROUPS):
        wanted = jnp.full((1, 128), -1.0, F32)
        for j in range(size):
            wanted = jnp.where(lane_group == place(j), u_buf[first + j][4:5, :], wanted)
        lists = onehot(iota((128, 128), 0) == wanted.astype(jnp.int32))
        chosen = mm(union_t, lists)
        selt[:, 128 * g : 128 * (g + 1)] = chosen.astype(BF16)
        sel[128 * g : 128 * (g + 1), :] = flipped(chosen).astype(BF16)

    dx, dy, dz = xyz[0:1, :], xyz[1:2, :], xyz[2:3, :]
    length = jnp.sqrt(dx * dx + dy * dy + dz * dz + SOFTENING)
    inv = 1.0 / length
    ua, ub, uc = dx * inv, dy * inv, dz * inv
    harmonic = (
        R3 * ua,
        R3 * ub,
        R3 * uc,
        R15 * ua * ub,
        R15 * ub * uc,
        (0.5 * R5) * (3.0 * uc * uc - 1.0),
        R15 * ua * uc,
        (0.5 * R15) * (ua * ua - ub * ub),
    )
    for m in range(8):
        ybuf[m : m + 1, :] = harmonic[m]
    orders = (iota((8, EDGES), 0) + 1).astype(F32) * STEP
    sines, cosines = sin_cos(orders * length)
    basis = BASIS_SCALE * sines * inv
    slope = (BASIS_SCALE * orders * cosines - basis) * inv
    b_hi, b_lo = split(basis)
    b_hi, b_lo = b_hi.astype(F32), b_lo.astype(F32)
    b_rows = jnp.concatenate([b_hi, b_hi, b_lo, b_lo], axis=0).astype(BF16)
    pre = mm(winT, b_rows)
    sig = 1.0 / (1.0 + jnp.exp(-pre))
    hidden = pre * sig
    dsil[...] = sig + hidden * (1.0 - sig)
    for t in range(2):
        h_hi, h_lo = split(hidden[RH * t : RH * (t + 1)])
        hid[t] = jnp.concatenate([h_hi, h_hi, h_lo, h_lo], axis=0)

    def lanes_of(k):
        return pl.ds(pl.multiple_of(k * CHUNK, CHUNK), CHUNK)

    def radial_of(t):
        def step(k, carry):
            rbuf[t, k] = mm(woT[t], hid[t, :, lanes_of(k)])
            return carry

        lax.fori_loop(0, CHUNKS, step, 0)

    def gather_first(k, carry):
        hs = mm(embT, sbuf[k])
        hsbuf[0, k] = hs[0:128] + hs[128:256]
        return carry

    def aggregate(t):
        acc[...] = jnp.zeros_like(acc)

        def step(k, carry):
            hs = hsbuf[t, k]
            y = ybuf[:, lanes_of(k)]
            for l in range(3):
                rh_l = rbuf[t, k, 128 * l : 128 * (l + 1), :] * hs
                for m in range(9):
                    if DEGREE[m] != l:
                        continue
                    message = rh_l if m == 0 else rh_l * y[m - 1 : m, :]
                    part = mm_nt(stack2(message), prt[k])
                    acc[:, 128 * m : 128 * (m + 1)] += part[0:128] + part[128:256]
            return carry

        lax.fori_loop(0, CHUNKS, step, 0)

    def update(t, h_local):
        agg = acc[...] * SPREAD
        for l, (lo, hi) in enumerate(((0, 1), (1, 4), (4, 9))):
            mixed[t, :, 128 * lo : 128 * hi] = mm3(mixT[t, l], agg[:, 128 * lo : 128 * hi])
        def square(lo, hi):
            total = None
            for m in range(lo, hi):
                v = mixed[t, :, 128 * m : 128 * (m + 1)]
                total = v * v if total is None else total + v * v
            return total

        invariants = jnp.concatenate(
            [mixed[t, :, 0:128], square(1, 4), square(4, 9), h_local], axis=0
        )
        return mm3(prT[t], invariants)

    def back_update(t, dh):
        dinv = mm3(prod2[t], dh)
        for l, (lo, hi) in enumerate(((0, 1), (1, 4), (4, 9))):
            grad = dinv[128 * l : 128 * (l + 1)]
            parts = []
            for m in range(lo, hi):
                if m == 0:
                    parts.append(grad)
                else:
                    parts.append(2.0 * mixed[t, :, 128 * m : 128 * (m + 1)] * grad)
            joined = parts[0] if len(parts) == 1 else jnp.concatenate(parts, axis=1)
            acc[:, 128 * lo : 128 * hi] = mm3(mix2[t, l], joined) * SPREAD

    def back_edges(t):
        def step(k, carry):
            hs = hsbuf[t, k]
            y = ybuf[:, lanes_of(k)]
            pr2 = jnp.concatenate([prt[k], prt[k]], axis=0)
            dhs_sum = None
            dy_rows = []
            for l in range(3):
                r_l = rbuf[t, k, 128 * l : 128 * (l + 1), :]
                rh_l = r_l * hs
                grad_l = None
                for m in range(9):
                    if DEGREE[m] != l:
                        continue
                    a_hi, a_lo = split(acc[:, 128 * m : 128 * (m + 1)])
                    d_m = mm(jnp.concatenate([a_hi, a_lo], axis=1), pr2)
                    if m:
                        dy_rows.append(jnp.sum(d_m * rh_l, axis=0, keepdims=True))
                        d_m = d_m * y[m - 1 : m, :]
                    grad_l = d_m if grad_l is None else grad_l + d_m
                d_hi, d_lo = split(grad_l * hs)
                drb[k, 128 * l : 128 * (l + 1), :] = d_hi
                drb[k, 384 + 128 * l : 384 + 128 * (l + 1), :] = d_lo
                if t == 1:
                    term = r_l * grad_l
                    dhs_sum = term if dhs_sum is None else dhs_sum + term
            dyb[t, :, lanes_of(k)] = jnp.concatenate(dy_rows, axis=0)
            if t == 1:
                dhs[k] = stack2(dhs_sum)
            return carry

        lax.fori_loop(0, CHUNKS, step, 0)

    def back_radial(t):
        rin_t = rin_pair[:, RH * t : RH * (t + 1)]

        def step(k, carry):
            first = mm(wo2[t], drb[k, 0:384, :])
            dhid = first[0:64] + first[64:128] + mm(wo2[t, 0:64, :], drb[k, 384:768, :])
            dpre = dhid * dsil[RH * t : RH * (t + 1), lanes_of(k)]
            p_hi, p_lo = split(dpre)
            low = mm(rin_t, p_hi)
            high = mm(rin_t, p_lo)
            dbas[t, :, lanes_of(k)] = low[0:8] + low[8:16] + high[0:8]
            return carry

        lax.fori_loop(0, CHUNKS, step, 0)

    radial_of(0)
    lax.fori_loop(0, CHUNKS, gather_first, 0)
    aggregate(0)
    h1 = update(0, hloc[...])
    h1_hi, h1_lo = split(h1)
    h1_pair = jnp.concatenate([h1_hi, h1_lo], axis=0)
    outgoing = mm_nt(sel[...], h1_pair)
    outgoing = outgoing[:, 0:128] + outgoing[:, 128:256]
    snd1[...] = outgoing.reshape(32, GHOST, C)
    for k in near:
        ship(snd1.at[row_block(k)], rcv1.at[26 - k], 1, ids[k])
    hloc[...] = h1
    table2[:, 0:ATOMS] = h1_pair
    radial_of(1)
    ro_rows = jnp.broadcast_to(ro_ref[...], (8, C))
    energy_one = exact(ro_rows, h1)[0:1]
    await_bytes(rcv1, recv_sem.at[1], len(near))
    ghosts = rcv1[...].reshape(BLOCKS * GHOST, C)
    for g, (first, size) in enumerate(GROUPS):
        part = ghosts[16 * first : 16 * (first + size)]
        if size < 8:
            part = jnp.concatenate([part, jnp.zeros((128 - 16 * size, C), F32)], axis=0)
        turned = stack2(flipped(part))
        table2[:, ATOMS + 16 * first : ATOMS + 16 * (first + size)] = turned[:, 0 : 16 * size]

    def gather_second(k, carry):
        hs = mm(table2[...], pst[k])
        hsbuf[1, k] = hs[0:128] + hs[128:256]
        return carry

    lax.fori_loop(0, CHUNKS, gather_second, 0)
    aggregate(1)
    h2 = update(1, hloc[...])
    pre_read = exact(rhT, h2)
    sig_read = 1.0 / (1.0 + jnp.exp(-pre_read))
    hid_read = pre_read * sig_read
    energy_two = jnp.sum(hid_read * rt_col, axis=0, keepdims=True)
    energy_ref[...] = (base_energy + energy_one + energy_two) * live
    dread = rt_col * live * (sig_read + hid_read * (1.0 - sig_read))
    dh2 = exact(rh, dread)

    back_update(1, dh2)
    back_edges(1)
    hgrad = None
    for k in range(CHUNKS):
        part = mm_nt(pst[k], dhs[k])
        hgrad = part if hgrad is None else hgrad + part
    hgrad = hgrad[:, 0:128] + hgrad[:, 128:256]
    snd2[...] = hgrad[ATOMS:TABLE].reshape(BLOCKS, GHOST, C)
    for k in near:
        ship(snd2.at[k], rcv2.at[row_block(26 - k)], 2, ids[k])
    own_rows = hgrad[0:ATOMS] + jnp.where(
        iota((ATOMS, C), 0) < count, jnp.broadcast_to(ro_ref[...], (ATOMS, C)), 0.0
    )
    own_cols = mm3(res2[1], dh2)
    back_radial(1)
    await_bytes(rcv2, recv_sem.at[2], len(near))
    back_hi, back_lo = split(rcv2[...].reshape(512, C))
    returned = mm(selt[...], jnp.concatenate([back_hi, back_lo], axis=1))
    dh1 = flipped(own_rows + returned[:, 0:128] + returned[:, 128:256]) + own_cols

    back_update(0, dh1)
    back_edges(0)
    back_radial(0)

    dlen = jnp.sum((dbas[0] + dbas[1]) * slope, axis=0, keepdims=True)
    g = dyb[0] + dyb[1]
    g1, g2, g3, g4, g5, g6, g7, g8 = [g[m : m + 1, :] for m in range(8)]
    da = R3 * g1 + R15 * (ub * g4 + uc * g7 + ua * g8)
    db = R3 * g2 + R15 * (ua * g4 + uc * g5 - ub * g8)
    dc = R3 * g3 + R15 * (ub * g5 + ua * g7) + (3.0 * R5) * uc * g6
    along = dlen - (da * ua + db * ub + dc * uc) * inv
    dvb[...] = jnp.zeros((8, EDGES), F32)
    dvb[0:1, :] = da * inv + ua * along
    dvb[1:2, :] = db * inv + ub * along
    dvb[2:3, :] = dc * inv + uc * along
    dvec = dvb[...]
    v_hi = dvec.astype(BF16).astype(F32)
    dv_pair = jnp.concatenate([v_hi, dvec - v_hi], axis=0).astype(BF16)
    cgrad = None
    rgrad = None
    for k in range(CHUNKS):
        lanes = slice(k * CHUNK, (k + 1) * CHUNK)
        part = mm_nt(dv_pair[:, lanes], pst[k])
        back = mm_nt(dv_pair[:, lanes], prt[k])
        cgrad = part if cgrad is None else cgrad + part
        rgrad = back if rgrad is None else rgrad + back
    cgrad = cgrad[0:8] + cgrad[8:16]
    rgrad = rgrad[0:8] + rgrad[8:16]
    for g, (first, size) in enumerate(GROUPS):
        tile = cgrad[:, ATOMS + 16 * first : ATOMS + 16 * (first + size)]
        if size < 8:
            tile = jnp.concatenate([tile, jnp.zeros((8, 128 - 16 * size), F32)], axis=1)
        snd3[g] = tile
    for k in near:
        ship(snd3.at[k // 8], rcv3.at[26 - k], 3, ids[k])
    strain = exact(dvec, xyz[...], ((1,), (1,)))
    tile_f[0:8, :] = jnp.zeros((8, 128), F32)
    tile_f[0:8, 0:8] = strain
    tile_f[3:4, 0:1] = jnp.full((1, 1), 1.0, F32) * count.astype(F32)
    own_part = tile_f[0:8, :]
    part_a[0] = own_part
    for s in others:
        ship(part_a.at[0], red_a.at[s - 1], 4, ring[s])
    await_bytes(red_a, recv_sem.at[4], 15)
    total = own_part + jnp.sum(red_a[...], axis=0)
    part_b[0] = total
    for s in others:
        ship(part_b.at[0], red_b.at[s - 1], 5, plane[s])

    await_bytes(rcv3, recv_sem.at[3], len(near))
    back = jnp.zeros((8, ATOMS), F32)
    for g, (first, size) in enumerate(GROUPS):
        tile = jnp.zeros((8, 128), F32)
        for j in range(size):
            tile = jnp.where(lane_group == place(j), rcv3[first + j], tile)
        t_hi = tile.astype(BF16).astype(F32)
        pair = jnp.concatenate([t_hi, tile - t_hi], axis=0).astype(BF16)
        got = mm(pair, sel[128 * g : 128 * (g + 1), :])
        back = back + got[0:8] + got[8:16]
    forces = rgrad - cgrad[:, 0:ATOMS] - back
    forces_ref[...] = forces[0:3]

    await_bytes(red_b, recv_sem.at[5], 15)
    total = total + jnp.sum(red_b[...], axis=0)
    virial_ref[...] = -total[0:3, 0:3] / total[3:4, 0:1]

    await_bytes(u_buf, send_sem.at[0], len(near))
    await_bytes(rcv1, send_sem.at[1], len(near))
    await_bytes(rcv2, send_sem.at[2], len(near))
    await_bytes(rcv3, send_sem.at[3], len(near))
    await_bytes(red_a, send_sem.at[4], 15)
    await_bytes(red_b, send_sem.at[5], 15)


def solution(mesh):
    sizes = tuple(mesh.shape[name] for name in ("gx", "gy", "gz"))

    def shards(
        positions,
        species,
        atom_count,
        export_union,
        ghost_map,
        edge_receiver,
        edge_sender,
        embed,
        species_energy,
        radial_in,
        radial_out,
        mixing,
        product,
        residual,
        read_one,
        read_hidden,
        read_two,
    ):
        vmem = pl.BlockSpec(memory_space=pltpu.VMEM)
        tile = (8, 128)
        scratch = [
            pltpu.VMEM((4,) + tile, F32),
            pltpu.VMEM((BLOCKS,) + tile, F32),
            pltpu.VMEM((32, GHOST, C), F32),
            pltpu.VMEM((BLOCKS, GHOST, C), F32),
            pltpu.VMEM((BLOCKS, GHOST, C), F32),
            pltpu.VMEM((32, GHOST, C), F32),
            pltpu.VMEM((4,) + tile, F32),
            pltpu.VMEM((BLOCKS,) + tile, F32),
            pltpu.VMEM((15,) + tile, F32),
            pltpu.VMEM((15,) + tile, F32),
            pltpu.VMEM((1,) + tile, F32),
            pltpu.VMEM((1,) + tile, F32),
            pltpu.VMEM((CHUNKS, TABLE, CHUNK), BF16),
            pltpu.VMEM((CHUNKS, ATOMS, CHUNK), BF16),
            pltpu.VMEM((BLOCKS * 128, 128), BF16),
            pltpu.VMEM((ATOMS, 512), BF16),
            pltpu.VMEM((512, ATOMS), BF16),
            pltpu.VMEM(tile, jnp.int32),
            pltpu.VMEM((128, 128), F32),
            pltpu.VMEM((2, 384, 256), BF16),
            pltpu.VMEM((2, 128, 384), BF16),
            pltpu.VMEM((2, 3, 256, 128), BF16),
            pltpu.VMEM((2, 3, 256, 128), BF16),
            pltpu.VMEM((2, 256, 512), BF16),
            pltpu.VMEM((2, 768, 128), BF16),
            pltpu.VMEM((2, 256, 128), BF16),
            pltpu.VMEM((8, EDGES), F32),
            pltpu.VMEM((8, EDGES), F32),
            pltpu.VMEM((CHUNKS, 16, CHUNK), BF16),
            pltpu.VMEM((2, 256, EDGES), BF16),
            pltpu.VMEM((128, EDGES), F32),
            pltpu.VMEM((2, CHUNKS, 384, CHUNK), F32),
            pltpu.VMEM((2, CHUNKS, 128, CHUNK), F32),
            pltpu.VMEM((CHUNKS, 256, CHUNK), BF16),
            pltpu.VMEM((CHUNKS, 768, CHUNK), BF16),
            pltpu.VMEM((2, 8, EDGES), F32),
            pltpu.VMEM((128, 9 * 128), F32),
            pltpu.VMEM((2, 128, 9 * 128), F32),
            pltpu.VMEM((256, TABLE), BF16),
            pltpu.VMEM((128, ATOMS), F32),
            pltpu.VMEM((2, 8, EDGES), F32),
            pltpu.VMEM((8, EDGES), F32),
            pltpu.SemaphoreType.DMA((6,)),
            pltpu.SemaphoreType.DMA((6,)),
        ]
        forces, energy, virial = pl.pallas_call(
            functools.partial(body, sizes),
            out_shape=(
                jax.ShapeDtypeStruct((3, ATOMS), F32),
                jax.ShapeDtypeStruct((1, ATOMS), F32),
                jax.ShapeDtypeStruct((3, 3), F32),
            ),
            in_specs=[pl.BlockSpec(memory_space=pltpu.SMEM)] + [vmem] * 16,
            out_specs=(vmem, vmem, vmem),
            scratch_shapes=scratch,
            compiler_params=pltpu.CompilerParams(
                collective_id=0, has_side_effects=True, vmem_limit_bytes=60 * 1024 * 1024
            ),
            name="potential",
        )(
            atom_count.reshape(1),
            positions.reshape(3, ATOMS),
            species.reshape(1, ATOMS),
            export_union.reshape(1, UNION),
            ghost_map.reshape(BLOCKS, GHOST),
            edge_receiver.reshape(1, EDGES),
            edge_sender.reshape(1, EDGES),
            embed,
            species_energy.reshape(1, -1),
            radial_in,
            radial_out,
            mixing,
            product,
            residual,
            read_one.reshape(1, C),
            read_hidden,
            read_two.reshape(1, -1),
        )
        return (
            forces.reshape(1, 1, 1, 3, ATOMS),
            energy.reshape(1, 1, 1, ATOMS),
            virial,
        )

    here = ("gx", "gy", "gz")
    in_specs = tuple(P(*here) for _ in range(7)) + tuple(P() for _ in range(10))
    out_specs = (P(*here), P(*here), P())
    return jax.shard_map(
        shards, mesh=mesh, in_specs=in_specs, out_specs=out_specs, check_vma=False
    )
```

```python
import functools

import jax
import jax.numpy as jnp
import numpy as np
from jax import lax
from jax.experimental import pallas as pl
from jax.experimental.pallas import tpu as pltpu
from jax.sharding import PartitionSpec as P

F32 = jnp.float32
BF16 = jnp.bfloat16
MESH = pl.DeviceIdType.MESH
HIGHEST = lax.Precision.HIGHEST

C = 128
ATOMS = 128
EDGES = 1024
CHUNK = 256
CHUNKS = EDGES // CHUNK
GHOST = 16
BLOCKS = 27
SELF = 13
TABLE = ATOMS + BLOCKS * GHOST
UNION = 64
RH = 64
DEG = 8
DOMAIN_SIDE = 5.0
SOFTENING = 0.25
STEP = float(np.pi / 18.0)
BASIS_SCALE = float((2.0 / 18.0) ** 0.5)
R3 = 3.0**0.5
R5 = 5.0**0.5
R15 = 15.0**0.5
DEGREE = (0, 1, 1, 1, 2, 2, 2, 2, 2)
SPREAD = float(DEG) ** (-0.5)
GROUPS = ((0, 8), (8, 8), (16, 8), (24, 3))


def place(j):
    return (2 - j) % 8


def row_block(k):
    return 8 * (k // 8) + place(k % 8)


def mm(a, b):
    return lax.dot_general(a, b, (((1,), (0,)), ((), ())), preferred_element_type=F32)


def exact(a, b, dims=((1,), (0,))):
    return lax.dot_general(a, b, (dims, ((), ())), precision=HIGHEST, preferred_element_type=F32)


def split(x):
    hi = x.astype(BF16)
    return hi, (x - hi.astype(F32)).astype(BF16)


def beside(x):
    return jnp.concatenate(split(x), axis=1)


def halves(y):
    n = y.shape[1] // 2
    return y[:, :n] + y[:, n:]


def both(x):
    return jnp.concatenate([x, x], axis=0)


def pieces(x):
    hi = x.astype(BF16).astype(F32)
    rest = x - hi
    mid = rest.astype(BF16).astype(F32)
    low = rest - mid
    return jnp.concatenate([hi, mid, low, jnp.zeros_like(x)], axis=0).astype(BF16)


def three(y):
    return y[0:8] + y[8:16] + y[16:24]


def activate(pre):
    sig = 1.0 / (1.0 + jnp.exp(-pre))
    return sig, pre * sig


def flipped(x):
    return jnp.transpose(x, (1, 0))


def onehot(cond):
    return jnp.where(cond, 1.0, 0.0).astype(BF16)


def iota(shape, dim):
    return lax.broadcasted_iota(jnp.int32, shape, dim)


def sin_cos(x):
    turns = jnp.floor(x * float(1.0 / np.pi) + 0.5)
    r = x - turns * 3.140625
    r = r - turns * 9.67502593994140625e-4
    r = r - turns * 1.509957990978376432e-7
    odd = turns - 2.0 * jnp.floor(turns * 0.5)
    sign = 1.0 - 2.0 * odd
    q = r * r
    s = 1.0 / 6227020800.0
    for c in (-1.0 / 39916800.0, 1.0 / 362880.0, -1.0 / 5040.0, 1.0 / 120.0, -1.0 / 6.0, 1.0):
        s = s * q + c
    c0 = -1.0 / 87178291200.0
    for c in (
        1.0 / 479001600.0,
        -1.0 / 3628800.0,
        1.0 / 40320.0,
        -1.0 / 720.0,
        1.0 / 24.0,
        -0.5,
        1.0,
    ):
        c0 = c0 * q + c
    return sign * (r * s), sign * c0


def neighbour(k, at, sizes):
    offsets = (k // 9 - 1, k // 3 % 3 - 1, k % 3 - 1)
    return tuple(lax.rem(a + (o + n), n) for a, o, n in zip(at, offsets, sizes))


def ring_partner(s, at):
    x, y, z = at
    dx, dh, dc = s % 4, s // 4 % 2, s // 8
    high = lax.rem(y // 4 + dh, 2)
    core = lax.rem(lax.rem(z, 2) + dc, 2)
    return (lax.rem(x + dx, 4), high * 4 + lax.rem(y, 4), z // 2 * 2 + core)


def plane_partner(s, at):
    x, y, z = at
    dy, dz = s % 4, s // 4
    return (x, y // 4 * 4 + lax.rem(lax.rem(y, 4) + dy, 4), lax.rem(z // 2 + dz, 4) * 2 + lax.rem(z, 2))


INPUTS = (
    ("pos", (3, 1, ATOMS), F32),
    ("spec", (1, ATOMS), jnp.int32),
    ("uni", (1, UNION), jnp.int32),
    ("gmap", (GHOST, BLOCKS), jnp.int32),
    ("recv", (1, EDGES), jnp.int32),
    ("send", (1, EDGES), jnp.int32),
    ("emb", (6, C), F32),
    ("sen", (1, 6), F32),
    ("rin", (2, 8, RH), F32),
    ("rout", (2, RH, 3 * C), F32),
    ("mix", (2, 3, C, C), F32),
    ("prod", (2, 3 * C, C), F32),
    ("res", (2, C, C), F32),
    ("ro", (1, C), F32),
    ("rhid", (GHOST, C), F32),
    ("rt", (1, GHOST), F32),
)
EARLY = 4
ALL = 9 * ATOMS
TILE = (8, 128)
SCRATCH = (
    ("msg0", (4,) + TILE, F32),
    ("u_buf", (BLOCKS,) + TILE, F32),
    ("snd1", (32, GHOST, C), F32),
    ("rcv1", (BLOCKS, GHOST, C), F32),
    ("snd2", (BLOCKS, GHOST, C), F32),
    ("rcv2", (32, GHOST, C), F32),
    ("snd3", (4,) + TILE, F32),
    ("rcv3", (BLOCKS,) + TILE, F32),
    ("red_a", (15,) + TILE, F32),
    ("red_b", (15,) + TILE, F32),
    ("part_a", (1,) + TILE, F32),
    ("part_b", (1,) + TILE, F32),
    ("pst", (TABLE, EDGES), BF16),
    ("ps", (EDGES, TABLE), BF16),
    ("prt", (ATOMS, EDGES), BF16),
    ("pr2", (EDGES, 2 * ATOMS), BF16),
    ("ybc", (8, EDGES, 128), F32),
    ("bsel", (BLOCKS * 128, 128), BF16),
    ("selt", (ATOMS, 512), BF16),
    ("sel", (512, ATOMS), BF16),
    ("tile_i", TILE, jnp.int32),
    ("tile_f", (128, 128), F32),
    ("win", (48, 512), BF16),
    ("winT", (256, 128), BF16),
    ("wo4", (2, 256, 384), BF16),
    ("woT", (2, 768, 256), BF16),
    ("mix4", (2, 3, 256, 256), BF16),
    ("mixT", (2, 3, 256, 256), BF16),
    ("pr4", (2, 512, 256), BF16),
    ("prT", (2, 256, 768), BF16),
    ("resT", (256, 256), BF16),
    ("ybuf", (8, EDGES), F32),
    ("xyz", (8, EDGES), F32),
    ("kind", (16, EDGES), F32),
    ("hcat", (2, EDGES, 256), BF16),
    ("dsil", (EDGES, 128), F32),
    ("pre1", (EDGES, 128), F32),
    ("ycol", (EDGES, 128), F32),
    ("rbuf", (2, EDGES, 384), F32),
    ("hsbuf", (2, EDGES, 128), F32),
    ("dap", (256, ALL), BF16),
    ("grads", (EDGES, 384), F32),
    ("dhp", (EDGES, 256), BF16),
    ("dhid", (EDGES, 128), F32),
    ("dyc", (EDGES, 128), F32),
    ("mixed", (2, ALL, 128), F32),
    ("table", (TABLE - ATOMS, 256), BF16),
    ("hloc", (ATOMS, 128), F32),
    ("dvb", TILE[:1] + (EDGES,), F32),
)


def body(sizes, cnt_ref, *refs):
    names = [name for name, _, _ in INPUTS]
    hbm = dict(zip(names, refs))
    forces_ref, energy_ref, virial_ref = refs[len(names) : len(names) + 3]
    rest = refs[len(names) + 3 :]
    vm = dict(zip(names, rest))
    rest = rest[len(names) :]
    v = dict(zip([name for name, _, _ in SCRATCH], rest))
    send_sem, recv_sem, load_sem = rest[len(SCRATCH) :]

    at = (lax.axis_index("gx"), lax.axis_index("gy"), lax.axis_index("gz"))
    near = [k for k in range(BLOCKS) if k != SELF]
    others = list(range(1, 16))
    ids = {k: neighbour(k, at, sizes) for k in near}
    ring = {s: ring_partner(s, at) for s in others}
    plane = {s: plane_partner(s, at) for s in others}

    u_buf, rcv1, rcv2, rcv3 = v["u_buf"], v["rcv1"], v["rcv2"], v["rcv3"]
    tile_i, tile_f = v["tile_i"], v["tile_f"]

    u_buf[SELF] = jnp.zeros((8, 128), F32)
    rcv1[SELF] = jnp.zeros((GHOST, C), F32)
    for b in (13, 27, 28, 29, 30, 31):
        rcv2[b] = jnp.zeros((GHOST, C), F32)
    rcv3[...] = jnp.zeros((BLOCKS, 8, 128), F32)
    v["red_a"][...] = jnp.zeros((15, 8, 128), F32)
    v["red_b"][...] = jnp.zeros((15, 8, 128), F32)

    loads = [
        pltpu.make_async_copy(hbm[name], vm[name], load_sem.at[n]) for n, name in enumerate(names)
    ]
    for load in loads[:EARLY]:
        load.start()
    barrier = pltpu.get_barrier_semaphore()
    for target in list(ids.values()) + list(ring.values()) + list(plane.values()):
        pl.semaphore_signal(barrier, inc=1, device_id=target, device_id_type=MESH)
    for load in loads[EARLY:]:
        load.start()

    def ship(src, dst, phase, target):
        pltpu.make_async_remote_copy(
            src_ref=src,
            dst_ref=dst,
            send_sem=send_sem.at[phase],
            recv_sem=recv_sem.at[phase],
            device_id=target,
            device_id_type=MESH,
        ).start()

    def await_bytes(ref, sem, count, rows=None):
        view = ref.at[pl.ds(0, count)] if rows is None else ref.at[pl.ds(0, count), pl.ds(0, rows)]
        pltpu.make_async_copy(view, view, sem).wait()

    lane = iota((1, 128), 1)
    lane_group = lane >> 4
    row8 = iota((8, 128), 0)
    count = cnt_ref[0]
    for load in loads[:EARLY]:
        load.wait()
    tile_i[...] = jnp.full((8, 128), -1, jnp.int32)
    tile_i[0:1, 0:UNION] = vm["uni"][...]
    union_row = tile_i[0:1, :]
    union_t = onehot(iota((ATOMS, 128), 0) == union_row)
    species = vm["spec"][...]
    pos = vm["pos"]
    geometry = jnp.concatenate(
        [pos[0], pos[1], pos[2], species.astype(F32), jnp.zeros((4, ATOMS), F32)], axis=0
    )
    offered = three(mm(pieces(geometry), union_t))
    tile_f[...] = jnp.zeros((128, 128), F32)
    tile_f[0:GHOST, 0:BLOCKS] = vm["gmap"][...].astype(F32)
    turned_map = flipped(tile_f[...])[0:32, :]
    tiling = onehot(iota((128, 128), 0) == (iota((128, 128), 1) & 15))
    tiled = mm(turned_map.astype(BF16), tiling)
    tiled = jnp.where((iota((32, 128), 1) >> 4) == (iota((32, 128), 0) & 7), tiled, 0.0)
    own_lists = [jnp.sum(tiled[8 * g : 8 * g + 8], axis=0, keepdims=True) for g in range(4)]
    for g in range(4):
        v["msg0"][g] = jnp.where(row8 == 4, own_lists[g], offered)

    pl.semaphore_wait(barrier, len(near) + 2 * len(others))
    for k in near:
        ship(v["msg0"].at[k // 8], u_buf.at[26 - k], 0, ids[k])

    for load in loads[EARLY:]:
        load.wait()
    lanes_all = iota((1, EDGES), 1)

    def edge_tables(k, carry):
        lanes = pl.ds(pl.multiple_of(k * 128, 128), 128)
        rows = pl.ds(pl.multiple_of(k * 128, 128), 128)
        to = vm["send"][:, lanes]
        by = vm["recv"][:, lanes]
        alive = iota((1, 128), 1) + k * 128 < DEG * count
        by = jnp.where(alive, by, -1)
        v["pst"][:, lanes] = onehot(iota((TABLE, 128), 0) == to)
        v["prt"][:, lanes] = onehot(iota((ATOMS, 128), 0) == by)
        to_col = flipped(jnp.broadcast_to(to.astype(F32), (128, 128))).astype(jnp.int32)
        by_col = flipped(jnp.broadcast_to(by.astype(F32), (128, 128))).astype(jnp.int32)
        column = iota((128, 128), 1)
        for b in range(4):
            v["ps"][rows, 128 * b : 128 * (b + 1)] = onehot(column + 128 * b == to_col)
        last = TABLE - 512
        v["ps"][rows, 512:TABLE] = onehot(column[:, 0:last] + 512 == to_col[:, 0:last])
        mine = onehot(column == by_col)
        v["pr2"][rows, :] = jnp.concatenate([mine, mine], axis=1)
        return carry

    lax.fori_loop(0, EDGES // 128, edge_tables, 0)
    for g, (first, size) in enumerate(GROUPS):
        target = jnp.where(
            lane_group < size, lane_group * 128 + own_lists[g].astype(jnp.int32), -1
        )
        v["bsel"][128 * first : 128 * (first + size), :] = onehot(
            iota((size * 128, 128), 0) == target
        )

    tile_f[...] = jnp.zeros((128, 128), F32)
    for t in range(2):
        tile_f[0:8, RH * t : RH * (t + 1)] = vm["rin"][t]
        tile_f[8 * t + 8 : 8 * t + 16, 0:RH] = vm["rin"][t]
        tile_f[8 * t + 8 : 8 * t + 16, RH : 2 * RH] = vm["rin"][t]
    tile_f[32:38, :] = vm["emb"][...]
    rin_both = tile_f[0:8, :]
    rin_hi = rin_both.astype(BF16).astype(F32)
    rin_lo = (rin_both - rin_hi).astype(BF16).astype(F32)
    emb_pair = beside(tile_f[32:48, :])
    for t in range(2):
        twice = tile_f[8 * t + 8 : 8 * t + 16, :]
        twice_hi = twice.astype(BF16).astype(F32)
        twice_lo = (twice - twice_hi).astype(BF16).astype(F32)
        v["win"][:, 128 * t : 128 * (t + 1)] = jnp.concatenate(
            [twice_hi, twice_lo, twice_hi, twice_lo, jnp.zeros((16, 128), F32)], axis=0
        ).astype(BF16)
    v["win"][:, 256:512] = jnp.concatenate([jnp.zeros((32, 256), BF16), emb_pair], axis=0)
    turned = flipped(
        jnp.concatenate([rin_hi, rin_lo, jnp.zeros((112, 128), F32)], axis=0)
    ).astype(BF16)
    v["winT"][...] = both(turned)
    for t in range(2):
        w = vm["rout"][t]
        w_hi, w_lo = split(w)
        v["wo4"][t] = jnp.concatenate([w_hi, w_lo, w_hi, w_lo], axis=0)
        tile_f[...] = jnp.zeros((128, 128), F32)
        for l in range(3):
            tile_f[RH * t : RH * (t + 1), :] = w[:, 128 * l : 128 * (l + 1)]
            turned = beside(flipped(tile_f[...]))
            v["woT"][t, 128 * l : 128 * (l + 1), :] = turned
            v["woT"][t, 384 + 128 * l : 384 + 128 * (l + 1), :] = turned
            v["mix4"][t, l] = both(beside(vm["mix"][t, l]))
            v["mixT"][t, l] = both(beside(flipped(vm["mix"][t, l])))
            block = slice(128 * l, 128 * (l + 1))
            v["pr4"][t, block, :] = beside(vm["prod"][t, block, :])
            p_hi, p_lo = split(flipped(vm["prod"][t, block, :]))
            v["prT"][t, :, block] = both(p_hi)
            v["prT"][t, :, 384 + 128 * l : 384 + 128 * (l + 1)] = both(p_lo)
        v["pr4"][t, 384:512, :] = beside(vm["res"][t])
    v["resT"][...] = both(beside(flipped(vm["res"][1])))
    rhT = vm["rhid"][...]
    tile_f[...] = jnp.zeros((128, 128), F32)
    tile_f[0:16, :] = rhT
    rh = flipped(tile_f[...])[:, 0:16]
    rt_row = vm["rt"][...]
    tile_f[0:16, :] = jnp.zeros((16, 128), F32)
    tile_f[0:1, 0:6] = vm["sen"][...]
    sen_col = flipped(tile_f[...])[0:16, 0:1]
    hot = jnp.where(iota((16, ATOMS), 0) == species, 1.0, 0.0)
    base_energy = jnp.sum(hot * sen_col, axis=0, keepdims=True)
    hot_rows = flipped(jnp.concatenate([hot, jnp.zeros((112, ATOMS), F32)], axis=0))
    v["hloc"][...] = halves(mm(hot_rows[:, 0:16].astype(BF16), emb_pair))
    live = jnp.where(lane < count, 1.0, 0.0)
    live_col = jnp.where(iota((ATOMS, C), 0) < count, 1.0, 0.0)

    await_bytes(u_buf, recv_sem.at[0], len(near))
    tables = [geometry]
    for g, (first, size) in enumerate(GROUPS):
        u_cat = jnp.concatenate([u_buf[first + j] for j in range(size)], axis=1)
        ghost = three(mm(pieces(u_cat), v["bsel"][128 * first : 128 * (first + size), :]))
        block = first + lane_group
        ninth = jnp.where(block >= 9, 1, 0) + jnp.where(block >= 18, 1, 0)
        third = sum(jnp.where(block >= 3 * n, 1, 0) for n in range(1, 9))
        steps = (ninth, third - 3 * ninth, block - 3 * third)
        shift = jnp.zeros((8, 128), F32)
        for axis, step in enumerate(steps):
            shift = jnp.where(row8 == axis, (step - 1).astype(F32) * DOMAIN_SIDE, shift)
        ghost = ghost + shift
        tables.append(ghost[:, 0 : size * GHOST])
    coord24 = pieces(jnp.concatenate(tables, axis=1))
    from_sender = three(mm(coord24, v["pst"][...]))
    at_receiver = three(mm(coord24[:, 0:ATOMS], v["prt"][...]))
    apart = from_sender - at_receiver
    v["xyz"][...] = apart
    kind = jnp.where(
        iota((16, EDGES), 0) == from_sender[3:4, :].astype(jnp.int32), 1.0, 0.0
    )

    dx, dy, dz = apart[0:1, :], apart[1:2, :], apart[2:3, :]
    length = jnp.sqrt(dx * dx + dy * dy + dz * dz + SOFTENING)
    inv = 1.0 / length
    ua, ub, uc = dx * inv, dy * inv, dz * inv
    harmonic = (
        R3 * ua,
        R3 * ub,
        R3 * uc,
        R15 * ua * ub,
        R15 * ub * uc,
        (0.5 * R5) * (3.0 * uc * uc - 1.0),
        R15 * ua * uc,
        (0.5 * R15) * (ua * ua - ub * ub),
    )
    for m in range(8):
        v["ybuf"][m : m + 1, :] = harmonic[m]
    orders = (iota((8, EDGES), 0) + 1).astype(F32) * STEP
    sines, cosines = sin_cos(orders * length)
    basis = BASIS_SCALE * sines * inv
    slope = (BASIS_SCALE * orders * cosines - basis) * inv
    b_hi, b_lo = split(basis)
    b_hi, b_lo = b_hi.astype(F32), b_lo.astype(F32)
    v_rows = jnp.concatenate([b_hi, b_hi, b_lo, b_lo, kind], axis=0)
    for j in range(EDGES // 128):
        span = slice(128 * j, 128 * (j + 1))
        block = jnp.concatenate([v_rows[:, span], jnp.zeros((80, 128), F32)], axis=0)
        turned = flipped(block)[:, 0:48].astype(BF16)
        out = mm(turned, v["win"][...])
        v["hsbuf"][0, span, :] = halves(out[:, 256:512])
        v["pre1"][span, :] = out[:, 128:256]
        sig, hidden = activate(out[:, 0:128])
        v["dsil"][span, :] = sig + hidden * (1.0 - sig)
        v["hcat"][0, span, :] = beside(hidden)
        y_block = jnp.concatenate([v["ybuf"][:, span], jnp.zeros((120, 128), F32)], axis=0)
        v["ycol"][span, :] = flipped(y_block)

    def rows_of(k):
        return pl.ds(pl.multiple_of(k * CHUNK, CHUNK), CHUNK)

    spans = ((0, 1), (1, 4), (4, 9))

    def hidden_second():
        low = iota((CHUNK, 128), 1) < RH

        def step(k, carry):
            rows = rows_of(k)
            sig, hidden = activate(v["pre1"][rows, :])
            v["dsil"][rows, :] = jnp.where(
                low, v["dsil"][rows, :], sig + hidden * (1.0 - sig)
            )
            v["hcat"][1, rows, :] = beside(hidden)
            return carry

        lax.fori_loop(0, CHUNKS, step, 0)

    def radial_of(t):
        def step(k, carry):
            v["rbuf"][t, rows_of(k), :] = mm(v["hcat"][t, rows_of(k), :], v["wo4"][t])
            return carry

        lax.fori_loop(0, CHUNKS, step, 0)

    def update(t, h_local):
        hs = v["hsbuf"][t]
        for l, (lo, hi) in enumerate(spans):
            rows = slice(128 * lo, 128 * hi)
            weighted = v["rbuf"][t, :, 128 * l : 128 * (l + 1)] * hs
            sums = []
            for m in range(lo, hi):
                message = weighted
                if m:
                    if t == 0:
                        v["ybc"][m - 1] = jnp.broadcast_to(
                            v["ycol"][:, m - 1 : m], (EDGES, 128)
                        )
                    message = weighted * v["ybc"][m - 1]
                sums.append(halves(mm(v["prt"][...], beside(message))))
            agg = (sums[0] if l == 0 else jnp.concatenate(sums, axis=0)) * SPREAD
            v["mixed"][t, rows, :] = halves(mm(beside(agg), v["mix4"][t, l]))

        def square(lo, hi):
            total = None
            for m in range(lo, hi):
                x = v["mixed"][t, 128 * m : 128 * (m + 1), :]
                total = x * x if total is None else total + x * x
            return total

        invariants = jnp.concatenate(
            [v["mixed"][t, 0:128, :], square(1, 4), square(4, 9), h_local], axis=1
        )
        x_hi, x_lo = split(invariants)
        out = mm(jnp.concatenate([x_hi, x_lo], axis=0), v["pr4"][t])
        out = out[0:128] + out[128:256]
        return halves(out)

    def back_update(t, dh):
        dinv = halves(mm(beside(dh), v["prT"][t]))
        for l, (lo, hi) in enumerate(spans):
            grad = dinv[:, 128 * l : 128 * (l + 1)]
            if l == 0:
                parts = grad
            else:
                parts = jnp.concatenate(
                    [
                        2.0 * v["mixed"][t, 128 * m : 128 * (m + 1), :] * grad
                        for m in range(lo, hi)
                    ],
                    axis=0,
                )
            out = halves(mm(beside(parts), v["mixT"][t, l])) * SPREAD
            for m in range(lo, hi):
                v["dap"][:, 128 * m : 128 * (m + 1)] = jnp.concatenate(
                    split(out[128 * (m - lo) : 128 * (m - lo + 1)]), axis=0
                )

    def back_edges(t, rows, grads, angles):
        hit = v["pr2"][rows, :]
        lanes = iota((CHUNK, 128), 1)
        turned = v["dyc"][rows, :] if angles else None
        hs = v["hsbuf"][t, rows, :] if angles else None
        out = []
        for l, (lo, hi) in enumerate(spans):
            weighted = v["rbuf"][t, rows, 128 * l : 128 * (l + 1)] * hs if angles else None
            total = None
            for m in range(lo, hi):
                if not grads and not m:
                    continue
                d_m = mm(hit, v["dap"][:, 128 * m : 128 * (m + 1)])
                if m and angles:
                    along = jnp.sum(d_m * weighted, axis=1, keepdims=True)
                    turned = jnp.where(lanes == m - 1, turned + along, turned)
                if grads:
                    term = d_m * v["ybc"][m - 1, rows, :] if m else d_m
                    total = term if total is None else total + term
            out.append(total)
        if angles:
            v["dyc"][rows, :] = turned
        return out

    def back_radial(t, rows, grads):
        hs = v["hsbuf"][t, rows, :]
        parts = [split(grad * hs) for grad in grads]
        dr = jnp.concatenate([p[0] for p in parts] + [p[1] for p in parts], axis=1)
        out = halves(mm(dr, v["woT"][t]))
        if t == 1:
            v["dhid"][rows, :] = out
        else:
            v["dhid"][rows, :] += out

    radial_of(0)
    h1 = update(0, v["hloc"][...])
    for g, (first, size) in enumerate(GROUPS):
        wanted = jnp.full((1, 128), -1.0, F32)
        for j in range(size):
            wanted = jnp.where(lane_group == place(j), u_buf[first + j][4:5, :], wanted)
        lists = onehot(iota((128, 128), 0) == wanted.astype(jnp.int32))
        chosen = mm(union_t, lists)
        v["selt"][:, 128 * g : 128 * (g + 1)] = chosen.astype(BF16)
        v["sel"][128 * g : 128 * (g + 1), :] = flipped(chosen).astype(BF16)
    h1_pair = beside(h1)
    v["snd1"][...] = halves(mm(v["sel"][...], h1_pair)).reshape(32, GHOST, C)
    for k in near:
        ship(v["snd1"].at[row_block(k)], rcv1.at[26 - k], 1, ids[k])
    v["hloc"][...] = h1
    hidden_second()
    radial_of(1)
    ro_rows = jnp.broadcast_to(vm["ro"][...], (8, C))
    energy_one = exact(ro_rows, h1, ((1,), (1,)))[0:1]

    def gather_local(k, carry):
        v["hsbuf"][1, rows_of(k), :] = halves(mm(v["ps"][rows_of(k), 0:ATOMS], h1_pair))
        return carry

    lax.fori_loop(0, CHUNKS, gather_local, 0)
    await_bytes(rcv1, recv_sem.at[1], len(near))
    v["table"][...] = beside(rcv1[...].reshape(BLOCKS * GHOST, C))

    def gather_second(k, carry):
        v["hsbuf"][1, rows_of(k), :] += halves(
            mm(v["ps"][rows_of(k), ATOMS:TABLE], v["table"][...])
        )
        return carry

    lax.fori_loop(0, CHUNKS, gather_second, 0)
    h2 = update(1, v["hloc"][...])
    pre_read = exact(h2, rh)
    sig_read = 1.0 / (1.0 + jnp.exp(-pre_read))
    hid_read = pre_read * sig_read
    dread = rt_row * live_col[:, 0:16] * (sig_read + hid_read * (1.0 - sig_read))
    dh2 = exact(dread, rhT)

    back_update(1, dh2)

    def features_second(k, carry):
        rows = rows_of(k)
        grads = back_edges(1, rows, True, False)
        total = None
        for l in range(3):
            v["grads"][rows, 128 * l : 128 * (l + 1)] = grads[l]
            term = v["rbuf"][1, rows, 128 * l : 128 * (l + 1)] * grads[l]
            total = term if total is None else total + term
        v["dhp"][rows, :] = beside(total)
        return carry

    lax.fori_loop(0, CHUNKS, features_second, 0)
    hgrad = halves(mm(v["pst"][ATOMS:TABLE, :], v["dhp"][...]))
    v["snd2"][...] = hgrad.reshape(BLOCKS, GHOST, C)
    for k in near:
        ship(v["snd2"].at[k], rcv2.at[row_block(26 - k)], 2, ids[k])
    own = (
        halves(mm(v["pst"][0:ATOMS, :], v["dhp"][...]))
        + live_col * jnp.broadcast_to(vm["ro"][...], (ATOMS, C))
        + halves(mm(beside(dh2), v["resT"][...]))
    )
    rt_rows = jnp.broadcast_to(rt_row, (8, GHOST))
    energy_two = exact(rt_rows, hid_read, ((1,), (1,)))[0:1]
    energy_ref[...] = (base_energy + energy_one + energy_two) * live
    v["dyc"][...] = jnp.zeros((EDGES, 128), F32)

    def angles_second(k, carry):
        rows = rows_of(k)
        back_edges(1, rows, False, True)
        back_radial(1, rows, [v["grads"][rows, 128 * l : 128 * (l + 1)] for l in range(3)])
        return carry

    lax.fori_loop(0, CHUNKS, angles_second, 0)
    await_bytes(rcv2, recv_sem.at[2], len(near))
    dh1 = own + halves(mm(v["selt"][...], beside(rcv2[...].reshape(512, C))))

    back_update(0, dh1)

    def edges_first(k, carry):
        rows = rows_of(k)
        back_radial(0, rows, back_edges(0, rows, True, True))
        return carry

    lax.fori_loop(0, CHUNKS, edges_first, 0)

    dbas, dys = [], []
    for j in range(EDGES // 128):
        span = slice(128 * j, 128 * (j + 1))
        dpre = v["dhid"][span, :] * v["dsil"][span, :]
        dbas.append(flipped(mm(beside(dpre), v["winT"][...]))[0:16])
        dys.append(flipped(v["dyc"][span, :])[0:8])
    g = jnp.concatenate(dys, axis=1)
    dbas = jnp.concatenate(dbas, axis=1)
    dbas = dbas[0:8] + dbas[8:16]
    dlen = jnp.sum(dbas * slope, axis=0, keepdims=True)
    g1, g2, g3, g4, g5, g6, g7, g8 = [g[m : m + 1, :] for m in range(8)]
    da = R3 * g1 + R15 * (ub * g4 + uc * g7 + ua * g8)
    db = R3 * g2 + R15 * (ua * g4 + uc * g5 - ub * g8)
    dc = R3 * g3 + R15 * (ub * g5 + ua * g7) + (3.0 * R5) * uc * g6
    along = dlen - (da * ua + db * ub + dc * uc) * inv
    dvb = v["dvb"]
    dvb[...] = jnp.zeros((8, EDGES), F32)
    dvb[0:1, :] = da * inv + ua * along
    dvb[1:2, :] = db * inv + ub * along
    dvb[2:3, :] = dc * inv + uc * along
    dvec = dvb[...]
    v_hi = dvec.astype(BF16).astype(F32)
    dv_pair = jnp.concatenate([v_hi, dvec - v_hi], axis=0).astype(BF16)
    cgrad = mm(dv_pair, v["ps"][...])
    cgrad = cgrad[0:8] + cgrad[8:16]
    for g, (first, size) in enumerate(GROUPS):
        tile = cgrad[:, ATOMS + 16 * first : ATOMS + 16 * (first + size)]
        if size < 8:
            tile = jnp.concatenate([tile, jnp.zeros((8, 128 - 16 * size), F32)], axis=1)
        v["snd3"][g] = tile
    for k in near:
        ship(v["snd3"].at[k // 8, pl.ds(0, 3)], rcv3.at[26 - k, pl.ds(0, 3)], 3, ids[k])
    strain = exact(dvec, v["xyz"][...], ((1,), (1,)))
    tile_f[0:8, :] = jnp.zeros((8, 128), F32)
    tile_f[0:8, 0:8] = strain
    tile_f[3:4, 0:1] = jnp.full((1, 1), 1.0, F32) * count.astype(F32)
    own_part = tile_f[0:8, :]
    red_a, red_b, part_a, part_b = v["red_a"], v["red_b"], v["part_a"], v["part_b"]
    part_a[0] = own_part
    for s in others:
        ship(part_a.at[0, pl.ds(0, 4)], red_a.at[s - 1, pl.ds(0, 4)], 4, ring[s])
    rgrad = mm(dv_pair, v["pr2"][:, 0:ATOMS])
    rgrad = rgrad[0:8] + rgrad[8:16]
    await_bytes(red_a, recv_sem.at[4], 15, 4)
    total = own_part + jnp.sum(red_a[...], axis=0)
    part_b[0] = total
    for s in others:
        ship(part_b.at[0, pl.ds(0, 4)], red_b.at[s - 1, pl.ds(0, 4)], 5, plane[s])

    await_bytes(rcv3, recv_sem.at[3], len(near), 3)
    back = jnp.zeros((8, ATOMS), F32)
    for g, (first, size) in enumerate(GROUPS):
        tile = jnp.zeros((8, 128), F32)
        for j in range(size):
            tile = jnp.where(lane_group == place(j), rcv3[first + j], tile)
        t_hi = tile.astype(BF16).astype(F32)
        pair = jnp.concatenate([t_hi, tile - t_hi], axis=0).astype(BF16)
        got = mm(pair, v["sel"][128 * g : 128 * (g + 1), :])
        back = back + got[0:8] + got[8:16]
    forces = rgrad - cgrad[:, 0:ATOMS] - back
    for axis in range(3):
        forces_ref[axis] = forces[axis : axis + 1]

    await_bytes(red_b, recv_sem.at[5], 15, 4)
    total = total + jnp.sum(red_b[...], axis=0)
    virial_ref[...] = -total[0:3, 0:3] / total[3:4, 0:1]

    await_bytes(u_buf, send_sem.at[0], len(near))
    await_bytes(rcv1, send_sem.at[1], len(near))
    await_bytes(rcv2, send_sem.at[2], len(near))
    await_bytes(rcv3, send_sem.at[3], len(near), 3)
    await_bytes(red_a, send_sem.at[4], 15, 4)
    await_bytes(red_b, send_sem.at[5], 15, 4)


def solution(mesh):
    sizes = tuple(mesh.shape[name] for name in ("gx", "gy", "gz"))

    def shards(
        positions,
        species,
        atom_count,
        export_union,
        ghost_map,
        edge_receiver,
        edge_sender,
        embed,
        species_energy,
        radial_in,
        radial_out,
        mixing,
        product,
        residual,
        read_one,
        read_hidden,
        read_two,
    ):
        vmem = pl.BlockSpec(memory_space=pltpu.VMEM)
        scratch = [pltpu.VMEM(shape, kind) for _, shape, kind in INPUTS + SCRATCH]
        scratch += [
            pltpu.SemaphoreType.DMA((6,)),
            pltpu.SemaphoreType.DMA((6,)),
            pltpu.SemaphoreType.DMA((len(INPUTS),)),
        ]
        forces, energy, virial = pl.pallas_call(
            functools.partial(body, sizes),
            out_shape=(
                jax.ShapeDtypeStruct((3, 1, ATOMS), F32),
                jax.ShapeDtypeStruct((1, ATOMS), F32),
                jax.ShapeDtypeStruct((3, 3), F32),
            ),
            in_specs=[pl.BlockSpec(memory_space=pltpu.SMEM)]
            + [pl.BlockSpec(memory_space=pl.ANY)] * len(INPUTS),
            out_specs=(vmem, vmem, vmem),
            scratch_shapes=scratch,
            compiler_params=pltpu.CompilerParams(
                collective_id=0, has_side_effects=True, vmem_limit_bytes=60 * 1024 * 1024
            ),
            name="potential",
        )(
            atom_count.reshape(1),
            positions.reshape(3, 1, ATOMS),
            species.reshape(1, ATOMS),
            export_union.reshape(1, UNION),
            ghost_map.reshape(BLOCKS, GHOST).T,
            edge_receiver.reshape(1, EDGES),
            edge_sender.reshape(1, EDGES),
            embed,
            species_energy.reshape(1, -1),
            radial_in,
            radial_out,
            mixing,
            product,
            residual,
            read_one.reshape(1, C),
            read_hidden.T,
            read_two.reshape(1, -1),
        )
        return (
            forces.reshape(1, 1, 1, 3, ATOMS),
            energy.reshape(1, 1, 1, ATOMS),
            virial,
        )

    here = ("gx", "gy", "gz")
    in_specs = tuple(P(*here) for _ in range(7)) + tuple(P() for _ in range(10))
    out_specs = (P(*here), P(*here), P())
    return jax.shard_map(
        shards, mesh=mesh, in_specs=in_specs, out_specs=out_specs, check_vma=False
    )
```

```python
import functools

import jax
import jax.numpy as jnp
import numpy as np
from jax import lax
from jax.experimental import pallas as pl
from jax.experimental.pallas import tpu as pltpu
from jax.sharding import PartitionSpec as P

F32 = jnp.float32
BF16 = jnp.bfloat16
MESH = pl.DeviceIdType.MESH
HIGHEST = lax.Precision.HIGHEST

C = 128
ATOMS = 128
EDGES = 1024
CHUNK = 256
CHUNKS = EDGES // CHUNK
GHOST = 16
BLOCKS = 27
SELF = 13
TABLE = ATOMS + BLOCKS * GHOST
UNION = 64
RH = 64
DEG = 8
DOMAIN_SIDE = 5.0
SOFTENING = 0.25
STEP = float(np.pi / 18.0)
BASIS_SCALE = float((2.0 / 18.0) ** 0.5)
R3 = 3.0**0.5
R5 = 5.0**0.5
R15 = 15.0**0.5
DEGREE = (0, 1, 1, 1, 2, 2, 2, 2, 2)
SPREAD = float(DEG) ** (-0.5)
GROUPS = ((0, 8), (8, 8), (16, 8), (24, 3))


def place(j):
    return (2 - j) % 8


def row_block(k):
    return 8 * (k // 8) + place(k % 8)


def mm(a, b):
    return lax.dot_general(a, b, (((1,), (0,)), ((), ())), preferred_element_type=F32)


def exact(a, b, dims=((1,), (0,))):
    return lax.dot_general(a, b, (dims, ((), ())), precision=HIGHEST, preferred_element_type=F32)


def split(x):
    hi = x.astype(BF16)
    return hi, (x - hi.astype(F32)).astype(BF16)


def beside(x):
    return jnp.concatenate(split(x), axis=1)


def halves(y):
    n = y.shape[1] // 2
    return y[:, :n] + y[:, n:]


def both(x):
    return jnp.concatenate([x, x], axis=0)


def pieces(x):
    hi = x.astype(BF16).astype(F32)
    rest = x - hi
    mid = rest.astype(BF16).astype(F32)
    low = rest - mid
    return jnp.concatenate([hi, mid, low, jnp.zeros_like(x)], axis=0).astype(BF16)


def three(y):
    return y[0:8] + y[8:16] + y[16:24]


def activate(pre):
    sig = 1.0 / (1.0 + jnp.exp(-pre))
    return sig, pre * sig


def flipped(x):
    return jnp.transpose(x, (1, 0))


def onehot(cond):
    return jnp.where(cond, 1.0, 0.0).astype(BF16)


def iota(shape, dim):
    return lax.broadcasted_iota(jnp.int32, shape, dim)


def sin_cos(x):
    turns = jnp.floor(x * float(1.0 / np.pi) + 0.5)
    r = x - turns * 3.140625
    r = r - turns * 9.67502593994140625e-4
    r = r - turns * 1.509957990978376432e-7
    odd = turns - 2.0 * jnp.floor(turns * 0.5)
    sign = 1.0 - 2.0 * odd
    q = r * r
    s = 1.0 / 6227020800.0
    for c in (-1.0 / 39916800.0, 1.0 / 362880.0, -1.0 / 5040.0, 1.0 / 120.0, -1.0 / 6.0, 1.0):
        s = s * q + c
    c0 = -1.0 / 87178291200.0
    for c in (
        1.0 / 479001600.0,
        -1.0 / 3628800.0,
        1.0 / 40320.0,
        -1.0 / 720.0,
        1.0 / 24.0,
        -0.5,
        1.0,
    ):
        c0 = c0 * q + c
    return sign * (r * s), sign * c0


def swapped(at):
    x, y, z = at
    return (lax.rem(y, 4), y // 4 * 4 + x, z)


def neighbour(k, domain, sizes):
    offsets = (k // 9 - 1, k // 3 % 3 - 1, k % 3 - 1)
    return swapped(tuple(lax.rem(a + (o + n), n) for a, o, n in zip(domain, offsets, sizes)))


def ring_partner(s, at):
    x, y, z = at
    dx, dh, dc = s % 4, s // 4 % 2, s // 8
    high = lax.rem(y // 4 + dh, 2)
    core = lax.rem(lax.rem(z, 2) + dc, 2)
    return (lax.rem(x + dx, 4), high * 4 + lax.rem(y, 4), z // 2 * 2 + core)


def plane_partner(s, at):
    x, y, z = at
    dy, dz = s % 4, s // 4
    return (x, y // 4 * 4 + lax.rem(lax.rem(y, 4) + dy, 4), lax.rem(z // 2 + dz, 4) * 2 + lax.rem(z, 2))


INPUTS = (
    ("pos", (3, 1, ATOMS), F32),
    ("spec", (1, ATOMS), jnp.int32),
    ("uni", (1, UNION), jnp.int32),
    ("gmap", (GHOST, BLOCKS), jnp.int32),
    ("recv", (1, EDGES), jnp.int32),
    ("send", (1, EDGES), jnp.int32),
    ("emb", (6, C), F32),
    ("sen", (1, 6), F32),
    ("rin", (2, 8, RH), F32),
    ("rout", (2, RH, 3 * C), F32),
    ("mix", (2, 3, C, C), F32),
    ("prod", (2, 3 * C, C), F32),
    ("res", (2, C, C), F32),
    ("ro", (1, C), F32),
    ("rhid", (GHOST, C), F32),
    ("rt", (1, GHOST), F32),
)
DOMAIN = 6
ALL = 9 * ATOMS
TILE = (8, 128)
SCRATCH = (
    ("cnt_out", (1, 128), jnp.int32),
    ("cnt", (1, 128), jnp.int32),
    ("done_out", TILE, F32),
    ("done", TILE, F32),
    ("msg0", (4,) + TILE, F32),
    ("u_buf", (BLOCKS,) + TILE, F32),
    ("snd1", (32, GHOST, C), F32),
    ("rcv1", (BLOCKS, GHOST, C), F32),
    ("snd2", (BLOCKS, GHOST, C), F32),
    ("rcv2", (32, GHOST, C), F32),
    ("snd3", (4,) + TILE, F32),
    ("rcv3", (BLOCKS,) + TILE, F32),
    ("red_a", (15,) + TILE, F32),
    ("red_b", (15,) + TILE, F32),
    ("part_a", (1,) + TILE, F32),
    ("part_b", (1,) + TILE, F32),
    ("pst", (TABLE, EDGES), BF16),
    ("ps", (EDGES, TABLE), BF16),
    ("prt", (ATOMS, EDGES), BF16),
    ("pr2", (EDGES, 2 * ATOMS), BF16),
    ("ybc", (8, EDGES, 128), F32),
    ("bsel", (BLOCKS * 128, 128), BF16),
    ("selt", (ATOMS, 512), BF16),
    ("sel", (512, ATOMS), BF16),
    ("tile_i", TILE, jnp.int32),
    ("tile_f", (128, 128), F32),
    ("win", (48, 512), BF16),
    ("winT", (256, 128), BF16),
    ("wo4", (2, 256, 384), BF16),
    ("woT", (2, 768, 256), BF16),
    ("mix4", (2, 3, 256, 256), BF16),
    ("mixT", (2, 3, 256, 256), BF16),
    ("pr4", (2, 512, 256), BF16),
    ("prT", (2, 256, 768), BF16),
    ("resT", (256, 256), BF16),
    ("ybuf", (8, EDGES), F32),
    ("xyz", (8, EDGES), F32),
    ("kind", (16, EDGES), F32),
    ("hcat", (2, EDGES, 256), BF16),
    ("dsil", (EDGES, 128), F32),
    ("pre1", (EDGES, 128), F32),
    ("rbuf", (2, EDGES, 384), F32),
    ("hsbuf", (2, EDGES, 128), F32),
    ("dap", (256, ALL), BF16),
    ("grads", (EDGES, 384), F32),
    ("dhp", (EDGES, 256), BF16),
    ("dhid", (EDGES, 128), F32),
    ("dyc", (EDGES, 128), F32),
    ("mixed", (2, ALL, 128), F32),
    ("table", (TABLE - ATOMS, 256), BF16),
    ("hloc", (ATOMS, 128), F32),
    ("dvb", TILE[:1] + (EDGES,), F32),
)


def body(sizes, cnt_ref, *refs):
    names = [name for name, _, _ in INPUTS]
    hbm = dict(zip(names, refs))
    forces_ref, energy_ref, virial_ref = refs[len(names) : len(names) + 3]
    rest = refs[len(names) + 3 :]
    vm = dict(zip(names, rest))
    rest = rest[len(names) :]
    v = dict(zip([name for name, _, _ in SCRATCH], rest))
    send_sem, recv_sem, load_sem, move_sem, land_sem = rest[len(SCRATCH) :]

    at = (lax.axis_index("gx"), lax.axis_index("gy"), lax.axis_index("gz"))
    near = [k for k in range(BLOCKS) if k != SELF]
    near = [near[7 * n % 26] for n in range(26)]
    others = list(range(1, 16))
    home = swapped(at)
    settled = home[0] == at[0]
    ids = {k: neighbour(k, home, sizes) for k in near}
    ring = {s: ring_partner(s, at) for s in others}
    plane = {s: plane_partner(s, at) for s in others}

    u_buf, rcv1, rcv2, rcv3 = v["u_buf"], v["rcv1"], v["rcv2"], v["rcv3"]
    tile_i, tile_f = v["tile_i"], v["tile_f"]

    u_buf[SELF] = jnp.zeros((8, 128), F32)
    rcv1[SELF] = jnp.zeros((GHOST, C), F32)
    for b in (13, 27, 28, 29, 30, 31):
        rcv2[b] = jnp.zeros((GHOST, C), F32)
    rcv3[...] = jnp.zeros((BLOCKS, 8, 128), F32)
    v["red_a"][...] = jnp.zeros((15, 8, 128), F32)
    v["done_out"][...] = jnp.zeros((8, 128), F32)
    v["red_b"][...] = jnp.zeros((15, 8, 128), F32)

    loads = [
        pltpu.make_async_copy(hbm[name], vm[name], load_sem.at[n])
        for n, name in enumerate(names)
        if n >= DOMAIN
    ]
    barrier = pltpu.get_barrier_semaphore()
    for target in list(ids.values()) + list(ring.values()) + list(plane.values()):
        pl.semaphore_signal(barrier, inc=1, device_id=target, device_id_type=MESH)

    @pl.when(jnp.logical_not(settled))
    def _():
        pl.semaphore_signal(barrier, inc=1, device_id=home, device_id_type=MESH)

    for load in loads:
        load.start()
    v["cnt_out"][...] = jnp.full((1, 128), 0, jnp.int32) + cnt_ref[0]

    def exchange(pairs, first):
        far = [
            pltpu.make_async_remote_copy(
                src_ref=src,
                dst_ref=dst,
                send_sem=move_sem.at[first + n],
                recv_sem=land_sem.at[first + n],
                device_id=home,
                device_id_type=MESH,
            )
            for n, (src, dst) in enumerate(pairs)
        ]
        close = [
            pltpu.make_async_copy(src, dst, land_sem.at[first + n])
            for n, (src, dst) in enumerate(pairs)
        ]

        @pl.when(settled)
        def _():
            for copy in close:
                copy.start()

        @pl.when(jnp.logical_not(settled))
        def _():
            for copy in far:
                copy.start()

        def landed():
            for copy in close:
                copy.wait()

        def left():
            @pl.when(jnp.logical_not(settled))
            def _():
                for copy in far:
                    copy.wait_send()

        return landed, left

    def ship(src, dst, phase, target):
        pltpu.make_async_remote_copy(
            src_ref=src,
            dst_ref=dst,
            send_sem=send_sem.at[phase],
            recv_sem=recv_sem.at[phase],
            device_id=target,
            device_id_type=MESH,
        ).start()

    def await_bytes(ref, sem, count, rows=None):
        view = ref.at[pl.ds(0, count)] if rows is None else ref.at[pl.ds(0, count), pl.ds(0, rows)]
        pltpu.make_async_copy(view, view, sem).wait()

    lane = iota((1, 128), 1)
    lane_group = lane >> 4
    row8 = iota((8, 128), 0)
    greeted = len(near) + 2 * len(others)

    @pl.when(settled)
    def _():
        pl.semaphore_wait(barrier, greeted)

    @pl.when(jnp.logical_not(settled))
    def _():
        pl.semaphore_wait(barrier, greeted + 1)

    domain_here, domain_left = exchange(
        [(hbm[name], vm[name]) for name in names[:DOMAIN]] + [(v["cnt_out"], v["cnt"])], 0
    )
    for load in loads:
        load.wait()
    tile_f[...] = jnp.zeros((128, 128), F32)
    for t in range(2):
        tile_f[0:8, RH * t : RH * (t + 1)] = vm["rin"][t]
        tile_f[8 * t + 8 : 8 * t + 16, 0:RH] = vm["rin"][t]
        tile_f[8 * t + 8 : 8 * t + 16, RH : 2 * RH] = vm["rin"][t]
    tile_f[32:38, :] = vm["emb"][...]
    rin_both = tile_f[0:8, :]
    rin_hi = rin_both.astype(BF16).astype(F32)
    rin_lo = (rin_both - rin_hi).astype(BF16).astype(F32)
    emb_pair = beside(tile_f[32:48, :])
    for t in range(2):
        twice = tile_f[8 * t + 8 : 8 * t + 16, :]
        twice_hi = twice.astype(BF16).astype(F32)
        twice_lo = (twice - twice_hi).astype(BF16).astype(F32)
        v["win"][:, 128 * t : 128 * (t + 1)] = jnp.concatenate(
            [twice_hi, twice_lo, twice_hi, twice_lo, jnp.zeros((16, 128), F32)], axis=0
        ).astype(BF16)
    v["win"][:, 256:512] = jnp.concatenate([jnp.zeros((32, 256), BF16), emb_pair], axis=0)
    turned = flipped(
        jnp.concatenate([rin_hi, rin_lo, jnp.zeros((112, 128), F32)], axis=0)
    ).astype(BF16)
    v["winT"][...] = both(turned)
    for t in range(2):
        w = vm["rout"][t]
        w_hi, w_lo = split(w)
        v["wo4"][t] = jnp.concatenate([w_hi, w_lo, w_hi, w_lo], axis=0)
        tile_f[...] = jnp.zeros((128, 128), F32)
        for l in range(3):
            tile_f[RH * t : RH * (t + 1), :] = w[:, 128 * l : 128 * (l + 1)]
            turned = beside(flipped(tile_f[...]))
            v["woT"][t, 128 * l : 128 * (l + 1), :] = turned
            v["woT"][t, 384 + 128 * l : 384 + 128 * (l + 1), :] = turned
            v["mix4"][t, l] = both(beside(vm["mix"][t, l]))
            v["mixT"][t, l] = both(beside(flipped(vm["mix"][t, l])))
            block = slice(128 * l, 128 * (l + 1))
            v["pr4"][t, block, :] = beside(vm["prod"][t, block, :])
            p_hi, p_lo = split(flipped(vm["prod"][t, block, :]))
            v["prT"][t, :, block] = both(p_hi)
            v["prT"][t, :, 384 + 128 * l : 384 + 128 * (l + 1)] = both(p_lo)
        v["pr4"][t, 384:512, :] = beside(vm["res"][t])
    v["resT"][...] = both(beside(flipped(vm["res"][1])))
    rhT = vm["rhid"][...]
    tile_f[...] = jnp.zeros((128, 128), F32)
    tile_f[0:16, :] = rhT
    rh = flipped(tile_f[...])[:, 0:16]
    rt_row = vm["rt"][...]
    tile_f[0:16, :] = jnp.zeros((16, 128), F32)
    tile_f[0:1, 0:6] = vm["sen"][...]
    sen_col = flipped(tile_f[...])[0:16, 0:1]
    domain_here()
    count = v["cnt"][...]
    tile_i[...] = jnp.full((8, 128), -1, jnp.int32)
    tile_i[0:1, 0:UNION] = vm["uni"][...]
    union_row = tile_i[0:1, :]
    union_t = onehot(iota((ATOMS, 128), 0) == union_row)
    species = vm["spec"][...]
    pos = vm["pos"]
    geometry = jnp.concatenate(
        [pos[0], pos[1], pos[2], species.astype(F32), jnp.zeros((4, ATOMS), F32)], axis=0
    )
    offered = three(mm(pieces(geometry), union_t))
    tile_f[...] = jnp.zeros((128, 128), F32)
    tile_f[0:GHOST, 0:BLOCKS] = vm["gmap"][...].astype(F32)
    turned_map = flipped(tile_f[...])[0:32, :]
    tiling = onehot(iota((128, 128), 0) == (iota((128, 128), 1) & 15))
    tiled = mm(turned_map.astype(BF16), tiling)
    tiled = jnp.where((iota((32, 128), 1) >> 4) == (iota((32, 128), 0) & 7), tiled, 0.0)
    own_lists = [jnp.sum(tiled[8 * g : 8 * g + 8], axis=0, keepdims=True) for g in range(4)]
    for g in range(4):
        v["msg0"][g] = jnp.where(row8 == 4, own_lists[g], offered)

    for k in near:
        ship(v["msg0"].at[k // 8], u_buf.at[26 - k], 0, ids[k])

    lanes_all = iota((1, EDGES), 1)

    def edge_tables(k, carry):
        lanes = pl.ds(pl.multiple_of(k * 128, 128), 128)
        rows = pl.ds(pl.multiple_of(k * 128, 128), 128)
        to = vm["send"][:, lanes]
        by = vm["recv"][:, lanes]
        alive = iota((1, 128), 1) + k * 128 < DEG * count
        by = jnp.where(alive, by, -1)
        v["pst"][:, lanes] = onehot(iota((TABLE, 128), 0) == to)
        v["prt"][:, lanes] = onehot(iota((ATOMS, 128), 0) == by)
        to_col = flipped(jnp.broadcast_to(to.astype(F32), (128, 128))).astype(jnp.int32)
        by_col = flipped(jnp.broadcast_to(by.astype(F32), (128, 128))).astype(jnp.int32)
        column = iota((128, 128), 1)
        for b in range(4):
            v["ps"][rows, 128 * b : 128 * (b + 1)] = onehot(column + 128 * b == to_col)
        last = TABLE - 512
        v["ps"][rows, 512:TABLE] = onehot(column[:, 0:last] + 512 == to_col[:, 0:last])
        mine = onehot(column == by_col)
        v["pr2"][rows, :] = jnp.concatenate([mine, mine], axis=1)
        return carry

    lax.fori_loop(0, EDGES // 128, edge_tables, 0)
    for g, (first, size) in enumerate(GROUPS):
        target = jnp.where(
            lane_group < size, lane_group * 128 + own_lists[g].astype(jnp.int32), -1
        )
        v["bsel"][128 * first : 128 * (first + size), :] = onehot(
            iota((size * 128, 128), 0) == target
        )

    hot = jnp.where(iota((16, ATOMS), 0) == species, 1.0, 0.0)
    base_energy = jnp.sum(hot * sen_col, axis=0, keepdims=True)
    hot_rows = flipped(jnp.concatenate([hot, jnp.zeros((112, ATOMS), F32)], axis=0))
    v["hloc"][...] = halves(mm(hot_rows[:, 0:16].astype(BF16), emb_pair))
    live = jnp.where(lane < count, 1.0, 0.0)
    live_col = jnp.where(iota((ATOMS, C), 0) < count, 1.0, 0.0)

    await_bytes(u_buf, recv_sem.at[0], len(near))
    tables = [geometry]
    for g, (first, size) in enumerate(GROUPS):
        u_cat = jnp.concatenate([u_buf[first + j] for j in range(size)], axis=1)
        ghost = three(mm(pieces(u_cat), v["bsel"][128 * first : 128 * (first + size), :]))
        block = first + lane_group
        ninth = jnp.where(block >= 9, 1, 0) + jnp.where(block >= 18, 1, 0)
        third = sum(jnp.where(block >= 3 * n, 1, 0) for n in range(1, 9))
        steps = (ninth, third - 3 * ninth, block - 3 * third)
        shift = jnp.zeros((8, 128), F32)
        for axis, step in enumerate(steps):
            shift = jnp.where(row8 == axis, (step - 1).astype(F32) * DOMAIN_SIDE, shift)
        ghost = ghost + shift
        tables.append(ghost[:, 0 : size * GHOST])
    coord24 = pieces(jnp.concatenate(tables, axis=1))
    from_sender = three(mm(coord24, v["pst"][...]))
    at_receiver = three(mm(coord24[:, 0:ATOMS], v["prt"][...]))
    apart = from_sender - at_receiver
    v["xyz"][...] = apart
    kind = jnp.where(
        iota((16, EDGES), 0) == from_sender[3:4, :].astype(jnp.int32), 1.0, 0.0
    )

    dx, dy, dz = apart[0:1, :], apart[1:2, :], apart[2:3, :]
    length = jnp.sqrt(dx * dx + dy * dy + dz * dz + SOFTENING)
    inv = 1.0 / length
    ua, ub, uc = dx * inv, dy * inv, dz * inv
    harmonic = (
        R3 * ua,
        R3 * ub,
        R3 * uc,
        R15 * ua * ub,
        R15 * ub * uc,
        (0.5 * R5) * (3.0 * uc * uc - 1.0),
        R15 * ua * uc,
        (0.5 * R15) * (ua * ua - ub * ub),
    )
    for m in range(8):
        v["ybuf"][m : m + 1, :] = harmonic[m]
    orders = (iota((8, EDGES), 0) + 1).astype(F32) * STEP
    sines, cosines = sin_cos(orders * length)
    basis = BASIS_SCALE * sines * inv
    slope = (BASIS_SCALE * orders * cosines - basis) * inv
    b_hi, b_lo = split(basis)
    b_hi, b_lo = b_hi.astype(F32), b_lo.astype(F32)
    v_rows = jnp.concatenate([b_hi, b_hi, b_lo, b_lo, kind], axis=0)
    for j in range(EDGES // 128):
        span = slice(128 * j, 128 * (j + 1))
        block = jnp.concatenate([v_rows[:, span], jnp.zeros((80, 128), F32)], axis=0)
        turned = flipped(block)[:, 0:48].astype(BF16)
        out = mm(turned, v["win"][...])
        v["hsbuf"][0, span, :] = halves(out[:, 256:512])
        v["pre1"][span, :] = out[:, 128:256]
        sig, hidden = activate(out[:, 0:128])
        v["dsil"][span, :] = sig + hidden * (1.0 - sig)
        v["hcat"][0, span, :] = beside(hidden)
        for m in range(8):
            v["ybc"][m, span, :] = flipped(
                jnp.broadcast_to(v["ybuf"][m : m + 1, span], (128, 128))
            )

    def rows_of(k):
        if isinstance(k, int):
            return pl.ds(k * CHUNK, CHUNK)
        return pl.ds(pl.multiple_of(k * CHUNK, CHUNK), CHUNK)

    spans = ((0, 1), (1, 4), (4, 9))

    def hidden_second():
        low = iota((CHUNK, 128), 1) < RH

        def step(k, carry):
            rows = rows_of(k)
            sig, hidden = activate(v["pre1"][rows, :])
            v["dsil"][rows, :] = jnp.where(
                low, v["dsil"][rows, :], sig + hidden * (1.0 - sig)
            )
            v["hcat"][1, rows, :] = beside(hidden)
            return carry

        lax.fori_loop(0, CHUNKS, step, 0, unroll=True)

    def radial_of(t):
        def step(k, carry):
            v["rbuf"][t, rows_of(k), :] = mm(v["hcat"][t, rows_of(k), :], v["wo4"][t])
            return carry

        lax.fori_loop(0, CHUNKS, step, 0, unroll=True)

    def update(t, h_local):
        hs = v["hsbuf"][t]
        for l, (lo, hi) in enumerate(spans):
            rows = slice(128 * lo, 128 * hi)
            weighted = v["rbuf"][t, :, 128 * l : 128 * (l + 1)] * hs
            sums = []
            for m in range(lo, hi):
                message = weighted
                if m:
                    message = weighted * v["ybc"][m - 1]
                sums.append(halves(mm(v["prt"][...], beside(message))))
            agg = (sums[0] if l == 0 else jnp.concatenate(sums, axis=0)) * SPREAD
            v["mixed"][t, rows, :] = halves(mm(beside(agg), v["mix4"][t, l]))

        def square(lo, hi):
            total = None
            for m in range(lo, hi):
                x = v["mixed"][t, 128 * m : 128 * (m + 1), :]
                total = x * x if total is None else total + x * x
            return total

        invariants = jnp.concatenate(
            [v["mixed"][t, 0:128, :], square(1, 4), square(4, 9), h_local], axis=1
        )
        x_hi, x_lo = split(invariants)
        out = mm(jnp.concatenate([x_hi, x_lo], axis=0), v["pr4"][t])
        out = out[0:128] + out[128:256]
        return halves(out)

    def back_update(t, dh):
        dinv = halves(mm(beside(dh), v["prT"][t]))
        for l, (lo, hi) in enumerate(spans):
            grad = dinv[:, 128 * l : 128 * (l + 1)]
            if l == 0:
                parts = grad
            else:
                parts = jnp.concatenate(
                    [
                        2.0 * v["mixed"][t, 128 * m : 128 * (m + 1), :] * grad
                        for m in range(lo, hi)
                    ],
                    axis=0,
                )
            out = halves(mm(beside(parts), v["mixT"][t, l])) * SPREAD
            for m in range(lo, hi):
                v["dap"][:, 128 * m : 128 * (m + 1)] = jnp.concatenate(
                    split(out[128 * (m - lo) : 128 * (m - lo + 1)]), axis=0
                )

    def back_edges(t, rows, grads, angles):
        hit = v["pr2"][rows, :]
        lanes = iota((CHUNK, 128), 1)
        turned = v["dyc"][rows, :] if angles else None
        hs = v["hsbuf"][t, rows, :] if angles else None
        pulled = {}
        for m in (0, 1, 3, 5, 7):
            if m:
                pair = mm(hit, v["dap"][:, 128 * m : 128 * (m + 2)])
                pulled[m], pulled[m + 1] = pair[:, 0:128], pair[:, 128:256]
            elif grads:
                pulled[0] = mm(hit, v["dap"][:, 0:128])
        out = []
        for l, (lo, hi) in enumerate(spans):
            weighted = v["rbuf"][t, rows, 128 * l : 128 * (l + 1)] * hs if angles else None
            total = None
            for m in range(lo, hi):
                if not grads and not m:
                    continue
                d_m = pulled[m]
                if m and angles:
                    along = jnp.sum(d_m * weighted, axis=1, keepdims=True)
                    turned = jnp.where(lanes == m - 1, turned + along, turned)
                if grads:
                    term = d_m * v["ybc"][m - 1, rows, :] if m else d_m
                    total = term if total is None else total + term
            out.append(total)
        if angles:
            v["dyc"][rows, :] = turned
        return out

    def back_radial(t, rows, grads):
        hs = v["hsbuf"][t, rows, :]
        parts = [split(grad * hs) for grad in grads]
        dr = jnp.concatenate([p[0] for p in parts] + [p[1] for p in parts], axis=1)
        out = halves(mm(dr, v["woT"][t]))
        if t == 1:
            v["dhid"][rows, :] = out
        else:
            v["dhid"][rows, :] += out

    radial_of(0)
    h1 = update(0, v["hloc"][...])
    for g, (first, size) in enumerate(GROUPS):
        wanted = jnp.full((1, 128), -1.0, F32)
        for j in range(size):
            wanted = jnp.where(lane_group == place(j), u_buf[first + j][4:5, :], wanted)
        lists = onehot(iota((128, 128), 0) == wanted.astype(jnp.int32))
        chosen = mm(union_t, lists)
        v["selt"][:, 128 * g : 128 * (g + 1)] = chosen.astype(BF16)
        v["sel"][128 * g : 128 * (g + 1), :] = flipped(chosen).astype(BF16)
    h1_pair = beside(h1)
    v["snd1"][...] = halves(mm(v["sel"][...], h1_pair)).reshape(32, GHOST, C)
    for k in near:
        ship(v["snd1"].at[row_block(k)], rcv1.at[26 - k], 1, ids[k])
    v["hloc"][...] = h1
    hidden_second()
    radial_of(1)
    ro_rows = jnp.broadcast_to(vm["ro"][...], (8, C))
    energy_one = exact(ro_rows, h1, ((1,), (1,)))[0:1]

    def gather_local(k, carry):
        v["hsbuf"][1, rows_of(k), :] = halves(mm(v["ps"][rows_of(k), 0:ATOMS], h1_pair))
        return carry

    lax.fori_loop(0, CHUNKS, gather_local, 0, unroll=True)
    await_bytes(rcv1, recv_sem.at[1], len(near))
    v["table"][...] = beside(rcv1[...].reshape(BLOCKS * GHOST, C))

    def gather_second(k, carry):
        v["hsbuf"][1, rows_of(k), :] += halves(
            mm(v["ps"][rows_of(k), ATOMS:TABLE], v["table"][...])
        )
        return carry

    lax.fori_loop(0, CHUNKS, gather_second, 0, unroll=True)
    h2 = update(1, v["hloc"][...])
    pre_read = exact(h2, rh)
    sig_read = 1.0 / (1.0 + jnp.exp(-pre_read))
    hid_read = pre_read * sig_read
    dread = rt_row * live_col[:, 0:16] * (sig_read + hid_read * (1.0 - sig_read))
    dh2 = exact(dread, rhT)

    back_update(1, dh2)

    def features_second(k, carry):
        rows = rows_of(k)
        grads = back_edges(1, rows, True, False)
        total = None
        for l in range(3):
            v["grads"][rows, 128 * l : 128 * (l + 1)] = grads[l]
            term = v["rbuf"][1, rows, 128 * l : 128 * (l + 1)] * grads[l]
            total = term if total is None else total + term
        v["dhp"][rows, :] = beside(total)
        return carry

    lax.fori_loop(0, CHUNKS, features_second, 0, unroll=True)
    hgrad = halves(mm(v["pst"][ATOMS:TABLE, :], v["dhp"][...]))
    v["snd2"][...] = hgrad.reshape(BLOCKS, GHOST, C)
    for k in near:
        ship(v["snd2"].at[k], rcv2.at[row_block(26 - k)], 2, ids[k])
    own = (
        halves(mm(v["pst"][0:ATOMS, :], v["dhp"][...]))
        + live_col * jnp.broadcast_to(vm["ro"][...], (ATOMS, C))
        + halves(mm(beside(dh2), v["resT"][...]))
    )
    rt_rows = jnp.broadcast_to(rt_row, (8, GHOST))
    energy_two = exact(rt_rows, hid_read, ((1,), (1,)))[0:1]
    energy = (base_energy + energy_one + energy_two) * live
    v["dyc"][...] = jnp.zeros((EDGES, 128), F32)

    def angles_second(k, carry):
        rows = rows_of(k)
        back_edges(1, rows, False, True)
        back_radial(1, rows, [v["grads"][rows, 128 * l : 128 * (l + 1)] for l in range(3)])
        return carry

    lax.fori_loop(0, CHUNKS, angles_second, 0, unroll=True)
    await_bytes(rcv2, recv_sem.at[2], len(near))
    dh1 = own + halves(mm(v["selt"][...], beside(rcv2[...].reshape(512, C))))

    back_update(0, dh1)

    def edges_first(k, carry):
        rows = rows_of(k)
        back_radial(0, rows, back_edges(0, rows, True, True))
        return carry

    lax.fori_loop(0, CHUNKS, edges_first, 0, unroll=True)

    dbas, dys = [], []
    for j in range(EDGES // 128):
        span = slice(128 * j, 128 * (j + 1))
        dpre = v["dhid"][span, :] * v["dsil"][span, :]
        dbas.append(flipped(mm(beside(dpre), v["winT"][...]))[0:16])
        dys.append(flipped(v["dyc"][span, :])[0:8])
    g = jnp.concatenate(dys, axis=1)
    dbas = jnp.concatenate(dbas, axis=1)
    dbas = dbas[0:8] + dbas[8:16]
    dlen = jnp.sum(dbas * slope, axis=0, keepdims=True)
    g1, g2, g3, g4, g5, g6, g7, g8 = [g[m : m + 1, :] for m in range(8)]
    da = R3 * g1 + R15 * (ub * g4 + uc * g7 + ua * g8)
    db = R3 * g2 + R15 * (ua * g4 + uc * g5 - ub * g8)
    dc = R3 * g3 + R15 * (ub * g5 + ua * g7) + (3.0 * R5) * uc * g6
    along = dlen - (da * ua + db * ub + dc * uc) * inv
    dvb = v["dvb"]
    dvb[...] = jnp.zeros((8, EDGES), F32)
    dvb[0:1, :] = da * inv + ua * along
    dvb[1:2, :] = db * inv + ub * along
    dvb[2:3, :] = dc * inv + uc * along
    dvec = dvb[...]
    v_hi = dvec.astype(BF16).astype(F32)
    dv_pair = jnp.concatenate([v_hi, dvec - v_hi], axis=0).astype(BF16)
    strain = exact(dvec, v["xyz"][...], ((1,), (1,)))
    tile_f[0:8, :] = jnp.zeros((8, 128), F32)
    tile_f[0:8, 0:8] = strain
    tile_f[3:4, 0:1] = count[:, 0:1].astype(F32)
    own_part = tile_f[0:8, :]
    red_a, red_b, part_a, part_b = v["red_a"], v["red_b"], v["part_a"], v["part_b"]
    part_a[0] = own_part
    for s in others:
        ship(part_a.at[0, pl.ds(0, 4)], red_a.at[s - 1, pl.ds(0, 4)], 4, ring[s])
    cgrad = mm(dv_pair, v["ps"][...])
    cgrad = cgrad[0:8] + cgrad[8:16]
    for g, (first, size) in enumerate(GROUPS):
        tile = cgrad[:, ATOMS + 16 * first : ATOMS + 16 * (first + size)]
        if size < 8:
            tile = jnp.concatenate([tile, jnp.zeros((8, 128 - 16 * size), F32)], axis=1)
        v["snd3"][g] = tile
    for k in near:
        ship(v["snd3"].at[k // 8, pl.ds(0, 3)], rcv3.at[26 - k, pl.ds(0, 3)], 3, ids[k])
    rgrad = mm(dv_pair, v["pr2"][:, 0:ATOMS])
    rgrad = rgrad[0:8] + rgrad[8:16]
    await_bytes(red_a, recv_sem.at[4], 15, 4)
    total = own_part + jnp.sum(red_a[...], axis=0)
    part_b[0] = total
    for s in others:
        ship(part_b.at[0, pl.ds(0, 4)], red_b.at[s - 1, pl.ds(0, 4)], 5, plane[s])

    await_bytes(rcv3, recv_sem.at[3], len(near), 3)
    back = jnp.zeros((8, ATOMS), F32)
    for g, (first, size) in enumerate(GROUPS):
        tile = jnp.zeros((8, 128), F32)
        for j in range(size):
            tile = jnp.where(lane_group == place(j), rcv3[first + j], tile)
        t_hi = tile.astype(BF16).astype(F32)
        pair = jnp.concatenate([t_hi, tile - t_hi], axis=0).astype(BF16)
        got = mm(pair, v["sel"][128 * g : 128 * (g + 1), :])
        back = back + got[0:8] + got[8:16]
    forces = rgrad - cgrad[:, 0:ATOMS] - back
    v["done_out"][0:3, :] = forces[0:3]
    v["done_out"][3:4, :] = energy
    result_here, result_left = exchange([(v["done_out"], v["done"])], DOMAIN + 1)

    await_bytes(red_b, recv_sem.at[5], 15, 4)
    total = total + jnp.sum(red_b[...], axis=0)
    virial_ref[...] = -total[0:3, 0:3] / total[3:4, 0:1]
    result_here()
    for axis in range(3):
        forces_ref[axis] = v["done"][axis : axis + 1, :]
    energy_ref[...] = v["done"][3:4, :]
    domain_left()
    result_left()

    await_bytes(u_buf, send_sem.at[0], len(near))
    await_bytes(rcv1, send_sem.at[1], len(near))
    await_bytes(rcv2, send_sem.at[2], len(near))
    await_bytes(rcv3, send_sem.at[3], len(near), 3)
    await_bytes(red_a, send_sem.at[4], 15, 4)
    await_bytes(red_b, send_sem.at[5], 15, 4)


def solution(mesh):
    sizes = tuple(mesh.shape[name] for name in ("gx", "gy", "gz"))

    def shards(
        positions,
        species,
        atom_count,
        export_union,
        ghost_map,
        edge_receiver,
        edge_sender,
        embed,
        species_energy,
        radial_in,
        radial_out,
        mixing,
        product,
        residual,
        read_one,
        read_hidden,
        read_two,
    ):
        vmem = pl.BlockSpec(memory_space=pltpu.VMEM)
        scratch = [pltpu.VMEM(shape, kind) for _, shape, kind in INPUTS + SCRATCH]
        scratch += [
            pltpu.SemaphoreType.DMA((6,)),
            pltpu.SemaphoreType.DMA((6,)),
            pltpu.SemaphoreType.DMA((len(INPUTS),)),
            pltpu.SemaphoreType.DMA((DOMAIN + 2,)),
            pltpu.SemaphoreType.DMA((DOMAIN + 2,)),
        ]
        forces, energy, virial = pl.pallas_call(
            functools.partial(body, sizes),
            out_shape=(
                jax.ShapeDtypeStruct((3, 1, ATOMS), F32),
                jax.ShapeDtypeStruct((1, ATOMS), F32),
                jax.ShapeDtypeStruct((3, 3), F32),
            ),
            in_specs=[pl.BlockSpec(memory_space=pltpu.SMEM)]
            + [pl.BlockSpec(memory_space=pl.ANY)] * len(INPUTS),
            out_specs=(vmem, vmem, vmem),
            scratch_shapes=scratch,
            compiler_params=pltpu.CompilerParams(
                collective_id=0, has_side_effects=True, vmem_limit_bytes=60 * 1024 * 1024
            ),
            name="potential",
        )(
            atom_count.reshape(1),
            positions.reshape(3, 1, ATOMS),
            species.reshape(1, ATOMS),
            export_union.reshape(1, UNION),
            ghost_map.reshape(BLOCKS, GHOST).T,
            edge_receiver.reshape(1, EDGES),
            edge_sender.reshape(1, EDGES),
            embed,
            species_energy.reshape(1, -1),
            radial_in,
            radial_out,
            mixing,
            product,
            residual,
            read_one.reshape(1, C),
            read_hidden.T,
            read_two.reshape(1, -1),
        )
        return (
            forces.reshape(1, 1, 1, 3, ATOMS),
            energy.reshape(1, 1, 1, ATOMS),
            virial,
        )

    here = ("gx", "gy", "gz")
    in_specs = tuple(P(*here) for _ in range(7)) + tuple(P() for _ in range(10))
    out_specs = (P(*here), P(*here), P())
    return jax.shard_map(
        shards, mesh=mesh, in_specs=in_specs, out_specs=out_specs, check_vma=False
    )
```

```python
import functools

import jax
import jax.numpy as jnp
import numpy as np
from jax import lax
from jax.experimental import pallas as pl
from jax.experimental.pallas import tpu as pltpu
from jax.sharding import PartitionSpec as P

F32 = jnp.float32
BF16 = jnp.bfloat16
MESH = pl.DeviceIdType.MESH
HIGHEST = lax.Precision.HIGHEST

C = 128
ATOMS = 128
EDGES = 1024
CHUNK = 256
CHUNKS = EDGES // CHUNK
GHOST = 16
BLOCKS = 27
SELF = 13
TABLE = ATOMS + BLOCKS * GHOST
UNION = 64
RH = 64
DEG = 8
DOMAIN_SIDE = 5.0
SOFTENING = 0.25
STEP = float(np.pi / 18.0)
BASIS_SCALE = float((2.0 / 18.0) ** 0.5)
R3 = 3.0**0.5
R5 = 5.0**0.5
R15 = 15.0**0.5
DEGREE = (0, 1, 1, 1, 2, 2, 2, 2, 2)
SPREAD = float(DEG) ** (-0.5)
GROUPS = ((0, 8), (8, 8), (16, 8), (24, 3))


def place(j):
    return (2 - j) % 8


def row_block(k):
    return 8 * (k // 8) + place(k % 8)


def mm(a, b):
    return lax.dot_general(a, b, (((1,), (0,)), ((), ())), preferred_element_type=F32)


def exact(a, b, dims=((1,), (0,))):
    return lax.dot_general(a, b, (dims, ((), ())), precision=HIGHEST, preferred_element_type=F32)


def split(x):
    hi = x.astype(BF16)
    return hi, (x - hi.astype(F32)).astype(BF16)


def beside(x):
    return jnp.concatenate(split(x), axis=1)


def halves(y):
    n = y.shape[1] // 2
    return y[:, :n] + y[:, n:]


def both(x):
    return jnp.concatenate([x, x], axis=0)


def pieces(x):
    hi = x.astype(BF16).astype(F32)
    rest = x - hi
    mid = rest.astype(BF16).astype(F32)
    low = rest - mid
    return jnp.concatenate([hi, mid, low, jnp.zeros_like(x)], axis=0).astype(BF16)


def three(y):
    return y[0:8] + y[8:16] + y[16:24]


def activate(pre):
    sig = 1.0 / (1.0 + jnp.exp(-pre))
    return sig, pre * sig


def flipped(x):
    return jnp.transpose(x, (1, 0))


def onehot(cond):
    return jnp.where(cond, 1.0, 0.0).astype(BF16)


def iota(shape, dim):
    return lax.broadcasted_iota(jnp.int32, shape, dim)


def sin_cos(x):
    turns = jnp.floor(x * float(1.0 / np.pi) + 0.5)
    r = x - turns * 3.140625
    r = r - turns * 9.67502593994140625e-4
    r = r - turns * 1.509957990978376432e-7
    odd = turns - 2.0 * jnp.floor(turns * 0.5)
    sign = 1.0 - 2.0 * odd
    q = r * r
    s = 1.0 / 6227020800.0
    for c in (-1.0 / 39916800.0, 1.0 / 362880.0, -1.0 / 5040.0, 1.0 / 120.0, -1.0 / 6.0, 1.0):
        s = s * q + c
    c0 = -1.0 / 87178291200.0
    for c in (
        1.0 / 479001600.0,
        -1.0 / 3628800.0,
        1.0 / 40320.0,
        -1.0 / 720.0,
        1.0 / 24.0,
        -0.5,
        1.0,
    ):
        c0 = c0 * q + c
    return sign * (r * s), sign * c0


def swapped(at):
    x, y, z = at
    return (lax.rem(y, 4), y // 4 * 4 + x, z)


def neighbour(k, domain, sizes):
    offsets = (k // 9 - 1, k // 3 % 3 - 1, k % 3 - 1)
    return swapped(tuple(lax.rem(a + (o + n), n) for a, o, n in zip(domain, offsets, sizes)))


def ring_partner(s, at):
    x, y, z = at
    dx, dh, dc = s % 4, s // 4 % 2, s // 8
    high = lax.rem(y // 4 + dh, 2)
    core = lax.rem(lax.rem(z, 2) + dc, 2)
    return (lax.rem(x + dx, 4), high * 4 + lax.rem(y, 4), z // 2 * 2 + core)


def plane_partner(s, at):
    x, y, z = at
    dy, dz = s % 4, s // 4
    return (x, y // 4 * 4 + lax.rem(lax.rem(y, 4) + dy, 4), lax.rem(z // 2 + dz, 4) * 2 + lax.rem(z, 2))


INPUTS = (
    ("pos", (3, 1, ATOMS), F32),
    ("spec", (1, ATOMS), jnp.int32),
    ("uni", (1, UNION), jnp.int32),
    ("gmap", (GHOST, BLOCKS), jnp.int32),
    ("recv", (1, EDGES), jnp.int32),
    ("send", (1, EDGES), jnp.int32),
    ("emb", (6, C), F32),
    ("sen", (1, 6), F32),
    ("rin", (2, 8, RH), F32),
    ("rout", (2, RH, 3 * C), F32),
    ("mix", (2, 3, C, C), F32),
    ("prod", (2, 3 * C, C), F32),
    ("res", (2, C, C), F32),
    ("ro", (1, C), F32),
    ("rhid", (GHOST, C), F32),
    ("rt", (1, GHOST), F32),
)
DOMAIN = 6
ALL = 9 * ATOMS
TILE = (8, 128)
SCRATCH = (
    ("cnt_out", (1, 128), jnp.int32),
    ("cnt", (1, 128), jnp.int32),
    ("done_out", TILE, F32),
    ("done", TILE, F32),
    ("msg0", (4,) + TILE, F32),
    ("u_buf", (BLOCKS,) + TILE, F32),
    ("snd1", (32, GHOST, C), F32),
    ("rcv1", (BLOCKS, GHOST, C), F32),
    ("snd2", (BLOCKS, GHOST, C), F32),
    ("rcv2", (32, GHOST, C), F32),
    ("snd3", (4,) + TILE, F32),
    ("rcv3", (BLOCKS,) + TILE, F32),
    ("red_a", (15,) + TILE, F32),
    ("red_b", (15,) + TILE, F32),
    ("part_a", (1,) + TILE, F32),
    ("part_b", (1,) + TILE, F32),
    ("pst", (TABLE, EDGES), BF16),
    ("ps", (EDGES, TABLE), BF16),
    ("prt", (ATOMS, EDGES), BF16),
    ("pr2", (EDGES, 2 * ATOMS), BF16),
    ("ybc", (8, EDGES, 128), F32),
    ("bsel", (BLOCKS * 128, 128), BF16),
    ("selt", (ATOMS, 512), BF16),
    ("sel", (512, ATOMS), BF16),
    ("tile_i", TILE, jnp.int32),
    ("tile_f", (128, 128), F32),
    ("win", (48, 512), BF16),
    ("winT", (256, 128), BF16),
    ("wo4", (2, 256, 384), BF16),
    ("woT", (2, 768, 256), BF16),
    ("mix4", (2, 3, 256, 256), BF16),
    ("mixT", (2, 3, 256, 256), BF16),
    ("pr4", (2, 512, 256), BF16),
    ("prT", (2, 256, 768), BF16),
    ("resT", (256, 256), BF16),
    ("ybuf", (8, EDGES), F32),
    ("xyz", (8, EDGES), F32),
    ("kind", (16, EDGES), F32),
    ("hcat", (2, EDGES, 256), BF16),
    ("dsil", (EDGES, 128), F32),
    ("pre1", (EDGES, 128), F32),
    ("rbuf", (2, EDGES, 384), F32),
    ("hsbuf", (2, EDGES, 128), F32),
    ("dap", (256, ALL), BF16),
    ("grads", (EDGES, 384), F32),
    ("dhp", (EDGES, 256), BF16),
    ("dhid", (EDGES, 128), F32),
    ("dyc", (EDGES, 128), F32),
    ("mixed", (2, ALL, 128), F32),
    ("table", (TABLE - ATOMS, 256), BF16),
    ("hloc", (ATOMS, 128), F32),
    ("dvb", TILE[:1] + (EDGES,), F32),
)


def body(sizes, cnt_ref, *refs):
    names = [name for name, _, _ in INPUTS]
    hbm = dict(zip(names, refs))
    result_ref = refs[len(names)]
    rest = refs[len(names) + 1 :]
    vm = dict(zip(names, rest))
    rest = rest[len(names) :]
    v = dict(zip([name for name, _, _ in SCRATCH], rest))
    send_sem, recv_sem, load_sem, move_sem, land_sem = rest[len(SCRATCH) :]

    at = (lax.axis_index("gx"), lax.axis_index("gy"), lax.axis_index("gz"))
    near = [k for k in range(BLOCKS) if k != SELF]
    near = [near[7 * n % 26] for n in range(26)]
    others = list(range(1, 16))
    home = swapped(at)
    settled = home[0] == at[0]
    ids = {k: neighbour(k, home, sizes) for k in near}
    ring = {s: ring_partner(s, at) for s in others}
    plane = {s: plane_partner(s, at) for s in others}

    u_buf, rcv1, rcv2, rcv3 = v["u_buf"], v["rcv1"], v["rcv2"], v["rcv3"]
    tile_i, tile_f = v["tile_i"], v["tile_f"]

    u_buf[SELF] = jnp.zeros((8, 128), F32)
    rcv1[SELF] = jnp.zeros((GHOST, C), F32)
    for b in (13, 27, 28, 29, 30, 31):
        rcv2[b] = jnp.zeros((GHOST, C), F32)
    rcv3[...] = jnp.zeros((BLOCKS, 8, 128), F32)
    v["red_a"][...] = jnp.zeros((15, 8, 128), F32)
    v["done_out"][...] = jnp.zeros((8, 128), F32)
    v["red_b"][...] = jnp.zeros((15, 8, 128), F32)

    loads = [
        pltpu.make_async_copy(hbm[name], vm[name], load_sem.at[n])
        for n, name in enumerate(names)
        if n >= DOMAIN
    ]
    barrier = pltpu.get_barrier_semaphore()
    for target in list(ids.values()) + list(ring.values()) + list(plane.values()):
        pl.semaphore_signal(barrier, inc=1, device_id=target, device_id_type=MESH)

    @pl.when(jnp.logical_not(settled))
    def _():
        pl.semaphore_signal(barrier, inc=1, device_id=home, device_id_type=MESH)

    for load in loads:
        load.start()
    v["cnt_out"][...] = jnp.full((1, 128), 0, jnp.int32) + cnt_ref[0]

    def exchange(pairs, first):
        far = [
            pltpu.make_async_remote_copy(
                src_ref=src,
                dst_ref=dst,
                send_sem=move_sem.at[first + n],
                recv_sem=land_sem.at[first + n],
                device_id=home,
                device_id_type=MESH,
            )
            for n, (src, dst) in enumerate(pairs)
        ]
        close = [
            pltpu.make_async_copy(src, dst, land_sem.at[first + n])
            for n, (src, dst) in enumerate(pairs)
        ]

        @pl.when(settled)
        def _():
            for copy in close:
                copy.start()

        @pl.when(jnp.logical_not(settled))
        def _():
            for copy in far:
                copy.start()

        def landed():
            for copy in close:
                copy.wait()

        def left():
            @pl.when(jnp.logical_not(settled))
            def _():
                for copy in far:
                    copy.wait_send()

        return landed, left

    def ship(src, dst, phase, target):
        pltpu.make_async_remote_copy(
            src_ref=src,
            dst_ref=dst,
            send_sem=send_sem.at[phase],
            recv_sem=recv_sem.at[phase],
            device_id=target,
            device_id_type=MESH,
        ).start()

    def await_bytes(ref, sem, count, rows=None):
        view = ref.at[pl.ds(0, count)] if rows is None else ref.at[pl.ds(0, count), pl.ds(0, rows)]
        pltpu.make_async_copy(view, view, sem).wait()

    lane = iota((1, 128), 1)
    lane_group = lane >> 4
    row8 = iota((8, 128), 0)
    greeted = len(near) + 2 * len(others)

    @pl.when(settled)
    def _():
        pl.semaphore_wait(barrier, greeted)

    @pl.when(jnp.logical_not(settled))
    def _():
        pl.semaphore_wait(barrier, greeted + 1)

    domain_here, domain_left = exchange(
        [(hbm[name], vm[name]) for name in names[:DOMAIN]] + [(v["cnt_out"], v["cnt"])], 0
    )
    for load in loads:
        load.wait()
    tile_f[...] = jnp.zeros((128, 128), F32)
    for t in range(2):
        tile_f[0:8, RH * t : RH * (t + 1)] = vm["rin"][t]
        tile_f[8 * t + 8 : 8 * t + 16, 0:RH] = vm["rin"][t]
        tile_f[8 * t + 8 : 8 * t + 16, RH : 2 * RH] = vm["rin"][t]
    tile_f[32:38, :] = vm["emb"][...]
    rin_both = tile_f[0:8, :]
    rin_hi = rin_both.astype(BF16).astype(F32)
    rin_lo = (rin_both - rin_hi).astype(BF16).astype(F32)
    emb_pair = beside(tile_f[32:48, :])
    for t in range(2):
        twice = tile_f[8 * t + 8 : 8 * t + 16, :]
        twice_hi = twice.astype(BF16).astype(F32)
        twice_lo = (twice - twice_hi).astype(BF16).astype(F32)
        v["win"][:, 128 * t : 128 * (t + 1)] = jnp.concatenate(
            [twice_hi, twice_lo, twice_hi, twice_lo, jnp.zeros((16, 128), F32)], axis=0
        ).astype(BF16)
    v["win"][:, 256:512] = jnp.concatenate([jnp.zeros((32, 256), BF16), emb_pair], axis=0)
    turned = flipped(
        jnp.concatenate([rin_hi, rin_lo, jnp.zeros((112, 128), F32)], axis=0)
    ).astype(BF16)
    v["winT"][...] = both(turned)
    for t in range(2):
        w = vm["rout"][t]
        w_hi, w_lo = split(w)
        v["wo4"][t] = jnp.concatenate([w_hi, w_lo, w_hi, w_lo], axis=0)
        tile_f[...] = jnp.zeros((128, 128), F32)
        for l in range(3):
            tile_f[RH * t : RH * (t + 1), :] = w[:, 128 * l : 128 * (l + 1)]
            turned = beside(flipped(tile_f[...]))
            v["woT"][t, 128 * l : 128 * (l + 1), :] = turned
            v["woT"][t, 384 + 128 * l : 384 + 128 * (l + 1), :] = turned
            v["mix4"][t, l] = both(beside(vm["mix"][t, l]))
            v["mixT"][t, l] = both(beside(flipped(vm["mix"][t, l])))
            block = slice(128 * l, 128 * (l + 1))
            v["pr4"][t, block, :] = beside(vm["prod"][t, block, :])
            p_hi, p_lo = split(flipped(vm["prod"][t, block, :]))
            v["prT"][t, :, block] = both(p_hi)
            v["prT"][t, :, 384 + 128 * l : 384 + 128 * (l + 1)] = both(p_lo)
        v["pr4"][t, 384:512, :] = beside(vm["res"][t])
    v["resT"][...] = both(beside(flipped(vm["res"][1])))
    rhT = vm["rhid"][...]
    tile_f[...] = jnp.zeros((128, 128), F32)
    tile_f[0:16, :] = rhT
    rh = flipped(tile_f[...])[:, 0:16]
    rt_row = vm["rt"][...]
    tile_f[0:16, :] = jnp.zeros((16, 128), F32)
    tile_f[0:1, 0:6] = vm["sen"][...]
    sen_col = flipped(tile_f[...])[0:16, 0:1]
    domain_here()
    count = v["cnt"][...]
    tile_i[...] = jnp.full((8, 128), -1, jnp.int32)
    tile_i[0:1, 0:UNION] = vm["uni"][...]
    union_row = tile_i[0:1, :]
    union_t = onehot(iota((ATOMS, 128), 0) == union_row)
    species = vm["spec"][...]
    pos = vm["pos"]
    geometry = jnp.concatenate(
        [pos[0], pos[1], pos[2], species.astype(F32), jnp.zeros((4, ATOMS), F32)], axis=0
    )
    offered = three(mm(pieces(geometry), union_t))
    tile_f[...] = jnp.zeros((128, 128), F32)
    tile_f[0:GHOST, 0:BLOCKS] = vm["gmap"][...].astype(F32)
    turned_map = flipped(tile_f[...])[0:32, :]
    tiling = onehot(iota((128, 128), 0) == (iota((128, 128), 1) & 15))
    tiled = mm(turned_map.astype(BF16), tiling)
    tiled = jnp.where((iota((32, 128), 1) >> 4) == (iota((32, 128), 0) & 7), tiled, 0.0)
    own_lists = [jnp.sum(tiled[8 * g : 8 * g + 8], axis=0, keepdims=True) for g in range(4)]
    for g in range(4):
        v["msg0"][g] = jnp.where(row8 == 4, own_lists[g], offered)

    for k in near:
        ship(v["msg0"].at[k // 8], u_buf.at[26 - k], 0, ids[k])

    lanes_all = iota((1, EDGES), 1)

    def edge_tables(k, carry):
        lanes = pl.ds(pl.multiple_of(k * 128, 128), 128)
        rows = pl.ds(pl.multiple_of(k * 128, 128), 128)
        to = vm["send"][:, lanes]
        by = vm["recv"][:, lanes]
        alive = iota((1, 128), 1) + k * 128 < DEG * count
        by = jnp.where(alive, by, -1)
        v["pst"][:, lanes] = onehot(iota((TABLE, 128), 0) == to)
        v["prt"][:, lanes] = onehot(iota((ATOMS, 128), 0) == by)
        to_col = flipped(jnp.broadcast_to(to.astype(F32), (128, 128))).astype(jnp.int32)
        by_col = flipped(jnp.broadcast_to(by.astype(F32), (128, 128))).astype(jnp.int32)
        column = iota((128, 128), 1)
        for b in range(4):
            v["ps"][rows, 128 * b : 128 * (b + 1)] = onehot(column + 128 * b == to_col)
        last = TABLE - 512
        v["ps"][rows, 512:TABLE] = onehot(column[:, 0:last] + 512 == to_col[:, 0:last])
        mine = onehot(column == by_col)
        v["pr2"][rows, :] = jnp.concatenate([mine, mine], axis=1)
        return carry

    lax.fori_loop(0, EDGES // 128, edge_tables, 0)
    for g, (first, size) in enumerate(GROUPS):
        target = jnp.where(
            lane_group < size, lane_group * 128 + own_lists[g].astype(jnp.int32), -1
        )
        v["bsel"][128 * first : 128 * (first + size), :] = onehot(
            iota((size * 128, 128), 0) == target
        )

    hot = jnp.where(iota((16, ATOMS), 0) == species, 1.0, 0.0)
    base_energy = jnp.sum(hot * sen_col, axis=0, keepdims=True)
    hot_rows = flipped(jnp.concatenate([hot, jnp.zeros((112, ATOMS), F32)], axis=0))
    v["hloc"][...] = halves(mm(hot_rows[:, 0:16].astype(BF16), emb_pair))
    live = jnp.where(lane < count, 1.0, 0.0)
    live_col = jnp.where(iota((ATOMS, C), 0) < count, 1.0, 0.0)

    await_bytes(u_buf, recv_sem.at[0], len(near))
    tables = [geometry]
    for g, (first, size) in enumerate(GROUPS):
        u_cat = jnp.concatenate([u_buf[first + j] for j in range(size)], axis=1)
        ghost = three(mm(pieces(u_cat), v["bsel"][128 * first : 128 * (first + size), :]))
        block = first + lane_group
        ninth = jnp.where(block >= 9, 1, 0) + jnp.where(block >= 18, 1, 0)
        third = sum(jnp.where(block >= 3 * n, 1, 0) for n in range(1, 9))
        steps = (ninth, third - 3 * ninth, block - 3 * third)
        shift = jnp.zeros((8, 128), F32)
        for axis, step in enumerate(steps):
            shift = jnp.where(row8 == axis, (step - 1).astype(F32) * DOMAIN_SIDE, shift)
        ghost = ghost + shift
        tables.append(ghost[:, 0 : size * GHOST])
    coord24 = pieces(jnp.concatenate(tables, axis=1))
    from_sender = three(mm(coord24, v["pst"][...]))
    at_receiver = three(mm(coord24[:, 0:ATOMS], v["prt"][...]))
    apart = from_sender - at_receiver
    v["xyz"][...] = apart
    kind = jnp.where(
        iota((16, EDGES), 0) == from_sender[3:4, :].astype(jnp.int32), 1.0, 0.0
    )

    dx, dy, dz = apart[0:1, :], apart[1:2, :], apart[2:3, :]
    length = jnp.sqrt(dx * dx + dy * dy + dz * dz + SOFTENING)
    inv = 1.0 / length
    ua, ub, uc = dx * inv, dy * inv, dz * inv
    harmonic = (
        R3 * ua,
        R3 * ub,
        R3 * uc,
        R15 * ua * ub,
        R15 * ub * uc,
        (0.5 * R5) * (3.0 * uc * uc - 1.0),
        R15 * ua * uc,
        (0.5 * R15) * (ua * ua - ub * ub),
    )
    for m in range(8):
        v["ybuf"][m : m + 1, :] = harmonic[m]
    orders = (iota((8, EDGES), 0) + 1).astype(F32) * STEP
    sines, cosines = sin_cos(orders * length)
    basis = BASIS_SCALE * sines * inv
    slope = (BASIS_SCALE * orders * cosines - basis) * inv
    b_hi, b_lo = split(basis)
    b_hi, b_lo = b_hi.astype(F32), b_lo.astype(F32)
    v_rows = jnp.concatenate([b_hi, b_hi, b_lo, b_lo, kind], axis=0)
    for j in range(EDGES // 128):
        span = slice(128 * j, 128 * (j + 1))
        block = jnp.concatenate([v_rows[:, span], jnp.zeros((80, 128), F32)], axis=0)
        turned = flipped(block)[:, 0:48].astype(BF16)
        out = mm(turned, v["win"][...])
        v["hsbuf"][0, span, :] = halves(out[:, 256:512])
        v["pre1"][span, :] = out[:, 128:256]
        sig, hidden = activate(out[:, 0:128])
        v["dsil"][span, :] = sig + hidden * (1.0 - sig)
        v["hcat"][0, span, :] = beside(hidden)
        for m in range(8):
            v["ybc"][m, span, :] = flipped(
                jnp.broadcast_to(v["ybuf"][m : m + 1, span], (128, 128))
            )

    def rows_of(k):
        if isinstance(k, int):
            return pl.ds(k * CHUNK, CHUNK)
        return pl.ds(pl.multiple_of(k * CHUNK, CHUNK), CHUNK)

    spans = ((0, 1), (1, 4), (4, 9))

    def hidden_second():
        low = iota((CHUNK, 128), 1) < RH

        def step(k, carry):
            rows = rows_of(k)
            sig, hidden = activate(v["pre1"][rows, :])
            v["dsil"][rows, :] = jnp.where(
                low, v["dsil"][rows, :], sig + hidden * (1.0 - sig)
            )
            v["hcat"][1, rows, :] = beside(hidden)
            return carry

        lax.fori_loop(0, CHUNKS, step, 0, unroll=True)

    def radial_of(t):
        def step(k, carry):
            v["rbuf"][t, rows_of(k), :] = mm(v["hcat"][t, rows_of(k), :], v["wo4"][t])
            return carry

        lax.fori_loop(0, CHUNKS, step, 0, unroll=True)

    def update(t, h_local):
        hs = v["hsbuf"][t]
        for l, (lo, hi) in enumerate(spans):
            rows = slice(128 * lo, 128 * hi)
            weighted = v["rbuf"][t, :, 128 * l : 128 * (l + 1)] * hs
            sums = []
            for m in range(lo, hi):
                message = weighted
                if m:
                    message = weighted * v["ybc"][m - 1]
                sums.append(halves(mm(v["prt"][...], beside(message))))
            agg = (sums[0] if l == 0 else jnp.concatenate(sums, axis=0)) * SPREAD
            v["mixed"][t, rows, :] = halves(mm(beside(agg), v["mix4"][t, l]))

        def square(lo, hi):
            total = None
            for m in range(lo, hi):
                x = v["mixed"][t, 128 * m : 128 * (m + 1), :]
                total = x * x if total is None else total + x * x
            return total

        invariants = jnp.concatenate(
            [v["mixed"][t, 0:128, :], square(1, 4), square(4, 9), h_local], axis=1
        )
        x_hi, x_lo = split(invariants)
        out = mm(jnp.concatenate([x_hi, x_lo], axis=0), v["pr4"][t])
        out = out[0:128] + out[128:256]
        return halves(out)

    def back_update(t, dh):
        dinv = halves(mm(beside(dh), v["prT"][t]))
        for l, (lo, hi) in enumerate(spans):
            grad = dinv[:, 128 * l : 128 * (l + 1)]
            if l == 0:
                parts = grad
            else:
                parts = jnp.concatenate(
                    [
                        2.0 * v["mixed"][t, 128 * m : 128 * (m + 1), :] * grad
                        for m in range(lo, hi)
                    ],
                    axis=0,
                )
            out = halves(mm(beside(parts), v["mixT"][t, l])) * SPREAD
            for m in range(lo, hi):
                v["dap"][:, 128 * m : 128 * (m + 1)] = jnp.concatenate(
                    split(out[128 * (m - lo) : 128 * (m - lo + 1)]), axis=0
                )

    def back_edges(t, rows, grads, angles):
        hit = v["pr2"][rows, :]
        lanes = iota((CHUNK, 128), 1)
        turned = v["dyc"][rows, :] if angles else None
        hs = v["hsbuf"][t, rows, :] if angles else None
        pulled = {}
        for m in (0, 1, 3, 5, 7):
            if m:
                pair = mm(hit, v["dap"][:, 128 * m : 128 * (m + 2)])
                pulled[m], pulled[m + 1] = pair[:, 0:128], pair[:, 128:256]
            elif grads:
                pulled[0] = mm(hit, v["dap"][:, 0:128])
        out = []
        for l, (lo, hi) in enumerate(spans):
            weighted = v["rbuf"][t, rows, 128 * l : 128 * (l + 1)] * hs if angles else None
            total = None
            for m in range(lo, hi):
                if not grads and not m:
                    continue
                d_m = pulled[m]
                if m and angles:
                    along = jnp.sum(d_m * weighted, axis=1, keepdims=True)
                    turned = jnp.where(lanes == m - 1, turned + along, turned)
                if grads:
                    term = d_m * v["ybc"][m - 1, rows, :] if m else d_m
                    total = term if total is None else total + term
            out.append(total)
        if angles:
            v["dyc"][rows, :] = turned
        return out

    def back_radial(t, rows, grads):
        hs = v["hsbuf"][t, rows, :]
        parts = [split(grad * hs) for grad in grads]
        dr = jnp.concatenate([p[0] for p in parts] + [p[1] for p in parts], axis=1)
        out = halves(mm(dr, v["woT"][t]))
        if t == 1:
            v["dhid"][rows, :] = out
        else:
            v["dhid"][rows, :] += out

    radial_of(0)
    h1 = update(0, v["hloc"][...])
    for g, (first, size) in enumerate(GROUPS):
        wanted = jnp.full((1, 128), -1.0, F32)
        for j in range(size):
            wanted = jnp.where(lane_group == place(j), u_buf[first + j][4:5, :], wanted)
        lists = onehot(iota((128, 128), 0) == wanted.astype(jnp.int32))
        chosen = mm(union_t, lists)
        v["selt"][:, 128 * g : 128 * (g + 1)] = chosen.astype(BF16)
        v["sel"][128 * g : 128 * (g + 1), :] = flipped(chosen).astype(BF16)
    h1_pair = beside(h1)
    v["snd1"][...] = halves(mm(v["sel"][...], h1_pair)).reshape(32, GHOST, C)
    for k in near:
        ship(v["snd1"].at[row_block(k)], rcv1.at[26 - k], 1, ids[k])
    v["hloc"][...] = h1
    hidden_second()
    radial_of(1)
    ro_rows = jnp.broadcast_to(vm["ro"][...], (8, C))
    energy_one = exact(ro_rows, h1, ((1,), (1,)))[0:1]

    def gather_local(k, carry):
        v["hsbuf"][1, rows_of(k), :] = halves(mm(v["ps"][rows_of(k), 0:ATOMS], h1_pair))
        return carry

    lax.fori_loop(0, CHUNKS, gather_local, 0, unroll=True)
    await_bytes(rcv1, recv_sem.at[1], len(near))
    v["table"][...] = beside(rcv1[...].reshape(BLOCKS * GHOST, C))

    def gather_second(k, carry):
        v["hsbuf"][1, rows_of(k), :] += halves(
            mm(v["ps"][rows_of(k), ATOMS:TABLE], v["table"][...])
        )
        return carry

    lax.fori_loop(0, CHUNKS, gather_second, 0, unroll=True)
    h2 = update(1, v["hloc"][...])
    pre_read = exact(h2, rh)
    sig_read = 1.0 / (1.0 + jnp.exp(-pre_read))
    hid_read = pre_read * sig_read
    dread = rt_row * live_col[:, 0:16] * (sig_read + hid_read * (1.0 - sig_read))
    dh2 = exact(dread, rhT)

    back_update(1, dh2)

    def features_second(k, carry):
        rows = rows_of(k)
        grads = back_edges(1, rows, True, False)
        total = None
        for l in range(3):
            v["grads"][rows, 128 * l : 128 * (l + 1)] = grads[l]
            term = v["rbuf"][1, rows, 128 * l : 128 * (l + 1)] * grads[l]
            total = term if total is None else total + term
        v["dhp"][rows, :] = beside(total)
        return carry

    lax.fori_loop(0, CHUNKS, features_second, 0, unroll=True)
    hgrad = halves(mm(v["pst"][ATOMS:TABLE, :], v["dhp"][...]))
    v["snd2"][...] = hgrad.reshape(BLOCKS, GHOST, C)
    for k in near:
        ship(v["snd2"].at[k], rcv2.at[row_block(26 - k)], 2, ids[k])
    own = (
        halves(mm(v["pst"][0:ATOMS, :], v["dhp"][...]))
        + live_col * jnp.broadcast_to(vm["ro"][...], (ATOMS, C))
        + halves(mm(beside(dh2), v["resT"][...]))
    )
    rt_rows = jnp.broadcast_to(rt_row, (8, GHOST))
    energy_two = exact(rt_rows, hid_read, ((1,), (1,)))[0:1]
    energy = (base_energy + energy_one + energy_two) * live
    v["dyc"][...] = jnp.zeros((EDGES, 128), F32)

    def angles_second(k, carry):
        rows = rows_of(k)
        back_edges(1, rows, False, True)
        back_radial(1, rows, [v["grads"][rows, 128 * l : 128 * (l + 1)] for l in range(3)])
        return carry

    lax.fori_loop(0, CHUNKS, angles_second, 0, unroll=True)
    await_bytes(rcv2, recv_sem.at[2], len(near))
    dh1 = own + halves(mm(v["selt"][...], beside(rcv2[...].reshape(512, C))))

    back_update(0, dh1)

    def edges_first(k, carry):
        rows = rows_of(k)
        back_radial(0, rows, back_edges(0, rows, True, True))
        return carry

    lax.fori_loop(0, CHUNKS, edges_first, 0, unroll=True)

    dbas, dys = [], []
    for j in range(EDGES // 128):
        span = slice(128 * j, 128 * (j + 1))
        dpre = v["dhid"][span, :] * v["dsil"][span, :]
        dbas.append(flipped(mm(beside(dpre), v["winT"][...]))[0:16])
        dys.append(flipped(v["dyc"][span, :])[0:8])
    g = jnp.concatenate(dys, axis=1)
    dbas = jnp.concatenate(dbas, axis=1)
    dbas = dbas[0:8] + dbas[8:16]
    dlen = jnp.sum(dbas * slope, axis=0, keepdims=True)
    g1, g2, g3, g4, g5, g6, g7, g8 = [g[m : m + 1, :] for m in range(8)]
    da = R3 * g1 + R15 * (ub * g4 + uc * g7 + ua * g8)
    db = R3 * g2 + R15 * (ua * g4 + uc * g5 - ub * g8)
    dc = R3 * g3 + R15 * (ub * g5 + ua * g7) + (3.0 * R5) * uc * g6
    along = dlen - (da * ua + db * ub + dc * uc) * inv
    dvb = v["dvb"]
    dvb[...] = jnp.zeros((8, EDGES), F32)
    dvb[0:1, :] = da * inv + ua * along
    dvb[1:2, :] = db * inv + ub * along
    dvb[2:3, :] = dc * inv + uc * along
    dvec = dvb[...]
    v_hi = dvec.astype(BF16).astype(F32)
    dv_pair = jnp.concatenate([v_hi, dvec - v_hi], axis=0).astype(BF16)
    strain = exact(dvec, v["xyz"][...], ((1,), (1,)))
    tile_f[0:8, :] = jnp.zeros((8, 128), F32)
    tile_f[0:8, 0:8] = strain
    tile_f[3:4, 0:1] = count[:, 0:1].astype(F32)
    own_part = tile_f[0:8, :]
    red_a, red_b, part_a, part_b = v["red_a"], v["red_b"], v["part_a"], v["part_b"]
    part_a[0] = own_part
    for s in others:
        ship(part_a.at[0, pl.ds(0, 4)], red_a.at[s - 1, pl.ds(0, 4)], 4, ring[s])
    cgrad = mm(dv_pair, v["ps"][...])
    cgrad = cgrad[0:8] + cgrad[8:16]
    for g, (first, size) in enumerate(GROUPS):
        tile = cgrad[:, ATOMS + 16 * first : ATOMS + 16 * (first + size)]
        if size < 8:
            tile = jnp.concatenate([tile, jnp.zeros((8, 128 - 16 * size), F32)], axis=1)
        v["snd3"][g] = tile
    for k in near:
        ship(v["snd3"].at[k // 8, pl.ds(0, 3)], rcv3.at[26 - k, pl.ds(0, 3)], 3, ids[k])
    rgrad = mm(dv_pair, v["pr2"][:, 0:ATOMS])
    rgrad = rgrad[0:8] + rgrad[8:16]
    await_bytes(red_a, recv_sem.at[4], 15, 4)
    total = own_part + jnp.sum(red_a[...], axis=0)
    part_b[0] = total
    for s in others:
        ship(part_b.at[0, pl.ds(0, 4)], red_b.at[s - 1, pl.ds(0, 4)], 5, plane[s])

    await_bytes(rcv3, recv_sem.at[3], len(near), 3)
    back = jnp.zeros((8, ATOMS), F32)
    for g, (first, size) in enumerate(GROUPS):
        tile = jnp.zeros((8, 128), F32)
        for j in range(size):
            tile = jnp.where(lane_group == place(j), rcv3[first + j], tile)
        t_hi = tile.astype(BF16).astype(F32)
        pair = jnp.concatenate([t_hi, tile - t_hi], axis=0).astype(BF16)
        got = mm(pair, v["sel"][128 * g : 128 * (g + 1), :])
        back = back + got[0:8] + got[8:16]
    forces = rgrad - cgrad[:, 0:ATOMS] - back
    v["done_out"][0:3, :] = forces[0:3]
    v["done_out"][3:4, :] = energy
    result_here, result_left = exchange([(v["done_out"], v["done"])], DOMAIN + 1)

    await_bytes(red_b, recv_sem.at[5], 15, 4)
    total = total + jnp.sum(red_b[...], axis=0)
    result_ref[8:16, :] = -total / total[3:4, 0:1]
    result_here()
    result_ref[0:8, :] = v["done"][...]
    domain_left()
    result_left()

    await_bytes(u_buf, send_sem.at[0], len(near))
    await_bytes(rcv1, send_sem.at[1], len(near))
    await_bytes(rcv2, send_sem.at[2], len(near))
    await_bytes(rcv3, send_sem.at[3], len(near), 3)
    await_bytes(red_a, send_sem.at[4], 15, 4)
    await_bytes(red_b, send_sem.at[5], 15, 4)


def parts(result_ref, forces_ref, energy_ref, virial_ref):
    for axis in range(3):
        forces_ref[axis] = result_ref[axis : axis + 1, :]
    energy_ref[...] = result_ref[3:4, :]
    virial_ref[...] = result_ref[8:11, 0:3]


def solution(mesh):
    sizes = tuple(mesh.shape[name] for name in ("gx", "gy", "gz"))

    def shards(
        positions,
        species,
        atom_count,
        export_union,
        ghost_map,
        edge_receiver,
        edge_sender,
        embed,
        species_energy,
        radial_in,
        radial_out,
        mixing,
        product,
        residual,
        read_one,
        read_hidden,
        read_two,
    ):
        vmem = pl.BlockSpec(memory_space=pltpu.VMEM)
        scratch = [pltpu.VMEM(shape, kind) for _, shape, kind in INPUTS + SCRATCH]
        scratch += [
            pltpu.SemaphoreType.DMA((6,)),
            pltpu.SemaphoreType.DMA((6,)),
            pltpu.SemaphoreType.DMA((len(INPUTS),)),
            pltpu.SemaphoreType.DMA((DOMAIN + 2,)),
            pltpu.SemaphoreType.DMA((DOMAIN + 2,)),
        ]
        result = pl.pallas_call(
            functools.partial(body, sizes),
            out_shape=jax.ShapeDtypeStruct((16, 128), F32),
            in_specs=[pl.BlockSpec(memory_space=pltpu.SMEM)]
            + [pl.BlockSpec(memory_space=pl.ANY)] * len(INPUTS),
            out_specs=vmem,
            scratch_shapes=scratch,
            compiler_params=pltpu.CompilerParams(
                collective_id=0,
                has_side_effects=True,
                vmem_limit_bytes=60 * 1024 * 1024,
            ),
            name="potential",
        )(
            atom_count.reshape(1),
            positions.reshape(3, 1, ATOMS),
            species.reshape(1, ATOMS),
            export_union.reshape(1, UNION),
            ghost_map.reshape(BLOCKS, GHOST).T,
            edge_receiver.reshape(1, EDGES),
            edge_sender.reshape(1, EDGES),
            embed,
            species_energy.reshape(1, -1),
            radial_in,
            radial_out,
            mixing,
            product,
            residual,
            read_one.reshape(1, C),
            read_hidden.T,
            read_two.reshape(1, -1),
        )
        forces, energy, virial = pl.pallas_call(
            parts,
            out_shape=(
                jax.ShapeDtypeStruct((3, 1, ATOMS), F32),
                jax.ShapeDtypeStruct((1, ATOMS), F32),
                jax.ShapeDtypeStruct((3, 3), F32),
            ),
            in_specs=[vmem],
            out_specs=(vmem, vmem, vmem),
            name="parts",
        )(result)
        return (
            forces.reshape(1, 1, 1, 3, ATOMS),
            energy.reshape(1, 1, 1, ATOMS),
            virial,
        )

    here = ("gx", "gy", "gz")
    in_specs = tuple(P(*here) for _ in range(7)) + tuple(P() for _ in range(10))
    out_specs = (P(*here), P(*here), P())
    return jax.shard_map(
        shards, mesh=mesh, in_specs=in_specs, out_specs=out_specs, check_vma=False
    )
```

```python
import functools

import jax
import jax.numpy as jnp
import numpy as np
from jax import lax
from jax.experimental import pallas as pl
from jax.experimental.pallas import tpu as pltpu
from jax.sharding import PartitionSpec as P

F32 = jnp.float32
BF16 = jnp.bfloat16
MESH = pl.DeviceIdType.MESH
HIGHEST = lax.Precision.HIGHEST

C = 128
ATOMS = 128
EDGES = 1024
CHUNK = 256
CHUNKS = EDGES // CHUNK
GHOST = 16
BLOCKS = 27
SELF = 13
TABLE = ATOMS + BLOCKS * GHOST
UNION = 64
RH = 64
DEG = 8
DOMAIN_SIDE = 5.0
SOFTENING = 0.25
STEP = float(np.pi / 18.0)
BASIS_SCALE = float((2.0 / 18.0) ** 0.5)
R3 = 3.0**0.5
R5 = 5.0**0.5
R15 = 15.0**0.5
DEGREE = (0, 1, 1, 1, 2, 2, 2, 2, 2)
SPREAD = float(DEG) ** (-0.5)
GROUPS = ((0, 8), (8, 8), (16, 8), (24, 3))


def place(j):
    return (2 - j) % 8


def row_block(k):
    return 8 * (k // 8) + place(k % 8)


def mm(a, b):
    return lax.dot_general(a, b, (((1,), (0,)), ((), ())), preferred_element_type=F32)


def exact(a, b, dims=((1,), (0,))):
    return lax.dot_general(a, b, (dims, ((), ())), precision=HIGHEST, preferred_element_type=F32)


def split(x):
    hi = x.astype(BF16)
    return hi, (x - hi.astype(F32)).astype(BF16)


def beside(x):
    return jnp.concatenate(split(x), axis=1)


def halves(y):
    n = y.shape[1] // 2
    return y[:, :n] + y[:, n:]


def both(x):
    return jnp.concatenate([x, x], axis=0)


def pieces(x):
    hi = x.astype(BF16).astype(F32)
    rest = x - hi
    mid = rest.astype(BF16).astype(F32)
    low = rest - mid
    return jnp.concatenate([hi, mid, low, jnp.zeros_like(x)], axis=0).astype(BF16)


def three(y):
    return y[0:8] + y[8:16] + y[16:24]


def activate(pre):
    sig = 1.0 / (1.0 + jnp.exp(-pre))
    return sig, pre * sig


def flipped(x):
    return jnp.transpose(x, (1, 0))


def onehot(cond):
    return jnp.where(cond, 1.0, 0.0).astype(BF16)


def iota(shape, dim):
    return lax.broadcasted_iota(jnp.int32, shape, dim)


def sin_cos(x):
    turns = jnp.floor(x * float(1.0 / np.pi) + 0.5)
    r = x - turns * 3.140625
    r = r - turns * 9.67502593994140625e-4
    r = r - turns * 1.509957990978376432e-7
    odd = turns - 2.0 * jnp.floor(turns * 0.5)
    sign = 1.0 - 2.0 * odd
    q = r * r
    s = 1.0 / 6227020800.0
    for c in (-1.0 / 39916800.0, 1.0 / 362880.0, -1.0 / 5040.0, 1.0 / 120.0, -1.0 / 6.0, 1.0):
        s = s * q + c
    c0 = -1.0 / 87178291200.0
    for c in (
        1.0 / 479001600.0,
        -1.0 / 3628800.0,
        1.0 / 40320.0,
        -1.0 / 720.0,
        1.0 / 24.0,
        -0.5,
        1.0,
    ):
        c0 = c0 * q + c
    return sign * (r * s), sign * c0


def swapped(at):
    x, y, z = at
    return (lax.rem(y, 4), y // 4 * 4 + x, z)


def neighbour(k, domain, sizes):
    offsets = (k // 9 - 1, k // 3 % 3 - 1, k % 3 - 1)
    return swapped(tuple(lax.rem(a + (o + n), n) for a, o, n in zip(domain, offsets, sizes)))


def ring_partner(s, at):
    x, y, z = at
    dx, dh, dc = s % 4, s // 4 % 2, s // 8
    high = lax.rem(y // 4 + dh, 2)
    core = lax.rem(lax.rem(z, 2) + dc, 2)
    return (lax.rem(x + dx, 4), high * 4 + lax.rem(y, 4), z // 2 * 2 + core)


def plane_partner(s, at):
    x, y, z = at
    dy, dz = s % 4, s // 4
    return (x, y // 4 * 4 + lax.rem(lax.rem(y, 4) + dy, 4), lax.rem(z // 2 + dz, 4) * 2 + lax.rem(z, 2))


INPUTS = (
    ("pos", (3, 1, ATOMS), F32),
    ("spec", (1, ATOMS), jnp.int32),
    ("uni", (1, UNION), jnp.int32),
    ("gmap", (GHOST, BLOCKS), jnp.int32),
    ("recv", (1, EDGES), jnp.int32),
    ("send", (1, EDGES), jnp.int32),
    ("emb", (6, C), F32),
    ("sen", (1, 6), F32),
    ("rin", (2, 8, RH), F32),
    ("rout", (2, RH, 3 * C), F32),
    ("mix", (2, 3, C, C), F32),
    ("prod", (2, 3 * C, C), F32),
    ("res", (2, C, C), F32),
    ("ro", (1, C), F32),
    ("rhid", (GHOST, C), F32),
    ("rt", (1, GHOST), F32),
)
DOMAIN = 6
ALL = 9 * ATOMS
TILE = (8, 128)
SCRATCH = (
    ("cnt_out", (1, 128), jnp.int32),
    ("cnt", (1, 128), jnp.int32),
    ("done_out", TILE, F32),
    ("done", TILE, F32),
    ("msg0", (4,) + TILE, F32),
    ("u_buf", (BLOCKS,) + TILE, F32),
    ("snd1", (32, GHOST, C), F32),
    ("rcv1", (BLOCKS, GHOST, C), F32),
    ("snd2", (BLOCKS, GHOST, C), F32),
    ("rcv2", (32, GHOST, C), F32),
    ("snd3", (4,) + TILE, F32),
    ("rcv3", (BLOCKS,) + TILE, F32),
    ("red_a", (15,) + TILE, F32),
    ("red_b", (15,) + TILE, F32),
    ("part_a", (1,) + TILE, F32),
    ("part_b", (1,) + TILE, F32),
    ("pst", (TABLE, EDGES), BF16),
    ("ps", (EDGES, TABLE), BF16),
    ("prt", (ATOMS, EDGES), BF16),
    ("pr2", (EDGES, 2 * ATOMS), BF16),
    ("ybc", (8, EDGES, 128), F32),
    ("bsel", (BLOCKS * 128, 128), BF16),
    ("selt", (ATOMS, 512), BF16),
    ("sel", (512, ATOMS), BF16),
    ("tile_i", TILE, jnp.int32),
    ("tile_f", (128, 128), F32),
    ("win", (48, 512), BF16),
    ("winT", (256, 128), BF16),
    ("wo4", (2, 256, 384), BF16),
    ("woT", (2, 768, 256), BF16),
    ("mix4", (2, 3, 256, 256), BF16),
    ("mixT", (2, 3, 256, 256), BF16),
    ("pr4", (2, 512, 256), BF16),
    ("prT", (2, 256, 768), BF16),
    ("resT", (256, 256), BF16),
    ("ybuf", (8, EDGES), F32),
    ("xyz", (8, EDGES), F32),
    ("kind", (16, EDGES), F32),
    ("hcat", (2, EDGES, 256), BF16),
    ("dsil", (EDGES, 128), F32),
    ("pre1", (EDGES, 128), F32),
    ("rbuf", (2, EDGES, 384), F32),
    ("hsbuf", (2, EDGES, 128), F32),
    ("dap", (256, ALL), BF16),
    ("grads", (EDGES, 384), F32),
    ("dhp", (EDGES, 256), BF16),
    ("dhid", (EDGES, 128), F32),
    ("dyc", (EDGES, 128), F32),
    ("mixed", (2, ALL, 128), F32),
    ("table", (TABLE - ATOMS, 256), BF16),
    ("hloc", (ATOMS, 128), F32),
    ("dvb", TILE[:1] + (EDGES,), F32),
)


def body(sizes, cnt_ref, *refs):
    names = [name for name, _, _ in INPUTS]
    hbm = dict(zip(names, refs))
    result_ref = refs[len(names)]
    rest = refs[len(names) + 1 :]
    vm = dict(zip(names, rest))
    rest = rest[len(names) :]
    v = dict(zip([name for name, _, _ in SCRATCH], rest))
    send_sem, recv_sem, load_sem, move_sem, land_sem = rest[len(SCRATCH) :]

    at = (lax.axis_index("gx"), lax.axis_index("gy"), lax.axis_index("gz"))
    near = [k for k in range(BLOCKS) if k != SELF]
    near = [near[7 * n % 26] for n in range(26)]
    others = list(range(1, 16))
    home = swapped(at)
    settled = home[0] == at[0]
    ids = {k: neighbour(k, home, sizes) for k in near}
    ring = {s: ring_partner(s, at) for s in others}
    plane = {s: plane_partner(s, at) for s in others}

    u_buf, rcv1, rcv2, rcv3 = v["u_buf"], v["rcv1"], v["rcv2"], v["rcv3"]
    tile_i, tile_f = v["tile_i"], v["tile_f"]

    u_buf[SELF] = jnp.zeros((8, 128), F32)
    rcv1[SELF] = jnp.zeros((GHOST, C), F32)
    for b in (13, 27, 28, 29, 30, 31):
        rcv2[b] = jnp.zeros((GHOST, C), F32)
    rcv3[...] = jnp.zeros((BLOCKS, 8, 128), F32)
    v["red_a"][...] = jnp.zeros((15, 8, 128), F32)
    v["done_out"][...] = jnp.zeros((8, 128), F32)
    v["red_b"][...] = jnp.zeros((15, 8, 128), F32)

    loads = [
        pltpu.make_async_copy(hbm[name], vm[name], load_sem.at[n])
        for n, name in enumerate(names)
        if n >= DOMAIN
    ]
    barrier = pltpu.get_barrier_semaphore()
    for target in list(ids.values()) + list(ring.values()) + list(plane.values()):
        pl.semaphore_signal(barrier, inc=1, device_id=target, device_id_type=MESH)

    @pl.when(jnp.logical_not(settled))
    def _():
        pl.semaphore_signal(barrier, inc=1, device_id=home, device_id_type=MESH)

    for load in loads:
        load.start()
    v["cnt_out"][...] = jnp.full((1, 128), 0, jnp.int32) + cnt_ref[0]

    def exchange(pairs, first):
        far = [
            pltpu.make_async_remote_copy(
                src_ref=src,
                dst_ref=dst,
                send_sem=move_sem.at[first + n],
                recv_sem=land_sem.at[first + n],
                device_id=home,
                device_id_type=MESH,
            )
            for n, (src, dst) in enumerate(pairs)
        ]
        close = [
            pltpu.make_async_copy(src, dst, land_sem.at[first + n])
            for n, (src, dst) in enumerate(pairs)
        ]

        @pl.when(settled)
        def _():
            for copy in close:
                copy.start()

        @pl.when(jnp.logical_not(settled))
        def _():
            for copy in far:
                copy.start()

        def landed():
            for copy in close:
                copy.wait()

        def left():
            @pl.when(jnp.logical_not(settled))
            def _():
                for copy in far:
                    copy.wait_send()

        return landed, left

    def ship(src, dst, phase, target):
        pltpu.make_async_remote_copy(
            src_ref=src,
            dst_ref=dst,
            send_sem=send_sem.at[phase],
            recv_sem=recv_sem.at[phase],
            device_id=target,
            device_id_type=MESH,
        ).start()

    def await_bytes(ref, sem, count, rows=None):
        view = ref.at[pl.ds(0, count)] if rows is None else ref.at[pl.ds(0, count), pl.ds(0, rows)]
        pltpu.make_async_copy(view, view, sem).wait()

    lane = iota((1, 128), 1)
    lane_group = lane >> 4
    row8 = iota((8, 128), 0)
    greeted = len(near) + 2 * len(others)

    @pl.when(settled)
    def _():
        pl.semaphore_wait(barrier, greeted)

    @pl.when(jnp.logical_not(settled))
    def _():
        pl.semaphore_wait(barrier, greeted + 1)

    domain_here, domain_left = exchange(
        [(hbm[name], vm[name]) for name in names[:DOMAIN]] + [(v["cnt_out"], v["cnt"])], 0
    )
    for load in loads:
        load.wait()
    tile_f[...] = jnp.zeros((128, 128), F32)
    for t in range(2):
        tile_f[0:8, RH * t : RH * (t + 1)] = vm["rin"][t]
        tile_f[8 * t + 8 : 8 * t + 16, 0:RH] = vm["rin"][t]
        tile_f[8 * t + 8 : 8 * t + 16, RH : 2 * RH] = vm["rin"][t]
    tile_f[32:38, :] = vm["emb"][...]
    rin_both = tile_f[0:8, :]
    rin_hi = rin_both.astype(BF16).astype(F32)
    rin_lo = (rin_both - rin_hi).astype(BF16).astype(F32)
    emb_pair = beside(tile_f[32:48, :])
    for t in range(2):
        twice = tile_f[8 * t + 8 : 8 * t + 16, :]
        twice_hi = twice.astype(BF16).astype(F32)
        twice_lo = (twice - twice_hi).astype(BF16).astype(F32)
        v["win"][:, 128 * t : 128 * (t + 1)] = jnp.concatenate(
            [twice_hi, twice_lo, twice_hi, twice_lo, jnp.zeros((16, 128), F32)], axis=0
        ).astype(BF16)
    v["win"][:, 256:512] = jnp.concatenate([jnp.zeros((32, 256), BF16), emb_pair], axis=0)
    turned = flipped(
        jnp.concatenate([rin_hi, rin_lo, jnp.zeros((112, 128), F32)], axis=0)
    ).astype(BF16)
    v["winT"][...] = both(turned)
    for t in range(2):
        w = vm["rout"][t]
        w_hi, w_lo = split(w)
        v["wo4"][t] = jnp.concatenate([w_hi, w_lo, w_hi, w_lo], axis=0)
        tile_f[...] = jnp.zeros((128, 128), F32)
        for l in range(3):
            tile_f[RH * t : RH * (t + 1), :] = w[:, 128 * l : 128 * (l + 1)]
            turned = beside(flipped(tile_f[...]))
            v["woT"][t, 128 * l : 128 * (l + 1), :] = turned
            v["woT"][t, 384 + 128 * l : 384 + 128 * (l + 1), :] = turned
            v["mix4"][t, l] = both(beside(vm["mix"][t, l]))
            v["mixT"][t, l] = both(beside(flipped(vm["mix"][t, l])))
            block = slice(128 * l, 128 * (l + 1))
            v["pr4"][t, block, :] = beside(vm["prod"][t, block, :])
            p_hi, p_lo = split(flipped(vm["prod"][t, block, :]))
            v["prT"][t, :, block] = both(p_hi)
            v["prT"][t, :, 384 + 128 * l : 384 + 128 * (l + 1)] = both(p_lo)
        v["pr4"][t, 384:512, :] = beside(vm["res"][t])
    v["resT"][...] = both(beside(flipped(vm["res"][1])))
    rhT = vm["rhid"][...]
    tile_f[...] = jnp.zeros((128, 128), F32)
    tile_f[0:16, :] = rhT
    rh = flipped(tile_f[...])[:, 0:16]
    rt_row = vm["rt"][...]
    tile_f[0:16, :] = jnp.zeros((16, 128), F32)
    tile_f[0:1, 0:6] = vm["sen"][...]
    sen_col = flipped(tile_f[...])[0:16, 0:1]
    domain_here()
    count = v["cnt"][...]
    tile_i[...] = jnp.full((8, 128), -1, jnp.int32)
    tile_i[0:1, 0:UNION] = vm["uni"][...]
    union_row = tile_i[0:1, :]
    union_t = onehot(iota((ATOMS, 128), 0) == union_row)
    species = vm["spec"][...]
    pos = vm["pos"]
    geometry = jnp.concatenate(
        [pos[0], pos[1], pos[2], species.astype(F32), jnp.zeros((4, ATOMS), F32)], axis=0
    )
    offered = three(mm(pieces(geometry), union_t))
    tile_f[...] = jnp.zeros((128, 128), F32)
    tile_f[0:GHOST, 0:BLOCKS] = vm["gmap"][...].astype(F32)
    turned_map = flipped(tile_f[...])[0:32, :]
    tiling = onehot(iota((128, 128), 0) == (iota((128, 128), 1) & 15))
    tiled = mm(turned_map.astype(BF16), tiling)
    tiled = jnp.where((iota((32, 128), 1) >> 4) == (iota((32, 128), 0) & 7), tiled, 0.0)
    own_lists = [jnp.sum(tiled[8 * g : 8 * g + 8], axis=0, keepdims=True) for g in range(4)]
    for g in range(4):
        v["msg0"][g] = jnp.where(row8 == 4, own_lists[g], offered)

    for k in near:
        ship(v["msg0"].at[k // 8], u_buf.at[26 - k], 0, ids[k])

    lanes_all = iota((1, EDGES), 1)

    def edge_tables(k, carry):
        lanes = pl.ds(pl.multiple_of(k * 128, 128), 128)
        rows = pl.ds(pl.multiple_of(k * 128, 128), 128)
        to = vm["send"][:, lanes]
        by = vm["recv"][:, lanes]
        alive = iota((1, 128), 1) + k * 128 < DEG * count
        by = jnp.where(alive, by, -1)
        v["pst"][:, lanes] = onehot(iota((TABLE, 128), 0) == to)
        v["prt"][:, lanes] = onehot(iota((ATOMS, 128), 0) == by)
        to_col = flipped(jnp.broadcast_to(to.astype(F32), (128, 128))).astype(jnp.int32)
        by_col = flipped(jnp.broadcast_to(by.astype(F32), (128, 128))).astype(jnp.int32)
        column = iota((128, 128), 1)
        for b in range(4):
            v["ps"][rows, 128 * b : 128 * (b + 1)] = onehot(column + 128 * b == to_col)
        last = TABLE - 512
        v["ps"][rows, 512:TABLE] = onehot(column[:, 0:last] + 512 == to_col[:, 0:last])
        mine = onehot(column == by_col)
        v["pr2"][rows, :] = jnp.concatenate([mine, mine], axis=1)
        return carry

    lax.fori_loop(0, EDGES // 128, edge_tables, 0)
    for g, (first, size) in enumerate(GROUPS):
        target = jnp.where(
            lane_group < size, lane_group * 128 + own_lists[g].astype(jnp.int32), -1
        )
        v["bsel"][128 * first : 128 * (first + size), :] = onehot(
            iota((size * 128, 128), 0) == target
        )

    hot = jnp.where(iota((16, ATOMS), 0) == species, 1.0, 0.0)
    base_energy = jnp.sum(hot * sen_col, axis=0, keepdims=True)
    hot_rows = flipped(jnp.concatenate([hot, jnp.zeros((112, ATOMS), F32)], axis=0))
    v["hloc"][...] = halves(mm(hot_rows[:, 0:16].astype(BF16), emb_pair))
    live = jnp.where(lane < count, 1.0, 0.0)
    live_col = jnp.where(iota((ATOMS, C), 0) < count, 1.0, 0.0)

    await_bytes(u_buf, recv_sem.at[0], len(near))
    tables = [geometry]
    for g, (first, size) in enumerate(GROUPS):
        u_cat = jnp.concatenate([u_buf[first + j] for j in range(size)], axis=1)
        ghost = three(mm(pieces(u_cat), v["bsel"][128 * first : 128 * (first + size), :]))
        block = first + lane_group
        ninth = jnp.where(block >= 9, 1, 0) + jnp.where(block >= 18, 1, 0)
        third = sum(jnp.where(block >= 3 * n, 1, 0) for n in range(1, 9))
        steps = (ninth, third - 3 * ninth, block - 3 * third)
        shift = jnp.zeros((8, 128), F32)
        for axis, step in enumerate(steps):
            shift = jnp.where(row8 == axis, (step - 1).astype(F32) * DOMAIN_SIDE, shift)
        ghost = ghost + shift
        tables.append(ghost[:, 0 : size * GHOST])
    coord24 = pieces(jnp.concatenate(tables, axis=1))
    from_sender = three(mm(coord24, v["pst"][...]))
    at_receiver = three(mm(coord24[:, 0:ATOMS], v["prt"][...]))
    apart = from_sender - at_receiver
    v["xyz"][...] = apart
    kind = jnp.where(
        iota((16, EDGES), 0) == from_sender[3:4, :].astype(jnp.int32), 1.0, 0.0
    )

    dx, dy, dz = apart[0:1, :], apart[1:2, :], apart[2:3, :]
    length = jnp.sqrt(dx * dx + dy * dy + dz * dz + SOFTENING)
    inv = 1.0 / length
    ua, ub, uc = dx * inv, dy * inv, dz * inv
    harmonic = (
        R3 * ua,
        R3 * ub,
        R3 * uc,
        R15 * ua * ub,
        R15 * ub * uc,
        (0.5 * R5) * (3.0 * uc * uc - 1.0),
        R15 * ua * uc,
        (0.5 * R15) * (ua * ua - ub * ub),
    )
    for m in range(8):
        v["ybuf"][m : m + 1, :] = harmonic[m]
    orders = (iota((8, EDGES), 0) + 1).astype(F32) * STEP
    sines, cosines = sin_cos(orders * length)
    basis = BASIS_SCALE * sines * inv
    b_hi, b_lo = split(basis)
    b_hi, b_lo = b_hi.astype(F32), b_lo.astype(F32)
    v_rows = jnp.concatenate([b_hi, b_hi, b_lo, b_lo, kind], axis=0)
    for j in range(EDGES // 128):
        span = slice(128 * j, 128 * (j + 1))
        block = jnp.concatenate([v_rows[:, span], jnp.zeros((80, 128), F32)], axis=0)
        turned = flipped(block)[:, 0:48].astype(BF16)
        out = mm(turned, v["win"][...])
        v["hsbuf"][0, span, :] = halves(out[:, 256:512])
        v["pre1"][span, :] = out[:, 128:256]
        v["dsil"][span, :] = out[:, 0:128]
        v["hcat"][0, span, :] = beside(activate(out[:, 0:128])[1])
        for m in range(8):
            v["ybc"][m, span, :] = flipped(
                jnp.broadcast_to(v["ybuf"][m : m + 1, span], (128, 128))
            )

    def rows_of(k):
        if isinstance(k, int):
            return pl.ds(k * CHUNK, CHUNK)
        return pl.ds(pl.multiple_of(k * CHUNK, CHUNK), CHUNK)

    spans = ((0, 1), (1, 4), (4, 9))

    def hidden_second():
        low = iota((CHUNK, 128), 1) < RH

        def step(k, carry):
            rows = rows_of(k)
            pre1 = v["pre1"][rows, :]
            v["hcat"][1, rows, :] = beside(activate(pre1)[1])
            sig, hidden = activate(jnp.where(low, v["dsil"][rows, :], pre1))
            v["dsil"][rows, :] = sig + hidden * (1.0 - sig)
            return carry

        lax.fori_loop(0, CHUNKS, step, 0, unroll=True)

    def radial_of(t):
        def step(k, carry):
            v["rbuf"][t, rows_of(k), :] = mm(v["hcat"][t, rows_of(k), :], v["wo4"][t])
            return carry

        lax.fori_loop(0, CHUNKS, step, 0, unroll=True)

    def update(t, h_local):
        hs = v["hsbuf"][t]
        for l, (lo, hi) in enumerate(spans):
            rows = slice(128 * lo, 128 * hi)
            weighted = v["rbuf"][t, :, 128 * l : 128 * (l + 1)] * hs
            sums = []
            for m in range(lo, hi):
                message = weighted
                if m:
                    message = weighted * v["ybc"][m - 1]
                sums.append(halves(mm(v["prt"][...], beside(message))))
            agg = (sums[0] if l == 0 else jnp.concatenate(sums, axis=0)) * SPREAD
            v["mixed"][t, rows, :] = halves(mm(beside(agg), v["mix4"][t, l]))

        def square(lo, hi):
            total = None
            for m in range(lo, hi):
                x = v["mixed"][t, 128 * m : 128 * (m + 1), :]
                total = x * x if total is None else total + x * x
            return total

        invariants = jnp.concatenate(
            [v["mixed"][t, 0:128, :], square(1, 4), square(4, 9), h_local], axis=1
        )
        x_hi, x_lo = split(invariants)
        out = mm(jnp.concatenate([x_hi, x_lo], axis=0), v["pr4"][t])
        out = out[0:128] + out[128:256]
        return halves(out)

    def back_update(t, dh):
        dinv = halves(mm(beside(dh), v["prT"][t]))
        for l, (lo, hi) in enumerate(spans):
            grad = dinv[:, 128 * l : 128 * (l + 1)]
            if l == 0:
                parts = grad
            else:
                parts = jnp.concatenate(
                    [
                        2.0 * v["mixed"][t, 128 * m : 128 * (m + 1), :] * grad
                        for m in range(lo, hi)
                    ],
                    axis=0,
                )
            out = halves(mm(beside(parts), v["mixT"][t, l])) * SPREAD
            for m in range(lo, hi):
                v["dap"][:, 128 * m : 128 * (m + 1)] = jnp.concatenate(
                    split(out[128 * (m - lo) : 128 * (m - lo + 1)]), axis=0
                )

    def back_edges(t, rows, grads, angles):
        hit = v["pr2"][rows, :]
        lanes = iota((CHUNK, 128), 1)
        turned = v["dyc"][rows, :] if angles else None
        hs = v["hsbuf"][t, rows, :] if angles else None
        pulled = {}
        for m in (0, 1, 3, 5, 7):
            if m:
                pair = mm(hit, v["dap"][:, 128 * m : 128 * (m + 2)])
                pulled[m], pulled[m + 1] = pair[:, 0:128], pair[:, 128:256]
            elif grads:
                pulled[0] = mm(hit, v["dap"][:, 0:128])
        out = []
        for l, (lo, hi) in enumerate(spans):
            weighted = v["rbuf"][t, rows, 128 * l : 128 * (l + 1)] * hs if angles else None
            total = None
            for m in range(lo, hi):
                if not grads and not m:
                    continue
                d_m = pulled[m]
                if m and angles:
                    along = jnp.sum(d_m * weighted, axis=1, keepdims=True)
                    turned = jnp.where(lanes == m - 1, turned + along, turned)
                if grads:
                    term = d_m * v["ybc"][m - 1, rows, :] if m else d_m
                    total = term if total is None else total + term
            out.append(total)
        if angles:
            v["dyc"][rows, :] = turned
        return out

    def back_radial(t, rows, grads):
        hs = v["hsbuf"][t, rows, :]
        parts = [split(grad * hs) for grad in grads]
        dr = jnp.concatenate([p[0] for p in parts] + [p[1] for p in parts], axis=1)
        out = halves(mm(dr, v["woT"][t]))
        if t == 1:
            v["dhid"][rows, :] = out
        else:
            v["dhid"][rows, :] += out

    radial_of(0)
    h1 = update(0, v["hloc"][...])
    for g, (first, size) in enumerate(GROUPS):
        wanted = jnp.full((1, 128), -1.0, F32)
        for j in range(size):
            wanted = jnp.where(lane_group == place(j), u_buf[first + j][4:5, :], wanted)
        lists = onehot(iota((128, 128), 0) == wanted.astype(jnp.int32))
        chosen = mm(union_t, lists)
        v["selt"][:, 128 * g : 128 * (g + 1)] = chosen.astype(BF16)
        v["sel"][128 * g : 128 * (g + 1), :] = flipped(chosen).astype(BF16)
    h1_pair = beside(h1)
    v["snd1"][...] = halves(mm(v["sel"][...], h1_pair)).reshape(32, GHOST, C)
    for k in near:
        ship(v["snd1"].at[row_block(k)], rcv1.at[26 - k], 1, ids[k])
    v["hloc"][...] = h1
    slope = (BASIS_SCALE * orders * cosines - basis) * inv
    hidden_second()
    radial_of(1)
    ro_rows = jnp.broadcast_to(vm["ro"][...], (8, C))
    energy_one = exact(ro_rows, h1, ((1,), (1,)))[0:1]

    def gather_local(k, carry):
        v["hsbuf"][1, rows_of(k), :] = halves(mm(v["ps"][rows_of(k), 0:ATOMS], h1_pair))
        return carry

    lax.fori_loop(0, CHUNKS, gather_local, 0, unroll=True)
    await_bytes(rcv1, recv_sem.at[1], len(near))
    v["table"][...] = beside(rcv1[...].reshape(BLOCKS * GHOST, C))

    def gather_second(k, carry):
        v["hsbuf"][1, rows_of(k), :] += halves(
            mm(v["ps"][rows_of(k), ATOMS:TABLE], v["table"][...])
        )
        return carry

    lax.fori_loop(0, CHUNKS, gather_second, 0, unroll=True)
    h2 = update(1, v["hloc"][...])
    pre_read = exact(h2, rh)
    sig_read = 1.0 / (1.0 + jnp.exp(-pre_read))
    hid_read = pre_read * sig_read
    dread = rt_row * live_col[:, 0:16] * (sig_read + hid_read * (1.0 - sig_read))
    dh2 = exact(dread, rhT)

    back_update(1, dh2)

    def features_second(k, carry):
        rows = rows_of(k)
        grads = back_edges(1, rows, True, False)
        total = None
        for l in range(3):
            v["grads"][rows, 128 * l : 128 * (l + 1)] = grads[l]
            term = v["rbuf"][1, rows, 128 * l : 128 * (l + 1)] * grads[l]
            total = term if total is None else total + term
        v["dhp"][rows, :] = beside(total)
        return carry

    lax.fori_loop(0, CHUNKS, features_second, 0, unroll=True)
    hgrad = halves(mm(v["pst"][ATOMS:TABLE, :], v["dhp"][...]))
    v["snd2"][...] = hgrad.reshape(BLOCKS, GHOST, C)
    for k in near:
        ship(v["snd2"].at[k], rcv2.at[row_block(26 - k)], 2, ids[k])
    own = (
        halves(mm(v["pst"][0:ATOMS, :], v["dhp"][...]))
        + live_col * jnp.broadcast_to(vm["ro"][...], (ATOMS, C))
        + halves(mm(beside(dh2), v["resT"][...]))
    )
    rt_rows = jnp.broadcast_to(rt_row, (8, GHOST))
    energy_two = exact(rt_rows, hid_read, ((1,), (1,)))[0:1]
    energy = (base_energy + energy_one + energy_two) * live
    v["dyc"][...] = jnp.zeros((EDGES, 128), F32)

    def angles_second(k, carry):
        rows = rows_of(k)
        back_edges(1, rows, False, True)
        back_radial(1, rows, [v["grads"][rows, 128 * l : 128 * (l + 1)] for l in range(3)])
        return carry

    lax.fori_loop(0, CHUNKS, angles_second, 0, unroll=True)
    await_bytes(rcv2, recv_sem.at[2], len(near))
    dh1 = own + halves(mm(v["selt"][...], beside(rcv2[...].reshape(512, C))))

    back_update(0, dh1)

    def edges_first(k, carry):
        rows = rows_of(k)
        back_radial(0, rows, back_edges(0, rows, True, True))
        return carry

    lax.fori_loop(0, CHUNKS, edges_first, 0, unroll=True)

    dbas, dys = [], []
    for j in range(EDGES // 128):
        span = slice(128 * j, 128 * (j + 1))
        dpre = v["dhid"][span, :] * v["dsil"][span, :]
        dbas.append(flipped(mm(beside(dpre), v["winT"][...]))[0:16])
        dys.append(flipped(v["dyc"][span, :])[0:8])
    g = jnp.concatenate(dys, axis=1)
    dbas = jnp.concatenate(dbas, axis=1)
    dbas = dbas[0:8] + dbas[8:16]
    dlen = jnp.sum(dbas * slope, axis=0, keepdims=True)
    g1, g2, g3, g4, g5, g6, g7, g8 = [g[m : m + 1, :] for m in range(8)]
    da = R3 * g1 + R15 * (ub * g4 + uc * g7 + ua * g8)
    db = R3 * g2 + R15 * (ua * g4 + uc * g5 - ub * g8)
    dc = R3 * g3 + R15 * (ub * g5 + ua * g7) + (3.0 * R5) * uc * g6
    along = dlen - (da * ua + db * ub + dc * uc) * inv
    dvb = v["dvb"]
    dvb[...] = jnp.zeros((8, EDGES), F32)
    dvb[0:1, :] = da * inv + ua * along
    dvb[1:2, :] = db * inv + ub * along
    dvb[2:3, :] = dc * inv + uc * along
    dvec = dvb[...]
    v_hi = dvec.astype(BF16).astype(F32)
    dv_pair = jnp.concatenate([v_hi, dvec - v_hi], axis=0).astype(BF16)
    cgrad = mm(dv_pair, v["ps"][...])
    cgrad = cgrad[0:8] + cgrad[8:16]
    for g, (first, size) in enumerate(GROUPS):
        tile = cgrad[:, ATOMS + 16 * first : ATOMS + 16 * (first + size)]
        if size < 8:
            tile = jnp.concatenate([tile, jnp.zeros((8, 128 - 16 * size), F32)], axis=1)
        v["snd3"][g] = tile
    for k in near:
        ship(v["snd3"].at[k // 8, pl.ds(0, 3)], rcv3.at[26 - k, pl.ds(0, 3)], 3, ids[k])
    strain = exact(dvec, v["xyz"][...], ((1,), (1,)))
    tile_f[0:8, :] = jnp.zeros((8, 128), F32)
    tile_f[0:8, 0:8] = strain
    tile_f[3:4, 0:1] = count[:, 0:1].astype(F32)
    own_part = tile_f[0:8, :]
    red_a, red_b, part_a, part_b = v["red_a"], v["red_b"], v["part_a"], v["part_b"]
    part_a[0] = own_part
    for s in others:
        ship(part_a.at[0, pl.ds(0, 4)], red_a.at[s - 1, pl.ds(0, 4)], 4, ring[s])
    rgrad = mm(dv_pair, v["pr2"][:, 0:ATOMS])
    rgrad = rgrad[0:8] + rgrad[8:16]
    await_bytes(red_a, recv_sem.at[4], 15, 4)
    total = own_part + jnp.sum(red_a[...], axis=0)
    part_b[0] = total
    for s in others:
        ship(part_b.at[0, pl.ds(0, 4)], red_b.at[s - 1, pl.ds(0, 4)], 5, plane[s])

    await_bytes(rcv3, recv_sem.at[3], len(near), 3)
    back = jnp.zeros((8, ATOMS), F32)
    for g, (first, size) in enumerate(GROUPS):
        tile = jnp.zeros((8, 128), F32)
        for j in range(size):
            tile = jnp.where(lane_group == place(j), rcv3[first + j], tile)
        t_hi = tile.astype(BF16).astype(F32)
        pair = jnp.concatenate([t_hi, tile - t_hi], axis=0).astype(BF16)
        got = mm(pair, v["sel"][128 * g : 128 * (g + 1), :])
        back = back + got[0:8] + got[8:16]
    forces = rgrad - cgrad[:, 0:ATOMS] - back
    v["done_out"][0:3, :] = forces[0:3]
    v["done_out"][3:4, :] = energy
    result_here, result_left = exchange([(v["done_out"], v["done"])], DOMAIN + 1)

    await_bytes(red_b, recv_sem.at[5], 15, 4)
    total = total + jnp.sum(red_b[...], axis=0)
    result_ref[8:16, :] = -total / total[3:4, 0:1]
    result_here()
    result_ref[0:8, :] = v["done"][...]
    domain_left()
    result_left()

    await_bytes(u_buf, send_sem.at[0], len(near))
    await_bytes(rcv1, send_sem.at[1], len(near))
    await_bytes(rcv2, send_sem.at[2], len(near))
    await_bytes(rcv3, send_sem.at[3], len(near), 3)
    await_bytes(red_a, send_sem.at[4], 15, 4)
    await_bytes(red_b, send_sem.at[5], 15, 4)


def parts(result_ref, forces_ref, energy_ref, virial_ref):
    for axis in range(3):
        forces_ref[axis] = result_ref[axis : axis + 1, :]
    energy_ref[...] = result_ref[3:4, :]
    virial_ref[...] = result_ref[8:11, 0:3]


def solution(mesh):
    sizes = tuple(mesh.shape[name] for name in ("gx", "gy", "gz"))

    def shards(
        positions,
        species,
        atom_count,
        export_union,
        ghost_map,
        edge_receiver,
        edge_sender,
        embed,
        species_energy,
        radial_in,
        radial_out,
        mixing,
        product,
        residual,
        read_one,
        read_hidden,
        read_two,
    ):
        vmem = pl.BlockSpec(memory_space=pltpu.VMEM)
        scratch = [pltpu.VMEM(shape, kind) for _, shape, kind in INPUTS + SCRATCH]
        scratch += [
            pltpu.SemaphoreType.DMA((6,)),
            pltpu.SemaphoreType.DMA((6,)),
            pltpu.SemaphoreType.DMA((len(INPUTS),)),
            pltpu.SemaphoreType.DMA((DOMAIN + 2,)),
            pltpu.SemaphoreType.DMA((DOMAIN + 2,)),
        ]
        result = pl.pallas_call(
            functools.partial(body, sizes),
            out_shape=jax.ShapeDtypeStruct((16, 128), F32),
            in_specs=[pl.BlockSpec(memory_space=pltpu.SMEM)]
            + [pl.BlockSpec(memory_space=pl.ANY)] * len(INPUTS),
            out_specs=vmem,
            scratch_shapes=scratch,
            compiler_params=pltpu.CompilerParams(
                collective_id=0,
                has_side_effects=True,
                vmem_limit_bytes=60 * 1024 * 1024,
            ),
            name="potential",
        )(
            atom_count.reshape(1),
            positions.reshape(3, 1, ATOMS),
            species.reshape(1, ATOMS),
            export_union.reshape(1, UNION),
            ghost_map.reshape(BLOCKS, GHOST).T,
            edge_receiver.reshape(1, EDGES),
            edge_sender.reshape(1, EDGES),
            embed,
            species_energy.reshape(1, -1),
            radial_in,
            radial_out,
            mixing,
            product,
            residual,
            read_one.reshape(1, C),
            read_hidden.T,
            read_two.reshape(1, -1),
        )
        forces, energy, virial = pl.pallas_call(
            parts,
            out_shape=(
                jax.ShapeDtypeStruct((3, 1, ATOMS), F32),
                jax.ShapeDtypeStruct((1, ATOMS), F32),
                jax.ShapeDtypeStruct((3, 3), F32),
            ),
            in_specs=[vmem],
            out_specs=(vmem, vmem, vmem),
            name="parts",
        )(result)
        return (
            forces.reshape(1, 1, 1, 3, ATOMS),
            energy.reshape(1, 1, 1, ATOMS),
            virial,
        )

    here = ("gx", "gy", "gz")
    in_specs = tuple(P(*here) for _ in range(7)) + tuple(P() for _ in range(10))
    out_specs = (P(*here), P(*here), P())
    return jax.shard_map(
        shards, mesh=mesh, in_specs=in_specs, out_specs=out_specs, check_vma=False
    )
```
